128 devices in a mesh: scan: 8 (over z, core), tile: 16 (over x, y).
Axes of the slice: x: 4, y: 4, z: 4, core: 2. Of those that a mesh axis runs over, the one named last changes fastest.
Arguments:
- object_tiles: float32 [16, 2, 2, 512, 512], P('tile'), may hold values from -5 to 5
- probe_wave: float32 [2, 256, 256], replicated, may hold values from -5 to 5
- patterns: float32 [512, 256, 256], P(('scan', 'tile')), may hold values from 0 to 2
- tile_of: int32 [512], P(('scan', 'tile')), may hold values from 0 to 15, as said below
- offsets: int32 [512, 2], P(('scan', 'tile')), may hold values from 0 to 256
- owner_map: int32 [16], replicated, may hold values from 0 to 15, each once
Outputs:
- object_grad: float32 [16, 2, 2, 512, 512], P('tile', None, None, 'scan')
- probe_grad: float32 [2, 256, 256], replicated
The draws below stay inside these ranges and needn't reach their ends.
Inputs may be any that keep to these rules, and one draw needn't show every extreme that they name: `tile_of`: positions are in groups of 64 consecutive ones (one group for each index of scan). The 4 positions of one device read 4 different tiles. In every group exactly two tiles are read by 8 positions each and every other tile by at most 4.
All inputs are finite; a program needn't handle non-finite values.
Results may differ from the reference program's by a relative error of at most 0.0003.
Values sent between devices are 32-bit elements; how exact they have to be, the bound alone decides.
A program may use at most 128 MiB of HBM per device.

```python
import math
import jax
import jax.numpy as jnp
from jax import lax

P_SIZE = 256
TILE = 512
NT = 16
ROWS = 8
POSITIONS = 512


def draw_tile_of(key, part):

    def one_group(group_key):
        key_tiles, key_devices, key_order = jax.random.split(group_key, 3)
        tile_perm = jax.random.permutation(key_tiles, NT)
        device_perm = jax.random.permutation(key_devices, NT)
        device = jnp.arange(NT, dtype=jnp.int32)
        leading = jnp.where(device < NT // 2, 0, 1).astype(jnp.int32)
        others = 2 + (device[:, None] * 3 + jnp.arange(3, dtype=jnp.int32)[None, :]) % (NT - 2)
        layout = jnp.concatenate([leading[:, None], others], axis=1)
        layout = layout[device_perm]
        scores = jax.random.randint(key_order, (NT, 4), 0, 1 << 20) * 4 + jnp.arange(4, dtype=jnp.int32)[None, :]
        ranking = jnp.argsort(scores, axis=1)
        layout = jnp.take_along_axis(layout, ranking, axis=1)
        return tile_perm[layout].reshape(-1)
    group_keys = jax.random.split(jax.random.fold_in(key, 17), ROWS)
    return jax.vmap(one_group)(group_keys).reshape(-1).astype(jnp.int32)


def with_ends(values, own_key, least, high):
    spot = [jax.random.randint(jax.random.fold_in(own_key, axis), (), 0, length) for axis, length in enumerate(values.shape)]
    widest = values.shape.index(max(values.shape))
    beside = spot[:widest] + [(spot[widest] + 1) % values.shape[widest]] + spot[widest + 1:]
    return values.at[tuple(spot)].set(least).at[tuple(beside)].set(high)


def levels(key, shape, cuts, low, top_value):
    level, own = 1.0, jax.random.fold_in(key, 6)
    for position, parts in cuts:
        draws = jnp.exp(jax.random.uniform(jax.random.fold_in(own, position), (parts,), jnp.float32, low / len(cuts), top_value / len(cuts)))
        level = level * jnp.repeat(draws, shape[position] // parts).reshape([-1 if axis == position else 1 for axis in range(len(shape))])
    return level


def gaussian(own_key, dims, scale, most, cuts=(), held_as=jnp.bfloat16):
    entries = jax.random.normal(own_key, dims, jnp.float32) * scale
    if len(cuts) > 0:
        entries = levels(own_key, dims, cuts, -0.22, 0.18) * entries
    return jnp.clip(entries, min=-most, max=most).astype(held_as)


def setup_inputs(seed: int = 0) -> dict:
    splits = jax.random.split(jax.random.key(seed), 7)
    object_tiles = gaussian(splits[0], (NT, 2, 2, TILE, TILE), 0.7, 5.0, ((0, 16),), jnp.float32)
    probe_wave = gaussian(splits[1], (2, P_SIZE, P_SIZE), 0.7, 5.0, (), jnp.float32)
    patterns = jnp.clip(2.0 * jax.random.uniform(splits[2], (POSITIONS, P_SIZE, P_SIZE), jnp.float32) ** levels(splits[2], (POSITIONS, P_SIZE, P_SIZE), ((0, 128),), -0.2, 0.2), 0.0, 2.0)
    tile_of = draw_tile_of(jax.random.fold_in(splits[6], 71), 0)
    offsets = with_ends(jax.random.randint(splits[4], (POSITIONS, 2), 0, TILE - P_SIZE + 1), jax.random.fold_in(splits[4], 1), 0, TILE - P_SIZE).astype(jnp.int32)
    owner_map = jax.random.permutation(splits[5], NT).astype(jnp.int32)
    return {"object_tiles": object_tiles, "probe_wave": probe_wave, "patterns": patterns, "tile_of": tile_of, "offsets": offsets, "owner_map": owner_map}


prop_phase = 0.75

def make_tables(side):
    counter = jnp.arange(side, dtype=jnp.int32)
    product = counter[:, None] * counter[None, :] % side
    angle = 2.0 * math.pi / side * product.astype(jnp.float32)
    norm_factor = 1.0 / math.sqrt(side)
    four_real = jnp.cos(angle) * norm_factor
    four_imag = -jnp.sin(angle) * norm_factor
    freq = jnp.where(counter < side // 2, counter, counter - side).astype(jnp.float32)
    phase = prop_phase * (freq[:, None] ** 2 + freq[None, :] ** 2) / side
    return (four_real, four_imag, jnp.cos(phase), -jnp.sin(phase))

def real_product(left, right):
    return jnp.dot(left, right, precision=lax.Precision.HIGHEST, preferred_element_type=jnp.float32)

def complex_product(left_re, left_im, right_re, right_im):
    return (real_product(left_re, right_re) - real_product(left_im, right_im), real_product(left_re, right_im) + real_product(left_im, right_re))

def transform(field_re, field_im, four_real, four_imag):
    temp_re, temp_im = complex_product(four_real, four_imag, field_re, field_im)
    return complex_product(temp_re, temp_im, four_real, four_imag)

def position_loss(probe_wave, patch, pattern, weight, tables):
    four_real, four_imag, prop_real, prop_imag = tables
    probe_re, probe_im = (probe_wave[0], probe_wave[1])
    first_re, first_im = (patch[0, 0], patch[0, 1])
    second_re, second_im = (patch[1, 0], patch[1, 1])
    enter_re = probe_re * first_re - probe_im * first_im
    enter_im = probe_re * first_im + probe_im * first_re
    spec_re, spec_im = transform(enter_re, enter_im, four_real, four_imag)
    moved_re = spec_re * prop_real - spec_im * prop_imag
    moved_im = spec_re * prop_imag + spec_im * prop_real
    back_re, back_im = transform(moved_re, moved_im, four_real, -four_imag)
    exit_re = back_re * second_re - back_im * second_im
    exit_im = back_re * second_im + back_im * second_re
    far_re, far_im = transform(exit_re, exit_im, four_real, four_imag)
    resid = far_re * far_re + far_im * far_im - pattern
    return 0.5 * weight * jnp.sum(resid * resid)

def reference(object_tiles, probe_wave, patterns, tile_of, offsets, owner_map):
    tables = make_tables(P_SIZE)
    grad_fn = jax.grad(position_loss, argnums=(0, 1))
    zero = jnp.zeros((), jnp.int32)

    def step(carry, item):
        object_total, probe_total = carry
        pattern, tile_id, offset = item
        row = owner_map[tile_id].astype(jnp.int32)
        start = (row, zero, zero, offset[0].astype(jnp.int32), offset[1].astype(jnp.int32))
        patch = lax.dynamic_slice(object_tiles, start, (1, 2, 2, P_SIZE, P_SIZE))[0]
        probe_term, patch_term = grad_fn(probe_wave, patch, pattern, jnp.ones((), jnp.float32), tables)
        current = lax.dynamic_slice(object_total, start, (1, 2, 2, P_SIZE, P_SIZE))
        object_total = lax.dynamic_update_slice(object_total, current + patch_term[None], start)
        return ((object_total, probe_total + probe_term), None)
    initial = (jnp.zeros(object_tiles.shape, jnp.float32), jnp.zeros(probe_wave.shape, jnp.float32))
    final, _ = lax.scan(step, initial, (patterns, tile_of, offsets))
    object_total, probe_total = final
    return (object_total, probe_total / jnp.sqrt(jnp.ones((), jnp.float32) * POSITIONS))
```

```python
import functools
import math

import jax
import jax.numpy as jnp
import ml_dtypes
import numpy as np
from jax import lax
from jax.experimental import pallas as pl
from jax.experimental.pallas import tpu as pltpu
from jax.sharding import PartitionSpec as P

PROP_PHASE = 0.75
SIDE = 256
HALF = 128
MAX_READS = 8
F32 = jnp.float32
BF16 = jnp.bfloat16


def embed(block):
    return np.block([[block.real, block.imag], [-block.imag, block.real]])


@functools.cache
def tables():
    index = np.arange(SIDE)
    freq = np.where(index < HALF, index, index - SIDE).astype(np.float64)
    wave = np.exp(-2j * math.pi * (index[:, None] * index[None, :] % SIDE) / SIDE) / math.sqrt(SIDE)
    step = np.exp(-1j * PROP_PHASE * freq**2 / SIDE)
    travel = wave.conj() @ (step[:, None] * wave)
    plus = (travel[:HALF, :HALF] + travel[:HALF, HALF:]) / 2
    minus = (travel[:HALF, :HALF] - travel[:HALF, HALF:]) / 2
    forms = []
    for block in (plus, minus, wave[:HALF, 0::2], wave[:HALF, 1::2]):
        form = embed(block)
        forms += [form, form.T]
    forms = np.stack(forms)
    high = forms.astype(ml_dtypes.bfloat16)
    low = (forms - high.astype(np.float64)).astype(ml_dtypes.bfloat16)
    shuffle = np.zeros((SIDE, SIDE), ml_dtypes.bfloat16)
    shuffle[2 * np.arange(HALF), np.arange(HALF)] = 1
    shuffle[2 * np.arange(HALF) + 1, HALF + np.arange(HALF)] = 1
    return high, low, shuffle


A_PLUS, A_MINUS, F_EVEN, F_ODD = 0, 2, 4, 6


def parts(x):
    high = x.astype(BF16)
    return high, (x - high.astype(F32)).astype(BF16)


def mm(x, y):
    return jnp.dot(x, y, preferred_element_type=F32)


def right(x, high_ref, low_ref, which):
    xh, xl = parts(x)
    wh, wl = high_ref[which], low_ref[which]
    total = mm(xh, wh)
    total = total + mm(xl, wh)
    return total + mm(xh, wl)


def left(x, high_ref, low_ref, which):
    xh, xl = parts(x)
    wh, wl = high_ref[which], low_ref[which]
    total = mm(wh, xh)
    total = total + mm(wl, xh)
    return total + mm(wh, xl)


def cols(re, im):
    return (
        jnp.concatenate([re[:, :HALF] + re[:, HALF:], im[:, :HALF] + im[:, HALF:]], axis=1),
        jnp.concatenate([re[:, :HALF] - re[:, HALF:], im[:, :HALF] - im[:, HALF:]], axis=1),
    )


def rows(re, im):
    return (
        jnp.concatenate([re[:HALF] + re[HALF:], im[:HALF] + im[HALF:]], axis=0),
        jnp.concatenate([re[:HALF] - re[HALF:], im[:HALF] - im[HALF:]], axis=0),
    )


def split_cols(p, q):
    return (
        jnp.concatenate([p[:, :HALF], q[:, :HALF]], axis=1),
        jnp.concatenate([p[:, HALF:], q[:, HALF:]], axis=1),
    )


def split_rows(p, q):
    return (
        jnp.concatenate([p[:HALF], q[:HALF]], axis=0),
        jnp.concatenate([p[HALF:], q[HALF:]], axis=0),
    )


def travel(re, im, hi, lo, conj):
    flip = 1 if conj else 0
    s, d = cols(re, im)
    p, q = right(s, hi, lo, A_PLUS + flip), right(d, hi, lo, A_MINUS + flip)
    re, im = split_cols(p + q, p - q)
    s, d = rows(re, im)
    p, q = left(s, hi, lo, A_PLUS + 1 - flip), left(d, hi, lo, A_MINUS + 1 - flip)
    return split_rows(p + q, p - q)


def to_far(re, im, hi, lo):
    s, d = cols(re, im)
    re, im = split_cols(right(s, hi, lo, F_EVEN), right(d, hi, lo, F_ODD))
    s, d = rows(re, im)
    return split_rows(left(s, hi, lo, F_EVEN + 1), left(d, hi, lo, F_ODD + 1))


def from_far(re, im, hi, lo):
    even, odd = (
        jnp.concatenate([re[:, :HALF], im[:, :HALF]], axis=1),
        jnp.concatenate([re[:, HALF:], im[:, HALF:]], axis=1),
    )
    p, q = right(even, hi, lo, F_EVEN + 1), right(odd, hi, lo, F_ODD + 1)
    re, im = split_cols(p + q, p - q)
    even, odd = (
        jnp.concatenate([re[:HALF], im[:HALF]], axis=0),
        jnp.concatenate([re[HALF:], im[HALF:]], axis=0),
    )
    p, q = left(even, hi, lo, F_EVEN), left(odd, hi, lo, F_ODD)
    return split_rows(p + q, p - q)


def lane_mask(shift):
    return lax.broadcasted_iota(jnp.int32, (SIDE, HALF), 1) < shift


def spots(a, b):
    base = b // HALF
    return [pl.ds(4 * a + jnp.minimum(base + k, 3), SIDE, stride=4) for k in range(3)]


def patch(plane, a, b):
    shift = b % HALF
    back = lax.rem(HALF - shift, HALF)
    tiles = [pltpu.roll(plane[spot, :], back, 1) for spot in spots(a, b)]
    mask = lane_mask(HALF - shift)
    return jnp.concatenate(
        [jnp.where(mask, tiles[0], tiles[1]), jnp.where(mask, tiles[1], tiles[2])], axis=1
    )


def add_patch(plane, a, b, value):
    shift = b % HALF
    first, second = pltpu.roll(value[:, :HALF], shift, 1), pltpu.roll(value[:, HALF:], shift, 1)
    mask = lane_mask(shift)
    zero = jnp.zeros_like(first)
    terms = [jnp.where(mask, zero, first), jnp.where(mask, first, second), jnp.where(mask, second, zero)]
    for spot, term in zip(spots(a, b), terms):
        plane[spot, :] = plane[spot, :] + term


def open_tile(tile, held):
    for plane in range(4):
        for k in range(4):
            held[plane, pl.ds(k, 2 * SIDE, stride=4), :] = tile[
                plane // 2, plane % 2, :, k * HALF : (k + 1) * HALF
            ]


def close_tile(held, grad):
    for plane in range(4):
        for k in range(4):
            grad[0, plane // 2, plane % 2, :, k * HALF : (k + 1) * HALF] = held[
                plane, pl.ds(k, 2 * SIDE, stride=4), :
            ]


def forward_kernel(info, tile, probe, hi, lo, back, far, held):
    k = pl.program_id(0)

    @pl.when(k == 0)
    def _():
        open_tile(tile, held)

    @pl.when(k < info[3 * MAX_READS])
    def _():
        a, b = info[MAX_READS + k], info[2 * MAX_READS + k]
        ore, oim = patch(held.at[0], a, b), patch(held.at[1], a, b)
        pre, pim = probe[0], probe[1]
        re, im = travel(pre * ore - pim * oim, pre * oim + pim * ore, hi, lo, False)
        back[0, 0], back[0, 1] = re, im
        ore, oim = patch(held.at[2], a, b), patch(held.at[3], a, b)
        far[0, 0], far[0, 1] = to_far(re * ore - im * oim, re * oim + im * ore, hi, lo)


def backward_kernel(
    info, tile, probe, hi, lo, shuffle, back, far, pattern, grad, probe_grad, held, total, mixed
):
    k = pl.program_id(0)

    @pl.when(k == 0)
    def _():
        open_tile(tile, held)
        total[...] = jnp.zeros_like(total)
        probe_grad[...] = jnp.zeros_like(probe_grad)

    @pl.when(k < info[3 * MAX_READS])
    def _():
        a, b = info[MAX_READS + k], info[2 * MAX_READS + k]
        for c in range(2):
            mixed[c] = pattern[0, :, c * HALF : (c + 1) * HALF]
        measured = jnp.concatenate(
            [
                jnp.concatenate([mixed[c, pl.ds(odd, HALF, stride=2), :] for c in range(2)], axis=1)
                for odd in range(2)
            ],
            axis=0,
        )
        mh, ml = parts(measured)
        measured = mm(mh, shuffle[...]) + mm(ml, shuffle[...])
        fre, fim = far[0, 0], far[0, 1]
        scale = 2.0 * (fre * fre + fim * fim - measured)
        gre, gim = from_far(scale * fre, scale * fim, hi, lo)
        bre, bim = back[0, 0], back[0, 1]
        add_patch(total.at[2], a, b, bre * gre + bim * gim)
        add_patch(total.at[3], a, b, bre * gim - bim * gre)
        ore, oim = patch(held.at[2], a, b), patch(held.at[3], a, b)
        gre, gim = travel(ore * gre + oim * gim, ore * gim - oim * gre, hi, lo, True)
        pre, pim = probe[0], probe[1]
        add_patch(total.at[0], a, b, pre * gre + pim * gim)
        add_patch(total.at[1], a, b, pre * gim - pim * gre)
        ore, oim = patch(held.at[0], a, b), patch(held.at[1], a, b)
        probe_grad[0] += ore * gre + oim * gim
        probe_grad[1] += ore * gim - oim * gre

    @pl.when(k == pl.num_programs(0) - 1)
    def _():
        close_tile(total, grad)


def plane_scratch():
    return pltpu.VMEM((4, 2 * SIDE * 4, HALF), F32)


def whole(array):
    ndim = array.ndim
    return pl.BlockSpec(array.shape, lambda k, info: (0,) * ndim, pipeline_mode=pl.Buffered(1))


def forward(info, tile, probe, hi, lo):
    block = pl.BlockSpec((1, 2, SIDE, SIDE), lambda k, info: (k, 0, 0, 0))
    out = jax.ShapeDtypeStruct((MAX_READS, 2, SIDE, SIDE), F32)
    return pl.pallas_call(
        forward_kernel,
        out_shape=(out, out),
        grid_spec=pltpu.PrefetchScalarGridSpec(
            num_scalar_prefetch=1,
            grid=(MAX_READS,),
            in_specs=[whole(x) for x in (tile, probe, hi, lo)],
            out_specs=(block, block),
            scratch_shapes=[plane_scratch()],
        ),
        cost_estimate=pl.CostEstimate(
            flops=MAX_READS * 24 * 2 * SIDE**3, bytes_accessed=14 << 20, transcendentals=0
        ),
        compiler_params=pltpu.CompilerParams(vmem_limit_bytes=48 << 20),
    )(info, tile, probe, hi, lo)


def backward(info, tile, probe, hi, lo, shuffle, back, far, arrived):
    block = pl.BlockSpec((1, 2, SIDE, SIDE), lambda k, info: (k, 0, 0, 0))
    pattern = pl.BlockSpec((1, SIDE, SIDE), lambda k, info: (info[k], 0, 0))
    grad = jax.ShapeDtypeStruct((1,) + tile.shape, F32)
    probe_grad = jax.ShapeDtypeStruct(probe.shape, F32)
    return pl.pallas_call(
        backward_kernel,
        out_shape=(grad, probe_grad),
        grid_spec=pltpu.PrefetchScalarGridSpec(
            num_scalar_prefetch=1,
            grid=(MAX_READS,),
            in_specs=[whole(x) for x in (tile, probe, hi, lo, shuffle)] + [block, block, pattern],
            out_specs=(whole(grad), whole(probe_grad)),
            scratch_shapes=[plane_scratch(), plane_scratch(), pltpu.VMEM((2, SIDE, HALF), F32)],
        ),
        cost_estimate=pl.CostEstimate(
            flops=MAX_READS * 26 * 2 * SIDE**3, bytes_accessed=20 << 20, transcendentals=0
        ),
        compiler_params=pltpu.CompilerParams(vmem_limit_bytes=48 << 20),
    )(info, tile, probe, hi, lo, shuffle, back, far, arrived)


def spread_kernel(which, patterns, out, held, in_sem, out_sem):
    count = out.shape[0]
    load = pltpu.make_async_copy(patterns, held, in_sem)
    load.start()
    load.wait()
    copies = [pltpu.make_async_copy(held.at[which[j]], out.at[j], out_sem.at[j]) for j in range(count)]
    for copy in copies:
        copy.start()
    for copy in copies:
        copy.wait()


def spread(which, patterns):
    count = which.shape[0]
    return pl.pallas_call(
        spread_kernel,
        out_shape=jax.ShapeDtypeStruct((count,) + patterns.shape[1:], F32),
        in_specs=[pl.BlockSpec(memory_space=pltpu.SMEM), pl.BlockSpec(memory_space=pl.ANY)],
        out_specs=pl.BlockSpec(memory_space=pl.ANY),
        scratch_shapes=[
            pltpu.VMEM(patterns.shape, F32),
            pltpu.SemaphoreType.DMA,
            pltpu.SemaphoreType.DMA((count,)),
        ],
    )(which, patterns)


def lookup(table, indices):
    choices = jnp.arange(table.shape[0], dtype=jnp.int32)
    return jnp.sum(jnp.where(indices[..., None] == choices, table, 0), axis=-1)


def per_device(object_tiles, probe_wave, patterns, tile_of, offsets, owner_map):
    tile_count = lax.axis_size("tile")
    pos_dev = tile_of.shape[0]
    high, low, shuffle = tables()
    high, low, shuffle = jnp.asarray(high), jnp.asarray(low), jnp.asarray(shuffle)
    owners = jnp.arange(tile_count, dtype=jnp.int32)
    reads = lookup(owner_map, tile_of)[None, :] == owners[:, None]
    which = jnp.sum(jnp.where(reads, jnp.arange(pos_dev, dtype=jnp.int32), 0), axis=1)
    notes = jnp.stack(
        [jnp.any(reads, axis=1).astype(jnp.int32)]
        + [jnp.sum(jnp.where(reads, offsets[:, axis], 0), axis=1) for axis in range(2)],
        axis=1,
    )
    notes = lax.all_to_all(notes, "tile", split_axis=0, concat_axis=0, tiled=True)
    notes, which = lax.optimization_barrier((notes, which))
    arrived = lax.all_to_all(spread(which, patterns), "tile", split_axis=0, concat_axis=0, tiled=True)
    present = notes[:, 0] > 0
    rank = jnp.sum(jnp.where((owners[None, :] < owners[:, None]) & present[None, :], 1, 0), axis=1)
    chosen = (rank[None, :] == jnp.arange(MAX_READS, dtype=jnp.int32)[:, None]) & present[None, :]
    info = jnp.stack([owners, notes[:, 1], notes[:, 2]])
    info = jnp.sum(jnp.where(chosen[None], info[:, None, :], 0), axis=2).reshape(-1)
    info = jnp.concatenate([info, jnp.sum(notes[:, 0])[None]])
    tile = object_tiles[0]
    back, far = forward(info, tile, probe_wave, high, low)
    tile_grad, probe_part = backward(
        info, tile, probe_wave, high, low, shuffle, back, far, arrived
    )
    object_part = lax.psum_scatter(tile_grad, "scan", scatter_dimension=3, tiled=True)
    probe_total = lax.psum(probe_part, ("scan", "tile"))
    count = tile_count * lax.axis_size("scan") * pos_dev
    return object_part, probe_total / jnp.sqrt(jnp.ones((), F32) * count)


def solution(mesh):
    return jax.shard_map(
        per_device,
        mesh=mesh,
        in_specs=(
            P("tile", None, None, None, None),
            P(),
            P(("scan", "tile"), None, None),
            P(("scan", "tile")),
            P(("scan", "tile"), None),
            P(),
        ),
        out_specs=(P("tile", None, None, "scan", None), P()),
        check_vma=False,
    )
```

```python
import functools
import math

import jax
import jax.numpy as jnp
import ml_dtypes
import numpy as np
from jax import lax
from jax.experimental import pallas as pl
from jax.experimental.pallas import tpu as pltpu
from jax.sharding import PartitionSpec as P

PROP_PHASE = 0.75
SIDE = 256
HALF = 128
MAX_READS = 8
F32 = jnp.float32
BF16 = jnp.bfloat16


def embed(block):
    return np.block([[block.real, block.imag], [-block.imag, block.real]])


@functools.cache
def tables():
    index = np.arange(SIDE)
    freq = np.where(index < HALF, index, index - SIDE).astype(np.float64)
    wave = np.exp(-2j * math.pi * (index[:, None] * index[None, :] % SIDE) / SIDE) / math.sqrt(SIDE)
    step = np.exp(-1j * PROP_PHASE * freq**2 / SIDE)
    travel = wave.conj() @ (step[:, None] * wave)
    plus = (travel[:HALF, :HALF] + travel[:HALF, HALF:]) / 2
    minus = (travel[:HALF, :HALF] - travel[:HALF, HALF:]) / 2
    forms = []
    for block in (plus, minus, wave[:HALF, 0::2], wave[:HALF, 1::2]):
        form = embed(block)
        forms += [form, form.T]
    forms = np.stack(forms)
    high = forms.astype(ml_dtypes.bfloat16)
    low = (forms - high.astype(np.float64)).astype(ml_dtypes.bfloat16)
    shuffle = np.zeros((SIDE, SIDE), ml_dtypes.bfloat16)
    shuffle[2 * np.arange(HALF), np.arange(HALF)] = 1
    shuffle[2 * np.arange(HALF) + 1, HALF + np.arange(HALF)] = 1
    return high, low, shuffle


A_PLUS, A_MINUS, F_EVEN, F_ODD = 0, 2, 4, 6


def parts(x):
    high = x.astype(BF16)
    return high, (x - high.astype(F32)).astype(BF16)


def mm(x, y):
    return jnp.dot(x, y, preferred_element_type=F32)


def right(x, high_ref, low_ref, which):
    xh, xl = parts(x)
    wh, wl = high_ref[which], low_ref[which]
    total = mm(xh, wh)
    total = total + mm(xl, wh)
    return total + mm(xh, wl)


def left(x, high_ref, low_ref, which):
    xh, xl = parts(x)
    wh, wl = high_ref[which], low_ref[which]
    total = mm(wh, xh)
    total = total + mm(wl, xh)
    return total + mm(wh, xl)


def cols(re, im):
    return (
        jnp.concatenate([re[:, :HALF] + re[:, HALF:], im[:, :HALF] + im[:, HALF:]], axis=1),
        jnp.concatenate([re[:, :HALF] - re[:, HALF:], im[:, :HALF] - im[:, HALF:]], axis=1),
    )


def rows(re, im):
    return (
        jnp.concatenate([re[:HALF] + re[HALF:], im[:HALF] + im[HALF:]], axis=0),
        jnp.concatenate([re[:HALF] - re[HALF:], im[:HALF] - im[HALF:]], axis=0),
    )


def split_cols(p, q):
    return (
        jnp.concatenate([p[:, :HALF], q[:, :HALF]], axis=1),
        jnp.concatenate([p[:, HALF:], q[:, HALF:]], axis=1),
    )


def split_rows(p, q):
    return (
        jnp.concatenate([p[:HALF], q[:HALF]], axis=0),
        jnp.concatenate([p[HALF:], q[HALF:]], axis=0),
    )


def travel(re, im, hi, lo, conj):
    flip = 1 if conj else 0
    s, d = cols(re, im)
    p, q = right(s, hi, lo, A_PLUS + flip), right(d, hi, lo, A_MINUS + flip)
    re, im = split_cols(p + q, p - q)
    s, d = rows(re, im)
    p, q = left(s, hi, lo, A_PLUS + 1 - flip), left(d, hi, lo, A_MINUS + 1 - flip)
    return split_rows(p + q, p - q)


def to_far(re, im, hi, lo):
    s, d = cols(re, im)
    re, im = split_cols(right(s, hi, lo, F_EVEN), right(d, hi, lo, F_ODD))
    s, d = rows(re, im)
    return split_rows(left(s, hi, lo, F_EVEN + 1), left(d, hi, lo, F_ODD + 1))


def from_far(re, im, hi, lo):
    even, odd = (
        jnp.concatenate([re[:, :HALF], im[:, :HALF]], axis=1),
        jnp.concatenate([re[:, HALF:], im[:, HALF:]], axis=1),
    )
    p, q = right(even, hi, lo, F_EVEN + 1), right(odd, hi, lo, F_ODD + 1)
    re, im = split_cols(p + q, p - q)
    even, odd = (
        jnp.concatenate([re[:HALF], im[:HALF]], axis=0),
        jnp.concatenate([re[HALF:], im[HALF:]], axis=0),
    )
    p, q = left(even, hi, lo, F_EVEN), left(odd, hi, lo, F_ODD)
    return split_rows(p + q, p - q)


def lane_mask(shift):
    return lax.broadcasted_iota(jnp.int32, (SIDE, HALF), 1) < shift


def spots(a, b):
    base = b // HALF
    return [pl.ds(4 * a + jnp.minimum(base + k, 3), SIDE, stride=4) for k in range(3)]


def patch(plane, a, b):
    shift = b % HALF
    back = lax.rem(HALF - shift, HALF)
    tiles = [pltpu.roll(plane[spot, :], back, 1) for spot in spots(a, b)]
    mask = lane_mask(HALF - shift)
    return jnp.concatenate(
        [jnp.where(mask, tiles[0], tiles[1]), jnp.where(mask, tiles[1], tiles[2])], axis=1
    )


def add_patch(plane, a, b, value):
    shift = b % HALF
    first, second = pltpu.roll(value[:, :HALF], shift, 1), pltpu.roll(value[:, HALF:], shift, 1)
    mask = lane_mask(shift)
    zero = jnp.zeros_like(first)
    terms = [jnp.where(mask, zero, first), jnp.where(mask, first, second), jnp.where(mask, second, zero)]
    for spot, term in zip(spots(a, b), terms):
        plane[spot, :] = plane[spot, :] + term


def open_tile(tile, held):
    for plane in range(4):
        for k in range(4):
            held[plane, pl.ds(k, 2 * SIDE, stride=4), :] = tile[
                plane // 2, plane % 2, :, k * HALF : (k + 1) * HALF
            ]


def close_tile(held, grad):
    for plane in range(4):
        for k in range(4):
            grad[0, plane // 2, plane % 2, :, k * HALF : (k + 1) * HALF] = held[
                plane, pl.ds(k, 2 * SIDE, stride=4), :
            ]


def forward_kernel(info, tile, probe, hi, lo, back, far, held):
    k = pl.program_id(0)

    @pl.when(k == 0)
    def _():
        open_tile(tile, held)

    @pl.when(k < info[3 * MAX_READS])
    def _():
        a, b = info[MAX_READS + k], info[2 * MAX_READS + k]
        ore, oim = patch(held.at[0], a, b), patch(held.at[1], a, b)
        pre, pim = probe[0], probe[1]
        re, im = travel(pre * ore - pim * oim, pre * oim + pim * ore, hi, lo, False)
        back[0, 0], back[0, 1] = re, im
        ore, oim = patch(held.at[2], a, b), patch(held.at[3], a, b)
        far[0, 0], far[0, 1] = to_far(re * ore - im * oim, re * oim + im * ore, hi, lo)


def backward_kernel(
    info, tile, probe, hi, lo, shuffle, back, far, pattern, grad, probe_grad, held, total, mixed
):
    k = pl.program_id(0)

    @pl.when(k == 0)
    def _():
        open_tile(tile, held)
        total[...] = jnp.zeros_like(total)
        probe_grad[...] = jnp.zeros_like(probe_grad)

    @pl.when(k < info[3 * MAX_READS])
    def _():
        a, b = info[MAX_READS + k], info[2 * MAX_READS + k]
        for c in range(2):
            mixed[c] = pattern[0, :, c * HALF : (c + 1) * HALF]
        measured = jnp.concatenate(
            [
                jnp.concatenate([mixed[c, pl.ds(odd, HALF, stride=2), :] for c in range(2)], axis=1)
                for odd in range(2)
            ],
            axis=0,
        )
        mh, ml = parts(measured)
        measured = mm(mh, shuffle[...]) + mm(ml, shuffle[...])
        fre, fim = far[0, 0], far[0, 1]
        scale = 2.0 * (fre * fre + fim * fim - measured)
        gre, gim = from_far(scale * fre, scale * fim, hi, lo)
        bre, bim = back[0, 0], back[0, 1]
        add_patch(total.at[2], a, b, bre * gre + bim * gim)
        add_patch(total.at[3], a, b, bre * gim - bim * gre)
        ore, oim = patch(held.at[2], a, b), patch(held.at[3], a, b)
        gre, gim = travel(ore * gre + oim * gim, ore * gim - oim * gre, hi, lo, True)
        pre, pim = probe[0], probe[1]
        add_patch(total.at[0], a, b, pre * gre + pim * gim)
        add_patch(total.at[1], a, b, pre * gim - pim * gre)
        ore, oim = patch(held.at[0], a, b), patch(held.at[1], a, b)
        probe_grad[0] += ore * gre + oim * gim
        probe_grad[1] += ore * gim - oim * gre

    @pl.when(k == pl.num_programs(0) - 1)
    def _():
        close_tile(total, grad)


def plane_scratch():
    return pltpu.VMEM((4, 2 * SIDE * 4, HALF), F32)


def whole(array):
    ndim = array.ndim
    return pl.BlockSpec(array.shape, lambda k, info: (0,) * ndim, pipeline_mode=pl.Buffered(1))


def forward(info, tile, probe, hi, lo):
    block = pl.BlockSpec((1, 2, SIDE, SIDE), lambda k, info: (k, 0, 0, 0))
    out = jax.ShapeDtypeStruct((MAX_READS, 2, SIDE, SIDE), F32)
    return pl.pallas_call(
        forward_kernel,
        out_shape=(out, out),
        grid_spec=pltpu.PrefetchScalarGridSpec(
            num_scalar_prefetch=1,
            grid=(MAX_READS,),
            in_specs=[whole(x) for x in (tile, probe, hi, lo)],
            out_specs=(block, block),
            scratch_shapes=[plane_scratch()],
        ),
        cost_estimate=pl.CostEstimate(
            flops=MAX_READS * 24 * 2 * SIDE**3, bytes_accessed=14 << 20, transcendentals=0
        ),
        compiler_params=pltpu.CompilerParams(vmem_limit_bytes=48 << 20),
    )(info, tile, probe, hi, lo)


def backward(info, tile, probe, hi, lo, shuffle, back, far, arrived):
    block = pl.BlockSpec((1, 2, SIDE, SIDE), lambda k, info: (k, 0, 0, 0))
    pattern = pl.BlockSpec((1, SIDE, SIDE), lambda k, info: (info[k], 0, 0))
    grad = jax.ShapeDtypeStruct((1,) + tile.shape, F32)
    probe_grad = jax.ShapeDtypeStruct(probe.shape, F32)
    return pl.pallas_call(
        backward_kernel,
        out_shape=(grad, probe_grad),
        grid_spec=pltpu.PrefetchScalarGridSpec(
            num_scalar_prefetch=1,
            grid=(MAX_READS,),
            in_specs=[whole(x) for x in (tile, probe, hi, lo, shuffle)] + [block, block, pattern],
            out_specs=(whole(grad), whole(probe_grad)),
            scratch_shapes=[plane_scratch(), plane_scratch(), pltpu.VMEM((2, SIDE, HALF), F32)],
        ),
        cost_estimate=pl.CostEstimate(
            flops=MAX_READS * 26 * 2 * SIDE**3, bytes_accessed=20 << 20, transcendentals=0
        ),
        compiler_params=pltpu.CompilerParams(vmem_limit_bytes=48 << 20),
    )(info, tile, probe, hi, lo, shuffle, back, far, arrived)


def spread_kernel(which, patterns, out, held, in_sem, out_sem):
    count = out.shape[0]
    load = pltpu.make_async_copy(patterns, held, in_sem)
    load.start()
    load.wait()
    copies = [pltpu.make_async_copy(held.at[which[j]], out.at[j], out_sem.at[j]) for j in range(count)]
    for copy in copies:
        copy.start()
    for copy in copies:
        copy.wait()


def spread(which, patterns):
    count = which.shape[0]
    return pl.pallas_call(
        spread_kernel,
        out_shape=jax.ShapeDtypeStruct((count,) + patterns.shape[1:], F32),
        in_specs=[pl.BlockSpec(memory_space=pltpu.SMEM), pl.BlockSpec(memory_space=pl.ANY)],
        out_specs=pl.BlockSpec(memory_space=pl.ANY),
        scratch_shapes=[
            pltpu.VMEM(patterns.shape, F32),
            pltpu.SemaphoreType.DMA,
            pltpu.SemaphoreType.DMA((count,)),
        ],
    )(which, patterns)


MESH = pl.DeviceIdType.MESH
CORES = 2


def reduce_kernel(
    zs, xs, ys, grad, probe, out, probe_out,
    own, core_in, half_in, direct_in, plane_in, piece_in, piece_z,
    load_sem, core_send, core_recv, ring_send, ring_recv, probe_send, probe_recv, z_send, z_recv,
    all_send, all_recv, pair_send, pair_recv,
):
    scan, tile = lax.axis_index("scan"), lax.axis_index("tile")
    z, c = scan // CORES, scan % CORES
    x, y = tile // ys, tile % ys
    height = out.shape[3]
    piece = piece_z.shape[1]

    def at_z(step):
        return {"scan": lax.rem(z + step + zs, zs) * CORES + c}

    def at_xy(j):
        return {"tile": lax.rem(x + j // ys, xs) * ys + lax.rem(y + j % ys, ys)}

    pair = {"scan": z * CORES + 1 - c}
    shifts = range(1, xs * ys)
    steps = [2, 1, -1, 0]

    def rows_of(step, core):
        return pl.ds(pl.multiple_of((lax.rem(z + step + zs, zs) * CORES + core) * height, height), height)

    barrier = pltpu.get_barrier_semaphore()
    partners = [pair] + [at_z(step) for step in (1, 2, 3)] + [at_xy(j) for j in shifts]
    for partner in partners:
        pl.semaphore_signal(barrier, inc=1, device_id=partner, device_id_type=MESH)
    loads = [
        pltpu.make_async_copy(grad.at[0, :, :, rows_of(step, c), :], own.at[k], load_sem.at[k])
        for k, step in enumerate(steps)
    ]
    for load in loads:
        load.start()
    pl.semaphore_wait(barrier, len(partners))

    def remote(src, dst, send, recv, device):
        return pltpu.make_async_remote_copy(
            src_ref=src, dst_ref=dst, send_sem=send, recv_sem=recv, device_id=device, device_id_type=MESH
        )

    started = []

    def go(copy):
        copy.start()
        started.append(copy)
        return copy

    probe_pair = go(remote(probe.at[1 - c], plane_in, core_send.at[4], core_recv.at[4], pair))
    cores = [
        go(remote(grad.at[0, :, :, rows_of(step, 1 - c), :], core_in.at[k], core_send.at[k], core_recv.at[k], pair))
        for k, step in enumerate(steps)
    ]

    def merge(k):
        loads[k].wait()
        cores[k].wait_recv()
        own[k] = own[k] + core_in[k]

    merge(0)
    halves = [
        go(remote(own.at[0, 0], half_in.at[0], ring_send.at[0], ring_recv.at[0], at_z(1))),
        go(remote(own.at[0, 1], half_in.at[1], ring_send.at[1], ring_recv.at[1], at_z(-1))),
    ]
    probe_pair.wait_recv()
    plane_in[...] = plane_in[...] + probe[c]

    def piece_rows(device):
        return pl.ds(pl.multiple_of(device["tile"] * piece, piece), piece)

    gathers = [
        go(remote(plane_in.at[piece_rows(at_xy(j))], piece_in.at[j], probe_send.at[j], probe_recv.at[j], at_xy(j)))
        for j in shifts
    ]
    merge(1)
    up = go(remote(own.at[1, 1], direct_in.at[0], ring_send.at[2], ring_recv.at[2], at_z(1)))
    merge(2)
    down = go(remote(own.at[2, 0], direct_in.at[1], ring_send.at[3], ring_recv.at[3], at_z(-1)))
    halves[0].wait_recv()
    own[1, 0] = own[1, 0] + half_in[0]
    up_sum = go(remote(own.at[1, 0], direct_in.at[2], ring_send.at[4], ring_recv.at[4], at_z(1)))
    halves[1].wait_recv()
    own[2, 1] = own[2, 1] + half_in[1]
    down_sum = go(remote(own.at[2, 1], direct_in.at[3], ring_send.at[5], ring_recv.at[5], at_z(-1)))

    total = plane_in[piece_rows({"tile": tile}), :]
    for copy, j in zip(gathers, shifts):
        copy.wait_recv()
        total = total + piece_in[j]
    piece_z[0] = total
    across = [go(remote(piece_z.at[0], piece_z.at[k], z_send.at[k], z_recv.at[k], at_z(k))) for k in (1, 2, 3)]
    merge(3)
    for copy in across:
        copy.wait_recv()
    mine = piece_rows({"tile": tile})
    probe_out[c, mine, :] = (piece_z[0] + piece_z[1]) + (piece_z[2] + piece_z[3])
    spreads = [
        go(remote(probe_out.at[c, mine], probe_out.at[c, mine], all_send.at[j], all_recv.at[j], at_xy(j)))
        for j in shifts
    ]
    for copy in spreads:
        copy.wait_recv()
    last = go(remote(probe_out.at[c], probe_out.at[c], pair_send, pair_recv, pair))
    up.wait_recv()
    down.wait_recv()
    up_sum.wait_recv()
    down_sum.wait_recv()
    out[0, 0] = own[3, 0] + (direct_in[2] + direct_in[1])
    out[0, 1] = own[3, 1] + (direct_in[0] + direct_in[3])
    last.wait_recv()
    for copy in started:
        copy.wait_send()


def reduce_all(sizes, grad, probe):
    zs, xs, ys = sizes
    tiles = xs * ys
    slices, comps, side, width = grad.shape[1:]
    height = side // (zs * CORES)
    piece = SIDE // tiles
    dma = pltpu.SemaphoreType.DMA
    return pl.pallas_call(
        functools.partial(reduce_kernel, zs, xs, ys),
        out_shape=(
            jax.ShapeDtypeStruct((1, slices, comps, height, width), F32),
            jax.ShapeDtypeStruct(probe.shape, F32),
        ),
        in_specs=[pl.BlockSpec(memory_space=pl.ANY), pl.BlockSpec(memory_space=pltpu.VMEM)],
        out_specs=(pl.BlockSpec(memory_space=pltpu.VMEM),) * 2,
        scratch_shapes=[
            pltpu.VMEM((4, slices, comps, height, width), F32),
            pltpu.VMEM((4, slices, comps, height, width), F32),
            pltpu.VMEM((2, comps, height, width), F32),
            pltpu.VMEM((4, comps, height, width), F32),
            pltpu.VMEM((SIDE, SIDE), F32),
            pltpu.VMEM((tiles, piece, SIDE), F32),
            pltpu.VMEM((4, piece, SIDE), F32),
            dma((4,)), dma((5,)), dma((5,)), dma((6,)), dma((6,)), dma((tiles,)), dma((tiles,)),
            dma((4,)), dma((4,)), dma((tiles,)), dma((tiles,)), dma, dma,
        ],
        compiler_params=pltpu.CompilerParams(
            collective_id=1, has_side_effects=True, vmem_limit_bytes=32 << 20
        ),
    )(grad, probe)


def lookup(table, indices):
    choices = jnp.arange(table.shape[0], dtype=jnp.int32)
    return jnp.sum(jnp.where(indices[..., None] == choices, table, 0), axis=-1)


def per_device(object_tiles, probe_wave, patterns, tile_of, offsets, owner_map):
    tile_count = lax.axis_size("tile")
    pos_dev = tile_of.shape[0]
    high, low, shuffle = tables()
    high, low, shuffle = jnp.asarray(high), jnp.asarray(low), jnp.asarray(shuffle)
    owners = jnp.arange(tile_count, dtype=jnp.int32)
    reads = lookup(owner_map, tile_of)[None, :] == owners[:, None]
    which = jnp.sum(jnp.where(reads, jnp.arange(pos_dev, dtype=jnp.int32), 0), axis=1)
    notes = jnp.stack(
        [jnp.any(reads, axis=1).astype(jnp.int32)]
        + [jnp.sum(jnp.where(reads, offsets[:, axis], 0), axis=1) for axis in range(2)],
        axis=1,
    )
    notes = lax.all_to_all(notes, "tile", split_axis=0, concat_axis=0, tiled=True)
    notes, which = lax.optimization_barrier((notes, which))
    arrived = lax.all_to_all(spread(which, patterns), "tile", split_axis=0, concat_axis=0, tiled=True)
    present = notes[:, 0] > 0
    rank = jnp.sum(jnp.where((owners[None, :] < owners[:, None]) & present[None, :], 1, 0), axis=1)
    chosen = (rank[None, :] == jnp.arange(MAX_READS, dtype=jnp.int32)[:, None]) & present[None, :]
    info = jnp.stack([owners, notes[:, 1], notes[:, 2]])
    info = jnp.sum(jnp.where(chosen[None], info[:, None, :], 0), axis=2).reshape(-1)
    info = jnp.concatenate([info, jnp.sum(notes[:, 0])[None]])
    tile = object_tiles[0]
    back, far = forward(info, tile, probe_wave, high, low)
    tile_grad, probe_part = backward(
        info, tile, probe_wave, high, low, shuffle, back, far, arrived
    )
    zs, xs = lax.axis_size("scan") // CORES, math.isqrt(tile_count)
    object_part, probe_total = reduce_all((zs, xs, tile_count // xs), tile_grad, probe_part)
    count = tile_count * lax.axis_size("scan") * pos_dev
    return object_part, probe_total / jnp.sqrt(jnp.ones((), F32) * count)


def solution(mesh):
    return jax.shard_map(
        per_device,
        mesh=mesh,
        in_specs=(
            P("tile", None, None, None, None),
            P(),
            P(("scan", "tile"), None, None),
            P(("scan", "tile")),
            P(("scan", "tile"), None),
            P(),
        ),
        out_specs=(P("tile", None, None, "scan", None), P()),
        check_vma=False,
    )
```

```python
import functools
import math

import jax
import jax.numpy as jnp
import ml_dtypes
import numpy as np
from jax import lax
from jax.experimental import pallas as pl
from jax.experimental.pallas import tpu as pltpu
from jax.sharding import PartitionSpec as P

PROP_PHASE = 0.75
SIDE = 256
HALF = 128
MAX_READS = 8
F32 = jnp.float32
BF16 = jnp.bfloat16


def embed(block):
    return np.block([[block.real, block.imag], [-block.imag, block.real]])


@functools.cache
def tables():
    index = np.arange(SIDE)
    freq = np.where(index < HALF, index, index - SIDE).astype(np.float64)
    wave = np.exp(-2j * math.pi * (index[:, None] * index[None, :] % SIDE) / SIDE) / math.sqrt(SIDE)
    step = np.exp(-1j * PROP_PHASE * freq**2 / SIDE)
    travel = wave.conj() @ (step[:, None] * wave)
    plus = (travel[:HALF, :HALF] + travel[:HALF, HALF:]) / 2
    minus = (travel[:HALF, :HALF] - travel[:HALF, HALF:]) / 2
    forms = []
    for block in (plus, minus, wave[:HALF, 0::2], wave[:HALF, 1::2]):
        form = embed(block)
        forms += [form, form.T]
    forms = np.stack(forms)
    high = forms.astype(ml_dtypes.bfloat16)
    low = (forms - high.astype(np.float64)).astype(ml_dtypes.bfloat16)
    shuffle = np.zeros((SIDE, SIDE), ml_dtypes.bfloat16)
    shuffle[2 * np.arange(HALF), np.arange(HALF)] = 1
    shuffle[2 * np.arange(HALF) + 1, HALF + np.arange(HALF)] = 1
    return high, low, shuffle


A_PLUS, A_MINUS, F_EVEN, F_ODD = 0, 2, 4, 6


def parts(x):
    high = x.astype(BF16)
    return high, (x - high.astype(F32)).astype(BF16)


def mm(x, y):
    return jnp.dot(x, y, preferred_element_type=F32)


def right(x, high_ref, low_ref, which):
    xh, xl = parts(x)
    wh, wl = high_ref[which], low_ref[which]
    total = mm(xh, wh)
    total = total + mm(xl, wh)
    return total + mm(xh, wl)


def left(x, high_ref, low_ref, which):
    xh, xl = parts(x)
    wh, wl = high_ref[which], low_ref[which]
    total = mm(wh, xh)
    total = total + mm(wl, xh)
    return total + mm(wh, xl)


def cols(re, im):
    return (
        jnp.concatenate([re[:, :HALF] + re[:, HALF:], im[:, :HALF] + im[:, HALF:]], axis=1),
        jnp.concatenate([re[:, :HALF] - re[:, HALF:], im[:, :HALF] - im[:, HALF:]], axis=1),
    )


def rows(re, im):
    return (
        jnp.concatenate([re[:HALF] + re[HALF:], im[:HALF] + im[HALF:]], axis=0),
        jnp.concatenate([re[:HALF] - re[HALF:], im[:HALF] - im[HALF:]], axis=0),
    )


def split_cols(p, q):
    return (
        jnp.concatenate([p[:, :HALF], q[:, :HALF]], axis=1),
        jnp.concatenate([p[:, HALF:], q[:, HALF:]], axis=1),
    )


def split_rows(p, q):
    return (
        jnp.concatenate([p[:HALF], q[:HALF]], axis=0),
        jnp.concatenate([p[HALF:], q[HALF:]], axis=0),
    )


def travel(re, im, hi, lo, conj):
    flip = 1 if conj else 0
    s, d = cols(re, im)
    p, q = right(s, hi, lo, A_PLUS + flip), right(d, hi, lo, A_MINUS + flip)
    re, im = split_cols(p + q, p - q)
    s, d = rows(re, im)
    p, q = left(s, hi, lo, A_PLUS + 1 - flip), left(d, hi, lo, A_MINUS + 1 - flip)
    return split_rows(p + q, p - q)


def to_far(re, im, hi, lo):
    s, d = cols(re, im)
    re, im = split_cols(right(s, hi, lo, F_EVEN), right(d, hi, lo, F_ODD))
    s, d = rows(re, im)
    return split_rows(left(s, hi, lo, F_EVEN + 1), left(d, hi, lo, F_ODD + 1))


def from_far(re, im, hi, lo):
    even, odd = (
        jnp.concatenate([re[:, :HALF], im[:, :HALF]], axis=1),
        jnp.concatenate([re[:, HALF:], im[:, HALF:]], axis=1),
    )
    p, q = right(even, hi, lo, F_EVEN + 1), right(odd, hi, lo, F_ODD + 1)
    re, im = split_cols(p + q, p - q)
    even, odd = (
        jnp.concatenate([re[:HALF], im[:HALF]], axis=0),
        jnp.concatenate([re[HALF:], im[HALF:]], axis=0),
    )
    p, q = left(even, hi, lo, F_EVEN), left(odd, hi, lo, F_ODD)
    return split_rows(p + q, p - q)


def lane_mask(shift):
    return lax.broadcasted_iota(jnp.int32, (SIDE, HALF), 1) < shift


def spots(a, b):
    base = b // HALF
    return [pl.ds(4 * a + jnp.minimum(base + k, 3), SIDE, stride=4) for k in range(3)]


def patch(plane, a, b):
    shift = b % HALF
    back = lax.rem(HALF - shift, HALF)
    tiles = [pltpu.roll(plane[spot, :], back, 1) for spot in spots(a, b)]
    mask = lane_mask(HALF - shift)
    return jnp.concatenate(
        [jnp.where(mask, tiles[0], tiles[1]), jnp.where(mask, tiles[1], tiles[2])], axis=1
    )


def add_patch(plane, a, b, value):
    shift = b % HALF
    first, second = pltpu.roll(value[:, :HALF], shift, 1), pltpu.roll(value[:, HALF:], shift, 1)
    mask = lane_mask(shift)
    zero = jnp.zeros_like(first)
    terms = [jnp.where(mask, zero, first), jnp.where(mask, first, second), jnp.where(mask, second, zero)]
    for spot, term in zip(spots(a, b), terms):
        plane[spot, :] = plane[spot, :] + term


def open_tile(tile, held):
    for plane in range(4):
        for k in range(4):
            held[plane, pl.ds(k, 2 * SIDE, stride=4), :] = tile[
                plane // 2, plane % 2, :, k * HALF : (k + 1) * HALF
            ]


def forward_one(a, b, held, probe, hi, lo):
    ore, oim = patch(held.at[0], a, b), patch(held.at[1], a, b)
    pre, pim = probe[0], probe[1]
    back = travel(pre * ore - pim * oim, pre * oim + pim * ore, hi, lo, False)
    ore, oim = patch(held.at[2], a, b), patch(held.at[3], a, b)
    re, im = back
    return back, to_far(re * ore - im * oim, re * oim + im * ore, hi, lo)


MESH = pl.DeviceIdType.MESH
CORES = 2


def remote(src, dst, send, recv, device):
    return pltpu.make_async_remote_copy(
        src_ref=src, dst_ref=dst, send_sem=send, recv_sem=recv, device_id=device, device_id_type=MESH
    )


def plane_steps(xs, ys):
    tile = lax.axis_index("tile")
    x, y = tile // ys, tile % ys

    def at_xy(j):
        return {"tile": lax.rem(x + j // ys, xs) * ys + lax.rem(y + j % ys, ys)}

    return tile, at_xy, range(1, xs * ys)


def read_lists(notes, tables_ref):
    count = notes.shape[0]
    note = notes[:, 0, :]
    owner = lax.broadcasted_iota(jnp.int32, note.shape, 1)
    source = lax.broadcasted_iota(jnp.int32, note.shape, 0)
    here = jnp.zeros(note.shape, jnp.int32)
    values = [jnp.zeros(note.shape, jnp.int32) for _ in range(3)]
    for i in range(4):
        hit = jnp.where(jnp.broadcast_to(note[:, i : i + 1], note.shape) == owner, 1, 0)
        here = here + hit
        fields = [4 * source + i] + [
            jnp.broadcast_to(note[:, 4 * f + i : 4 * f + i + 1], note.shape) for f in (1, 2)
        ]
        values = [v + hit * f for v, f in zip(values, fields)]
    lower = (
        lax.broadcasted_iota(jnp.int32, (count, count), 0) > lax.broadcasted_iota(jnp.int32, (count, count), 1)
    ).astype(F32)
    rank = mm(lower.astype(BF16), here.astype(F32).astype(BF16)).astype(jnp.int32)
    for k in range(MAX_READS):
        chosen = here * jnp.where(rank == k, 1, 0)
        for f in range(3):
            row = MAX_READS * f + k
            tables_ref[row : row + 1, :] = jnp.sum(chosen * values[f], axis=0, keepdims=True)
    tables_ref[24:25, :] = jnp.sum(here, axis=0, keepdims=True)


def exchange_kernel(
    xs, ys, tile_of, offsets, owner_map, patterns, tile, probe_hbm, hi_hbm, lo_hbm,
    held, arrived, back, far, info,
    opened, probe, hi, lo, notes, lists, lists_smem, mid, stage,
    load_sem, own_sem, list_sem, note_send, note_recv, first_send, first_recv, second_send, second_recv,
):
    me, at_xy, shifts = plane_steps(xs, ys)
    piece = mid.shape[1]
    reads = patterns.shape[0]

    def piece_rows(index):
        return pl.ds(pl.multiple_of(index * piece, piece), piece)

    barrier = pltpu.get_barrier_semaphore()
    for j in shifts:
        pl.semaphore_signal(barrier, inc=1, device_id=at_xy(j), device_id_type=MESH)
    loads = [
        pltpu.make_async_copy(src, dst, load_sem.at[k])
        for k, (src, dst) in enumerate(
            [(tile, opened), (probe_hbm, probe), (hi_hbm, hi), (lo_hbm, lo)]
        )
    ]
    for load in loads:
        load.start()
    own = pltpu.make_async_copy(
        patterns.at[:, piece_rows(me), :], mid.at[pl.ds(reads * me, reads)], own_sem
    )
    own.start()
    lane = lax.broadcasted_iota(jnp.int32, (1, HALF), 1)
    note = jnp.zeros((1, HALF), jnp.int32)
    for i in range(reads):
        for f, value in enumerate((owner_map[tile_of[i]], offsets[i, 0], offsets[i, 1])):
            note = jnp.where(lane == 4 * f + i, value, note)
    notes[me] = note
    pl.semaphore_wait(barrier, len(shifts))

    tells = [
        remote(notes.at[me], notes.at[me], note_send.at[j], note_recv.at[j], at_xy(j)) for j in shifts
    ]
    firsts = [
        remote(
            patterns.at[:, piece_rows(at_xy(j)["tile"]), :], mid.at[pl.ds(reads * me, reads)],
            first_send.at[j], first_recv.at[j], at_xy(j),
        )
        for j in shifts
    ]
    for copy in tells + firsts:
        copy.start()
    loads[0].wait()
    open_tile(opened.at[0], held)
    for copy in tells:
        copy.wait_recv()
    lists[...] = jnp.zeros_like(lists)
    read_lists(notes, lists)
    listed = pltpu.make_async_copy(lists, lists_smem, list_sem)
    listed.start()
    listed.wait()
    for row in range(3):
        for k in range(MAX_READS):
            info[row, k] = lists_smem[MAX_READS * row + k, me]
    for k in range(MAX_READS):
        info[3, k] = lists_smem[24, me]
    own.wait()
    for copy in firsts:
        copy.wait_recv()
    seconds = []
    for j in shifts:
        to = at_xy(j)["tile"]
        for k in range(MAX_READS):
            stage[j, k] = mid[lists_smem[k, to]]
        copy = remote(
            stage.at[j], arrived.at[:, piece_rows(me), :], second_send.at[j], second_recv.at[j], at_xy(j)
        )
        copy.start()
        seconds.append(copy)
    for k in range(MAX_READS):
        arrived[k, piece_rows(me), :] = mid[lists_smem[k, me]]
    for load in loads[1:]:
        load.wait()

    def one(k, carry):
        a, b = lists_smem[MAX_READS + k, me], lists_smem[2 * MAX_READS + k, me]
        (bre, bim), (fre, fim) = forward_one(a, b, held, probe, hi, lo)
        back[k, 0], back[k, 1], far[k, 0], far[k, 1] = bre, bim, fre, fim
        return carry

    lax.fori_loop(0, MAX_READS, one, 0)
    for copy in seconds:
        copy.wait_recv()
    for copy in tells + firsts + seconds:
        copy.wait_send()


def exchange(xs, ys, tile_of, offsets, owner_map, patterns, tile, probe, hi, lo):
    tiles = xs * ys
    piece = SIDE // tiles
    reads = patterns.shape[0]
    dma = pltpu.SemaphoreType.DMA
    vmem, smem, hbm = (
        pl.BlockSpec(memory_space=space) for space in (pltpu.VMEM, pltpu.SMEM, pl.ANY)
    )
    field = jax.ShapeDtypeStruct((MAX_READS, 2, SIDE, SIDE), F32)
    return pl.pallas_call(
        functools.partial(exchange_kernel, xs, ys),
        out_shape=(
            jax.ShapeDtypeStruct((4, 2 * SIDE * 4, HALF), F32),
            jax.ShapeDtypeStruct((MAX_READS, SIDE, SIDE), F32),
            field,
            field,
            jax.ShapeDtypeStruct((4, MAX_READS), jnp.int32),
        ),
        in_specs=[smem, smem, smem] + [hbm] * 5,
        out_specs=(vmem, vmem, vmem, vmem, smem),
        scratch_shapes=[
            pltpu.VMEM(tile.shape, F32),
            pltpu.VMEM(probe.shape, F32),
            pltpu.VMEM(hi.shape, BF16),
            pltpu.VMEM(lo.shape, BF16),
            pltpu.VMEM((tiles, 1, HALF), jnp.int32),
            pltpu.VMEM((32, HALF), jnp.int32),
            pltpu.SMEM((32, HALF), jnp.int32),
            pltpu.VMEM((tiles * reads, piece, SIDE), F32),
            pltpu.VMEM((tiles, MAX_READS, piece, SIDE), F32),
            dma((4,)), dma, dma, dma((tiles,)), dma((tiles,)), dma((tiles,)), dma((tiles,)),
            dma((tiles,)), dma((tiles,)),
        ],
        cost_estimate=pl.CostEstimate(flops=MAX_READS * 24 * 2 * SIDE**3, bytes_accessed=14 << 20, transcendentals=0),
        compiler_params=pltpu.CompilerParams(
            collective_id=0, has_side_effects=True, vmem_limit_bytes=40 << 20
        ),
    )(tile_of, offsets, owner_map, patterns, tile, probe, hi, lo)


def backward_kernel(
    info, held, probe, hi, lo, shuffle, back, far, arrived, total, probe_grad, mixed
):
    total[...] = jnp.zeros_like(total)
    probe_grad[...] = jnp.zeros_like(probe_grad)

    def one(k, carry):
        a, b = info[1, k], info[2, k]
        for c in range(2):
            mixed[c] = arrived[k, :, c * HALF : (c + 1) * HALF]
        measured = jnp.concatenate(
            [
                jnp.concatenate([mixed[c, pl.ds(odd, HALF, stride=2), :] for c in range(2)], axis=1)
                for odd in range(2)
            ],
            axis=0,
        )
        mh, ml = parts(measured)
        measured = mm(mh, shuffle[...]) + mm(ml, shuffle[...])
        fre, fim = far[k, 0], far[k, 1]
        scale = 2.0 * (fre * fre + fim * fim - measured)
        gre, gim = from_far(scale * fre, scale * fim, hi, lo)
        bre, bim = back[k, 0], back[k, 1]
        add_patch(total.at[2], a, b, bre * gre + bim * gim)
        add_patch(total.at[3], a, b, bre * gim - bim * gre)
        ore, oim = patch(held.at[2], a, b), patch(held.at[3], a, b)
        gre, gim = travel(ore * gre + oim * gim, ore * gim - oim * gre, hi, lo, True)
        pre, pim = probe[0], probe[1]
        add_patch(total.at[0], a, b, pre * gre + pim * gim)
        add_patch(total.at[1], a, b, pre * gim - pim * gre)
        ore, oim = patch(held.at[0], a, b), patch(held.at[1], a, b)
        probe_grad[0] += ore * gre + oim * gim
        probe_grad[1] += ore * gim - oim * gre
        return carry

    lax.fori_loop(0, info[3, 0], one, 0)


def backward(info, held, probe, hi, lo, shuffle, back, far, arrived):
    vmem, smem = pl.BlockSpec(memory_space=pltpu.VMEM), pl.BlockSpec(memory_space=pltpu.SMEM)
    return pl.pallas_call(
        backward_kernel,
        out_shape=(jax.ShapeDtypeStruct(held.shape, F32), jax.ShapeDtypeStruct(probe.shape, F32)),
        in_specs=[smem] + [vmem] * 8,
        out_specs=(vmem, vmem),
        scratch_shapes=[pltpu.VMEM((2, SIDE, HALF), F32)],
        cost_estimate=pl.CostEstimate(flops=MAX_READS * 26 * 2 * SIDE**3, bytes_accessed=20 << 20, transcendentals=0),
        compiler_params=pltpu.CompilerParams(vmem_limit_bytes=40 << 20),
    )(info, held, probe, hi, lo, shuffle, back, far, arrived)


def reduce_kernel(
    zs, xs, ys, grad, probe, out, probe_out,
    own, core_in, half_in, direct_in, plane_in, piece_in, piece_z,
    load_sem, core_send, core_recv, ring_send, ring_recv, probe_send, probe_recv, z_send, z_recv,
    all_send, all_recv, pair_send, pair_recv,
):
    scan = lax.axis_index("scan")
    z, c = scan // CORES, scan % CORES
    tile, at_xy, shifts = plane_steps(xs, ys)
    height = own.shape[3]
    piece = piece_z.shape[1]

    def at_z(step):
        return {"scan": lax.rem(z + step + zs, zs) * CORES + c}

    pair = {"scan": z * CORES + 1 - c}
    steps = [2, 1, -1, 0]

    def rows_of(step, core):
        return pl.ds(pl.multiple_of((lax.rem(z + step + zs, zs) * CORES + core) * height, height), height)

    barrier = pltpu.get_barrier_semaphore()
    partners = [pair] + [at_z(step) for step in (1, 2, 3)] + [at_xy(j) for j in shifts]
    for partner in partners:
        pl.semaphore_signal(barrier, inc=1, device_id=partner, device_id_type=MESH)
    loads = [
        pltpu.make_async_copy(grad.at[:, :, rows_of(step, c), :], own.at[k], load_sem.at[k])
        for k, step in enumerate(steps)
    ]
    for load in loads:
        load.start()
    pl.semaphore_wait(barrier, len(partners))

    started = []

    def go(copy):
        copy.start()
        started.append(copy)
        return copy

    probe_pair = go(remote(probe.at[1 - c], plane_in, core_send.at[4], core_recv.at[4], pair))
    cores = [
        go(remote(grad.at[:, :, rows_of(step, 1 - c), :], core_in.at[k], core_send.at[k], core_recv.at[k], pair))
        for k, step in enumerate(steps)
    ]

    def merge(k):
        loads[k].wait()
        cores[k].wait_recv()
        own[k] = own[k] + core_in[k]

    merge(0)
    halves = [
        go(remote(own.at[0, 0], half_in.at[0], ring_send.at[0], ring_recv.at[0], at_z(1))),
        go(remote(own.at[0, 1], half_in.at[1], ring_send.at[1], ring_recv.at[1], at_z(-1))),
    ]
    probe_pair.wait_recv()
    plane_in[...] = plane_in[...] + probe[c]

    def piece_rows(device):
        return pl.ds(pl.multiple_of(device["tile"] * piece, piece), piece)

    gathers = [
        go(remote(plane_in.at[piece_rows(at_xy(j))], piece_in.at[j], probe_send.at[j], probe_recv.at[j], at_xy(j)))
        for j in shifts
    ]
    merge(1)
    up = go(remote(own.at[1, 1], direct_in.at[0], ring_send.at[2], ring_recv.at[2], at_z(1)))
    merge(2)
    down = go(remote(own.at[2, 0], direct_in.at[1], ring_send.at[3], ring_recv.at[3], at_z(-1)))
    halves[0].wait_recv()
    own[1, 0] = own[1, 0] + half_in[0]
    up_sum = go(remote(own.at[1, 0], direct_in.at[2], ring_send.at[4], ring_recv.at[4], at_z(1)))
    halves[1].wait_recv()
    own[2, 1] = own[2, 1] + half_in[1]
    down_sum = go(remote(own.at[2, 1], direct_in.at[3], ring_send.at[5], ring_recv.at[5], at_z(-1)))

    total = plane_in[piece_rows({"tile": tile}), :]
    for copy, j in zip(gathers, shifts):
        copy.wait_recv()
        total = total + piece_in[j]
    piece_z[0] = total
    across = [go(remote(piece_z.at[0], piece_z.at[k], z_send.at[k], z_recv.at[k], at_z(k))) for k in (1, 2, 3)]
    merge(3)
    for copy in across:
        copy.wait_recv()
    mine = piece_rows({"tile": tile})
    probe_out[c, mine, :] = (piece_z[0] + piece_z[1]) + (piece_z[2] + piece_z[3])
    spreads = [
        go(remote(probe_out.at[c, mine], probe_out.at[c, mine], all_send.at[j], all_recv.at[j], at_xy(j)))
        for j in shifts
    ]
    for copy in spreads:
        copy.wait_recv()
    last = go(remote(probe_out.at[c], probe_out.at[c], pair_send, pair_recv, pair))
    up.wait_recv()
    down.wait_recv()
    up_sum.wait_recv()
    down_sum.wait_recv()
    own[3, 0] = own[3, 0] + (direct_in[2] + direct_in[1])
    own[3, 1] = own[3, 1] + (direct_in[0] + direct_in[3])
    lines = out.shape[3]
    for plane in range(4):
        for k in range(4):
            out[0, plane // 2, plane % 2, :, k * HALF : (k + 1) * HALF] = own[
                3, plane // 2, plane % 2, pl.ds(k, lines, stride=4), :
            ]
    last.wait_recv()
    for copy in started:
        copy.wait_send()


def reduce_all(sizes, grad, probe):
    zs, xs, ys = sizes
    tiles = xs * ys
    slices, comps, side, width = grad.shape
    height = side // (zs * CORES)
    piece = SIDE // tiles
    dma = pltpu.SemaphoreType.DMA
    return pl.pallas_call(
        functools.partial(reduce_kernel, zs, xs, ys),
        out_shape=(
            jax.ShapeDtypeStruct((1, slices, comps, height // 4, 4 * width), F32),
            jax.ShapeDtypeStruct(probe.shape, F32),
        ),
        in_specs=[pl.BlockSpec(memory_space=pl.ANY), pl.BlockSpec(memory_space=pltpu.VMEM)],
        out_specs=(pl.BlockSpec(memory_space=pltpu.VMEM),) * 2,
        scratch_shapes=[
            pltpu.VMEM((4, slices, comps, height, width), F32),
            pltpu.VMEM((4, slices, comps, height, width), F32),
            pltpu.VMEM((2, comps, height, width), F32),
            pltpu.VMEM((4, comps, height, width), F32),
            pltpu.VMEM((SIDE, SIDE), F32),
            pltpu.VMEM((tiles, piece, SIDE), F32),
            pltpu.VMEM((4, piece, SIDE), F32),
            dma((4,)), dma((5,)), dma((5,)), dma((6,)), dma((6,)), dma((tiles,)), dma((tiles,)),
            dma((4,)), dma((4,)), dma((tiles,)), dma((tiles,)), dma, dma,
        ],
        compiler_params=pltpu.CompilerParams(
            collective_id=1, has_side_effects=True, vmem_limit_bytes=32 << 20
        ),
    )(grad, probe)


def per_device(object_tiles, probe_wave, patterns, tile_of, offsets, owner_map):
    tile_count = lax.axis_size("tile")
    high, low, shuffle = (jnp.asarray(table) for table in tables())
    zs, xs = lax.axis_size("scan") // CORES, math.isqrt(tile_count)
    ys = tile_count // xs
    held, arrived, back, far, info = exchange(
        xs, ys, tile_of, offsets, owner_map, patterns, object_tiles, probe_wave, high, low
    )
    tile_grad, probe_part = backward(info, held, probe_wave, high, low, shuffle, back, far, arrived)
    tile_grad = tile_grad.reshape((2, 2) + tile_grad.shape[1:])
    object_part, probe_total = reduce_all((zs, xs, ys), tile_grad, probe_part)
    count = tile_count * lax.axis_size("scan") * patterns.shape[0]
    return object_part, probe_total / jnp.sqrt(jnp.ones((), F32) * count)


def solution(mesh):
    return jax.shard_map(
        per_device,
        mesh=mesh,
        in_specs=(
            P("tile", None, None, None, None),
            P(),
            P(("scan", "tile"), None, None),
            P(("scan", "tile")),
            P(("scan", "tile"), None),
            P(),
        ),
        out_specs=(P("tile", None, None, "scan", None), P()),
        check_vma=False,
    )
```

```python
import functools
import math

import jax
import jax.numpy as jnp
import ml_dtypes
import numpy as np
from jax import lax
from jax.experimental import pallas as pl
from jax.experimental.pallas import tpu as pltpu
from jax.sharding import PartitionSpec as P

PROP_PHASE = 0.75
SIDE = 256
HALF = 128
MAX_READS = 8
F32 = jnp.float32
BF16 = jnp.bfloat16


def embed(block):
    return np.block([[block.real, block.imag], [-block.imag, block.real]])


@functools.cache
def tables():
    index = np.arange(SIDE)
    freq = np.where(index < HALF, index, index - SIDE).astype(np.float64)
    wave = np.exp(-2j * math.pi * (index[:, None] * index[None, :] % SIDE) / SIDE) / math.sqrt(SIDE)
    step = np.exp(-1j * PROP_PHASE * freq**2 / SIDE)
    travel = wave.conj() @ (step[:, None] * wave)
    plus = (travel[:HALF, :HALF] + travel[:HALF, HALF:]) / 2
    minus = (travel[:HALF, :HALF] - travel[:HALF, HALF:]) / 2
    forms = []
    for block in (plus, minus, wave[:HALF, 0::2], wave[:HALF, 1::2]):
        form = embed(block)
        forms += [form, form.T]
    forms = np.stack(forms)
    high = forms.astype(ml_dtypes.bfloat16)
    low = (forms - high.astype(np.float64)).astype(ml_dtypes.bfloat16)
    shuffle = np.zeros((SIDE, SIDE), ml_dtypes.bfloat16)
    shuffle[2 * np.arange(HALF), np.arange(HALF)] = 1
    shuffle[2 * np.arange(HALF) + 1, HALF + np.arange(HALF)] = 1
    return high, low, shuffle


A_PLUS, A_MINUS, F_EVEN, F_ODD = 0, 2, 4, 6


def parts(x):
    high = x.astype(BF16)
    return high, (x - high.astype(F32)).astype(BF16)


def mm(x, y):
    return jnp.dot(x, y, preferred_element_type=F32)


def right(x, high_ref, low_ref, which):
    xh, xl = parts(x)
    wh, wl = high_ref[which], low_ref[which]
    total = mm(xh, wh)
    total = total + mm(xl, wh)
    return total + mm(xh, wl)


def left(x, high_ref, low_ref, which):
    xh, xl = parts(x)
    wh, wl = high_ref[which], low_ref[which]
    total = mm(wh, xh)
    total = total + mm(wl, xh)
    return total + mm(wh, xl)


def cols(re, im):
    return (
        jnp.concatenate([re[:, :HALF] + re[:, HALF:], im[:, :HALF] + im[:, HALF:]], axis=1),
        jnp.concatenate([re[:, :HALF] - re[:, HALF:], im[:, :HALF] - im[:, HALF:]], axis=1),
    )


def rows(re, im):
    return (
        jnp.concatenate([re[:HALF] + re[HALF:], im[:HALF] + im[HALF:]], axis=0),
        jnp.concatenate([re[:HALF] - re[HALF:], im[:HALF] - im[HALF:]], axis=0),
    )


def split_cols(p, q):
    return (
        jnp.concatenate([p[:, :HALF], q[:, :HALF]], axis=1),
        jnp.concatenate([p[:, HALF:], q[:, HALF:]], axis=1),
    )


def split_rows(p, q):
    return (
        jnp.concatenate([p[:HALF], q[:HALF]], axis=0),
        jnp.concatenate([p[HALF:], q[HALF:]], axis=0),
    )


def travel(re, im, hi, lo, conj):
    flip = 1 if conj else 0
    s, d = cols(re, im)
    p, q = right(s, hi, lo, A_PLUS + flip), right(d, hi, lo, A_MINUS + flip)
    re, im = split_cols(p + q, p - q)
    s, d = rows(re, im)
    p, q = left(s, hi, lo, A_PLUS + 1 - flip), left(d, hi, lo, A_MINUS + 1 - flip)
    return split_rows(p + q, p - q)


def to_far(re, im, hi, lo):
    s, d = cols(re, im)
    re, im = split_cols(right(s, hi, lo, F_EVEN), right(d, hi, lo, F_ODD))
    s, d = rows(re, im)
    return split_rows(left(s, hi, lo, F_EVEN + 1), left(d, hi, lo, F_ODD + 1))


def from_far(re, im, hi, lo):
    even, odd = (
        jnp.concatenate([re[:, :HALF], im[:, :HALF]], axis=1),
        jnp.concatenate([re[:, HALF:], im[:, HALF:]], axis=1),
    )
    p, q = right(even, hi, lo, F_EVEN + 1), right(odd, hi, lo, F_ODD + 1)
    re, im = split_cols(p + q, p - q)
    even, odd = (
        jnp.concatenate([re[:HALF], im[:HALF]], axis=0),
        jnp.concatenate([re[HALF:], im[HALF:]], axis=0),
    )
    p, q = left(even, hi, lo, F_EVEN), left(odd, hi, lo, F_ODD)
    return split_rows(p + q, p - q)


def lane_mask(shift):
    return lax.broadcasted_iota(jnp.int32, (SIDE, HALF), 1) < shift


def spots(a, b):
    base = b // HALF
    return [pl.ds(4 * a + jnp.minimum(base + k, 3), SIDE, stride=4) for k in range(3)]


def patch(plane, a, b):
    shift = b % HALF
    back = lax.rem(HALF - shift, HALF)
    tiles = [pltpu.roll(plane[spot, :], back, 1) for spot in spots(a, b)]
    mask = lane_mask(HALF - shift)
    return jnp.concatenate(
        [jnp.where(mask, tiles[0], tiles[1]), jnp.where(mask, tiles[1], tiles[2])], axis=1
    )


def add_patch(plane, a, b, value):
    shift = b % HALF
    first, second = pltpu.roll(value[:, :HALF], shift, 1), pltpu.roll(value[:, HALF:], shift, 1)
    mask = lane_mask(shift)
    zero = jnp.zeros_like(first)
    terms = [jnp.where(mask, zero, first), jnp.where(mask, first, second), jnp.where(mask, second, zero)]
    for spot, term in zip(spots(a, b), terms):
        plane[spot, :] = plane[spot, :] + term


def open_tile(tile, held):
    for plane in range(4):
        for k in range(4):
            held[plane, pl.ds(k, 2 * SIDE, stride=4), :] = tile[
                plane // 2, plane % 2, :, k * HALF : (k + 1) * HALF
            ]


def forward_one(a, b, held, probe, hi, lo):
    ore, oim = patch(held.at[0], a, b), patch(held.at[1], a, b)
    pre, pim = probe[0], probe[1]
    back = travel(pre * ore - pim * oim, pre * oim + pim * ore, hi, lo, False)
    ore, oim = patch(held.at[2], a, b), patch(held.at[3], a, b)
    re, im = back
    return back, to_far(re * ore - im * oim, re * oim + im * ore, hi, lo)


MESH = pl.DeviceIdType.MESH
CORES = 2


def remote(src, dst, send, recv, device):
    return pltpu.make_async_remote_copy(
        src_ref=src, dst_ref=dst, send_sem=send, recv_sem=recv, device_id=device, device_id_type=MESH
    )


def plane_steps(xs, ys):
    tile = lax.axis_index("tile")
    x, y = tile // ys, tile % ys

    def at_xy(j):
        return {"tile": lax.rem(x + j // ys, xs) * ys + lax.rem(y + j % ys, ys)}

    return tile, at_xy, range(1, xs * ys)


def read_lists(notes, tables_ref):
    count = notes.shape[0]
    note = notes[:, 0, :]
    owner = lax.broadcasted_iota(jnp.int32, note.shape, 1)
    source = lax.broadcasted_iota(jnp.int32, note.shape, 0)
    here = jnp.zeros(note.shape, jnp.int32)
    values = [jnp.zeros(note.shape, jnp.int32) for _ in range(3)]
    for i in range(4):
        hit = jnp.where(jnp.broadcast_to(note[:, i : i + 1], note.shape) == owner, 1, 0)
        here = here + hit
        fields = [4 * source + i] + [
            jnp.broadcast_to(note[:, 4 * f + i : 4 * f + i + 1], note.shape) for f in (1, 2)
        ]
        values = [v + hit * f for v, f in zip(values, fields)]
    lower = (
        lax.broadcasted_iota(jnp.int32, (count, count), 0) > lax.broadcasted_iota(jnp.int32, (count, count), 1)
    ).astype(F32)
    rank = mm(lower.astype(BF16), here.astype(F32).astype(BF16)).astype(jnp.int32)
    for k in range(MAX_READS):
        chosen = here * jnp.where(rank == k, 1, 0)
        for f in range(3):
            row = MAX_READS * f + k
            tables_ref[row : row + 1, :] = jnp.sum(chosen * values[f], axis=0, keepdims=True)
    tables_ref[24:25, :] = jnp.sum(here, axis=0, keepdims=True)


def exchange_kernel(
    xs, ys, tile_hbm, offset_hbm, owner_hbm, patterns, tile, probe_hbm, hi_hbm, lo_hbm,
    held, arrived, back, far, info,
    tile_of, offsets, owner_map, opened, probe, hi, lo, notes, lists, lists_smem, mid, stage,
    small_sem, load_sem, own_sem, list_sem, note_send, note_recv, first_send, first_recv, second_send, second_recv,
):
    me, at_xy, shifts = plane_steps(xs, ys)
    piece = mid.shape[1]
    reads = patterns.shape[0]

    def piece_rows(index):
        return pl.ds(pl.multiple_of(index * piece, piece), piece)

    barrier = pltpu.get_barrier_semaphore()
    for j in shifts:
        pl.semaphore_signal(barrier, inc=1, device_id=at_xy(j), device_id_type=MESH)
    smalls = [
        pltpu.make_async_copy(src, dst, small_sem.at[k])
        for k, (src, dst) in enumerate([(tile_hbm, tile_of), (offset_hbm, offsets), (owner_hbm, owner_map)])
    ]
    for load in smalls:
        load.start()
    loads = [
        pltpu.make_async_copy(src, dst, load_sem.at[k])
        for k, (src, dst) in enumerate(
            [(tile, opened), (probe_hbm, probe), (hi_hbm, hi), (lo_hbm, lo)]
        )
    ]
    for load in loads:
        load.start()
    own = pltpu.make_async_copy(
        patterns.at[:, piece_rows(me), :], mid.at[pl.ds(reads * me, reads)], own_sem
    )
    own.start()
    for load in smalls:
        load.wait()
    lane = lax.broadcasted_iota(jnp.int32, (1, HALF), 1)
    note = jnp.zeros((1, HALF), jnp.int32)
    for i in range(reads):
        for f, value in enumerate((owner_map[tile_of[i]], offsets[0, i], offsets[1, i])):
            note = jnp.where(lane == 4 * f + i, value, note)
    notes[me] = note
    pl.semaphore_wait(barrier, len(shifts))

    tells = [
        remote(notes.at[me], notes.at[me], note_send.at[j], note_recv.at[j], at_xy(j)) for j in shifts
    ]
    firsts = [
        remote(
            patterns.at[:, piece_rows(at_xy(j)["tile"]), :], mid.at[pl.ds(reads * me, reads)],
            first_send.at[j], first_recv.at[j], at_xy(j),
        )
        for j in shifts
    ]
    for copy in tells + firsts:
        copy.start()
    loads[0].wait()
    open_tile(opened.at[0], held)
    for copy in tells:
        copy.wait_recv()
    lists[...] = jnp.zeros_like(lists)
    read_lists(notes, lists)
    listed = pltpu.make_async_copy(lists, lists_smem, list_sem)
    listed.start()
    listed.wait()
    for row in range(3):
        for k in range(MAX_READS):
            info[row, k] = lists_smem[MAX_READS * row + k, me]
    for k in range(MAX_READS):
        info[3, k] = lists_smem[24, me]
    own.wait()
    for copy in firsts:
        copy.wait_recv()
    seconds = []
    for j in shifts:
        to = at_xy(j)["tile"]
        for k in range(MAX_READS):
            stage[j, k] = mid[lists_smem[k, to]]
        copy = remote(
            stage.at[j], arrived.at[:, piece_rows(me), :], second_send.at[j], second_recv.at[j], at_xy(j)
        )
        copy.start()
        seconds.append(copy)
    for k in range(MAX_READS):
        arrived[k, piece_rows(me), :] = mid[lists_smem[k, me]]
    for load in loads[1:]:
        load.wait()

    def one(k, carry):
        a, b = lists_smem[MAX_READS + k, me], lists_smem[2 * MAX_READS + k, me]
        (bre, bim), (fre, fim) = forward_one(a, b, held, probe, hi, lo)
        back[k, 0], back[k, 1], far[k, 0], far[k, 1] = bre, bim, fre, fim
        return carry

    lax.fori_loop(0, MAX_READS, one, 0)
    for copy in seconds:
        copy.wait_recv()
    for copy in tells + firsts + seconds:
        copy.wait_send()


def exchange(xs, ys, tile_of, offsets, owner_map, patterns, tile, probe, hi, lo):
    tiles = xs * ys
    piece = SIDE // tiles
    reads = patterns.shape[0]
    dma = pltpu.SemaphoreType.DMA
    vmem, smem, hbm = (
        pl.BlockSpec(memory_space=space) for space in (pltpu.VMEM, pltpu.SMEM, pltpu.HBM)
    )
    field = jax.ShapeDtypeStruct((MAX_READS, 2, SIDE, SIDE), F32)
    return pl.pallas_call(
        functools.partial(exchange_kernel, xs, ys),
        out_shape=(
            jax.ShapeDtypeStruct((4, 2 * SIDE * 4, HALF), F32),
            jax.ShapeDtypeStruct((MAX_READS, SIDE, SIDE), F32),
            field,
            field,
            jax.ShapeDtypeStruct((4, MAX_READS), jnp.int32),
        ),
        in_specs=[hbm] * 8,
        out_specs=(vmem, vmem, vmem, vmem, smem),
        scratch_shapes=[
            pltpu.SMEM(tile_of.shape, jnp.int32),
            pltpu.SMEM(offsets.shape, jnp.int32),
            pltpu.SMEM(owner_map.shape, jnp.int32),
            pltpu.VMEM(tile.shape, F32),
            pltpu.VMEM(probe.shape, F32),
            pltpu.VMEM(hi.shape, BF16),
            pltpu.VMEM(lo.shape, BF16),
            pltpu.VMEM((tiles, 1, HALF), jnp.int32),
            pltpu.VMEM((32, HALF), jnp.int32),
            pltpu.SMEM((32, HALF), jnp.int32),
            pltpu.VMEM((tiles * reads, piece, SIDE), F32),
            pltpu.VMEM((tiles, MAX_READS, piece, SIDE), F32),
            dma((3,)), dma((4,)), dma, dma, dma((tiles,)), dma((tiles,)), dma((tiles,)), dma((tiles,)),
            dma((tiles,)), dma((tiles,)),
        ],
        cost_estimate=pl.CostEstimate(flops=MAX_READS * 24 * 2 * SIDE**3, bytes_accessed=14 << 20, transcendentals=0),
        compiler_params=pltpu.CompilerParams(
            collective_id=0, has_side_effects=True, vmem_limit_bytes=16 << 20
        ),
    )(*(pltpu.with_memory_space_constraint(x, pltpu.HBM) for x in (tile_of, offsets, owner_map, patterns, tile, probe, hi, lo)))


def backward_kernel(
    info, held, probe, hi, lo, shuffle, back, far, arrived, total, probe_grad, mixed
):
    total[...] = jnp.zeros_like(total)
    probe_grad[...] = jnp.zeros_like(probe_grad)

    def one(k, carry):
        a, b = info[1, k], info[2, k]
        for c in range(2):
            mixed[c] = arrived[k, :, c * HALF : (c + 1) * HALF]
        measured = jnp.concatenate(
            [
                jnp.concatenate([mixed[c, pl.ds(odd, HALF, stride=2), :] for c in range(2)], axis=1)
                for odd in range(2)
            ],
            axis=0,
        )
        mh, ml = parts(measured)
        measured = mm(mh, shuffle[...]) + mm(ml, shuffle[...])
        fre, fim = far[k, 0], far[k, 1]
        scale = 2.0 * (fre * fre + fim * fim - measured)
        gre, gim = from_far(scale * fre, scale * fim, hi, lo)
        bre, bim = back[k, 0], back[k, 1]
        add_patch(total.at[2], a, b, bre * gre + bim * gim)
        add_patch(total.at[3], a, b, bre * gim - bim * gre)
        ore, oim = patch(held.at[2], a, b), patch(held.at[3], a, b)
        gre, gim = travel(ore * gre + oim * gim, ore * gim - oim * gre, hi, lo, True)
        pre, pim = probe[0], probe[1]
        add_patch(total.at[0], a, b, pre * gre + pim * gim)
        add_patch(total.at[1], a, b, pre * gim - pim * gre)
        ore, oim = patch(held.at[0], a, b), patch(held.at[1], a, b)
        probe_grad[0] += ore * gre + oim * gim
        probe_grad[1] += ore * gim - oim * gre
        return carry

    lax.fori_loop(0, info[3, 0], one, 0)


def backward(info, held, probe, hi, lo, shuffle, back, far, arrived):
    vmem, smem = pl.BlockSpec(memory_space=pltpu.VMEM), pl.BlockSpec(memory_space=pltpu.SMEM)
    return pl.pallas_call(
        backward_kernel,
        out_shape=(jax.ShapeDtypeStruct(held.shape, F32), jax.ShapeDtypeStruct(probe.shape, F32)),
        in_specs=[smem] + [vmem] * 8,
        out_specs=(vmem, vmem),
        scratch_shapes=[pltpu.VMEM((2, SIDE, HALF), F32)],
        cost_estimate=pl.CostEstimate(flops=MAX_READS * 26 * 2 * SIDE**3, bytes_accessed=20 << 20, transcendentals=0),
        compiler_params=pltpu.CompilerParams(vmem_limit_bytes=8 << 20),
    )(info, held, probe, hi, lo, shuffle, back, far, arrived)


def reduce_kernel(
    zs, xs, ys, grad, probe, out, probe_out,
    own, core_in, half_in, direct_in, plane_in, piece_in, piece_z,
    load_sem, core_send, core_recv, ring_send, ring_recv, probe_send, probe_recv, z_send, z_recv,
    all_send, all_recv, pair_send, pair_recv,
):
    scan = lax.axis_index("scan")
    z, c = scan // CORES, scan % CORES
    tile, at_xy, shifts = plane_steps(xs, ys)
    height = own.shape[3]
    piece = piece_z.shape[1]

    def at_z(step):
        return {"scan": lax.rem(z + step + zs, zs) * CORES + c}

    pair = {"scan": z * CORES + 1 - c}
    steps = [2, 1, -1, 0]

    def rows_of(step, core):
        return pl.ds(pl.multiple_of((lax.rem(z + step + zs, zs) * CORES + core) * height, height), height)

    barrier = pltpu.get_barrier_semaphore()
    partners = [pair] + [at_z(step) for step in (1, 2, 3)] + [at_xy(j) for j in shifts]
    for partner in partners:
        pl.semaphore_signal(barrier, inc=1, device_id=partner, device_id_type=MESH)
    loads = [
        pltpu.make_async_copy(grad.at[:, :, rows_of(step, c), :], own.at[k], load_sem.at[k])
        for k, step in enumerate(steps)
    ]
    for load in loads:
        load.start()
    pl.semaphore_wait(barrier, len(partners))

    started = []

    def go(copy):
        copy.start()
        started.append(copy)
        return copy

    probe_pair = go(remote(probe.at[1 - c], plane_in, core_send.at[4], core_recv.at[4], pair))
    cores = [
        go(remote(grad.at[:, :, rows_of(step, 1 - c), :], core_in.at[k], core_send.at[k], core_recv.at[k], pair))
        for k, step in enumerate(steps)
    ]

    def merge(k):
        loads[k].wait()
        cores[k].wait_recv()
        own[k] = own[k] + core_in[k]

    merge(0)
    halves = [
        go(remote(own.at[0, 0], half_in.at[0], ring_send.at[0], ring_recv.at[0], at_z(1))),
        go(remote(own.at[0, 1], half_in.at[1], ring_send.at[1], ring_recv.at[1], at_z(-1))),
    ]
    probe_pair.wait_recv()
    plane_in[...] = plane_in[...] + probe[c]

    def piece_rows(device):
        return pl.ds(pl.multiple_of(device["tile"] * piece, piece), piece)

    gathers = [
        go(remote(plane_in.at[piece_rows(at_xy(j))], piece_in.at[j], probe_send.at[j], probe_recv.at[j], at_xy(j)))
        for j in shifts
    ]
    merge(1)
    up = go(remote(own.at[1, 1], direct_in.at[0], ring_send.at[2], ring_recv.at[2], at_z(1)))
    merge(2)
    down = go(remote(own.at[2, 0], direct_in.at[1], ring_send.at[3], ring_recv.at[3], at_z(-1)))
    halves[0].wait_recv()
    own[1, 0] = own[1, 0] + half_in[0]
    up_sum = go(remote(own.at[1, 0], direct_in.at[2], ring_send.at[4], ring_recv.at[4], at_z(1)))
    halves[1].wait_recv()
    own[2, 1] = own[2, 1] + half_in[1]
    down_sum = go(remote(own.at[2, 1], direct_in.at[3], ring_send.at[5], ring_recv.at[5], at_z(-1)))

    total = plane_in[piece_rows({"tile": tile}), :]
    for copy, j in zip(gathers, shifts):
        copy.wait_recv()
        total = total + piece_in[j]
    piece_z[0] = total
    across = [go(remote(piece_z.at[0], piece_z.at[k], z_send.at[k], z_recv.at[k], at_z(k))) for k in (1, 2, 3)]
    merge(3)
    for copy in across:
        copy.wait_recv()
    mine = piece_rows({"tile": tile})
    probe_out[c, mine, :] = (piece_z[0] + piece_z[1]) + (piece_z[2] + piece_z[3])
    spreads = [
        go(remote(probe_out.at[c, mine], probe_out.at[c, mine], all_send.at[j], all_recv.at[j], at_xy(j)))
        for j in shifts
    ]
    for copy in spreads:
        copy.wait_recv()
    last = go(remote(probe_out.at[c], probe_out.at[c], pair_send, pair_recv, pair))
    up.wait_recv()
    down.wait_recv()
    up_sum.wait_recv()
    down_sum.wait_recv()
    own[3, 0] = own[3, 0] + (direct_in[2] + direct_in[1])
    own[3, 1] = own[3, 1] + (direct_in[0] + direct_in[3])
    lines = out.shape[3]
    for plane in range(4):
        for k in range(4):
            out[0, plane // 2, plane % 2, :, k * HALF : (k + 1) * HALF] = own[
                3, plane // 2, plane % 2, pl.ds(k, lines, stride=4), :
            ]
    last.wait_recv()
    for copy in started:
        copy.wait_send()


def reduce_all(sizes, grad, probe):
    zs, xs, ys = sizes
    tiles = xs * ys
    slices, comps, side, width = grad.shape
    height = side // (zs * CORES)
    piece = SIDE // tiles
    dma = pltpu.SemaphoreType.DMA
    return pl.pallas_call(
        functools.partial(reduce_kernel, zs, xs, ys),
        out_shape=(
            jax.ShapeDtypeStruct((1, slices, comps, height // 4, 4 * width), F32),
            jax.ShapeDtypeStruct(probe.shape, F32),
        ),
        in_specs=[pl.BlockSpec(memory_space=pl.ANY), pl.BlockSpec(memory_space=pltpu.VMEM)],
        out_specs=(pl.BlockSpec(memory_space=pltpu.VMEM),) * 2,
        scratch_shapes=[
            pltpu.VMEM((4, slices, comps, height, width), F32),
            pltpu.VMEM((4, slices, comps, height, width), F32),
            pltpu.VMEM((2, comps, height, width), F32),
            pltpu.VMEM((4, comps, height, width), F32),
            pltpu.VMEM((SIDE, SIDE), F32),
            pltpu.VMEM((tiles, piece, SIDE), F32),
            pltpu.VMEM((4, piece, SIDE), F32),
            dma((4,)), dma((5,)), dma((5,)), dma((6,)), dma((6,)), dma((tiles,)), dma((tiles,)),
            dma((4,)), dma((4,)), dma((tiles,)), dma((tiles,)), dma, dma,
        ],
        compiler_params=pltpu.CompilerParams(
            collective_id=1, has_side_effects=True, vmem_limit_bytes=12 << 20
        ),
    )(grad, probe)


def per_device(object_tiles, probe_wave, patterns, tile_of, offsets, owner_map):
    tile_count = lax.axis_size("tile")
    high, low, shuffle = (jnp.asarray(table) for table in tables())
    zs, xs = lax.axis_size("scan") // CORES, math.isqrt(tile_count)
    ys = tile_count // xs
    held, arrived, back, far, info = exchange(
        xs, ys, tile_of, offsets.T, owner_map, patterns, object_tiles, probe_wave, high, low
    )
    tile_grad, probe_part = backward(info, held, probe_wave, high, low, shuffle, back, far, arrived)
    tile_grad = tile_grad.reshape((2, 2) + tile_grad.shape[1:])
    object_part, probe_total = reduce_all((zs, xs, ys), tile_grad, probe_part)
    count = tile_count * lax.axis_size("scan") * patterns.shape[0]
    return object_part, probe_total / jnp.sqrt(jnp.ones((), F32) * count)


def solution(mesh):
    return jax.shard_map(
        per_device,
        mesh=mesh,
        in_specs=(
            P("tile", None, None, None, None),
            P(),
            P(("scan", "tile"), None, None),
            P(("scan", "tile")),
            P(("scan", "tile"), None),
            P(),
        ),
        out_specs=(P("tile", None, None, "scan", None), P()),
        check_vma=False,
    )
```

```python
import functools
import math

import jax
import jax.numpy as jnp
import ml_dtypes
import numpy as np
from jax import lax
from jax.experimental import pallas as pl
from jax.experimental.pallas import tpu as pltpu
from jax.sharding import PartitionSpec as P

PROP_PHASE = 0.75
SIDE = 256
HALF = 128
MAX_READS = 8
F32 = jnp.float32
BF16 = jnp.bfloat16


def embed(block):
    return np.block([[block.real, block.imag], [-block.imag, block.real]])


@functools.cache
def tables():
    index = np.arange(SIDE)
    freq = np.where(index < HALF, index, index - SIDE).astype(np.float64)
    wave = np.exp(-2j * math.pi * (index[:, None] * index[None, :] % SIDE) / SIDE) / math.sqrt(SIDE)
    step = np.exp(-1j * PROP_PHASE * freq**2 / SIDE)
    travel = wave.conj() @ (step[:, None] * wave)
    plus = (travel[:HALF, :HALF] + travel[:HALF, HALF:]) / 2
    minus = (travel[:HALF, :HALF] - travel[:HALF, HALF:]) / 2
    forms = []
    for block in (plus, minus, wave[:HALF, 0::2], wave[:HALF, 1::2]):
        form = embed(block)
        forms += [form, form.T]
    forms = np.stack(forms)
    high = forms.astype(ml_dtypes.bfloat16)
    low = (forms - high.astype(np.float64)).astype(ml_dtypes.bfloat16)
    shuffle = np.zeros((SIDE, SIDE), ml_dtypes.bfloat16)
    shuffle[2 * np.arange(HALF), np.arange(HALF)] = 1
    shuffle[2 * np.arange(HALF) + 1, HALF + np.arange(HALF)] = 1
    return high, low, shuffle


A_PLUS, A_MINUS, F_EVEN, F_ODD = 0, 2, 4, 6


def parts(x):
    high = x.astype(BF16)
    return high, (x - high.astype(F32)).astype(BF16)


def mm(x, y):
    return jnp.dot(x, y, preferred_element_type=F32)


def right(x, high_ref, low_ref, which):
    xh, xl = parts(x)
    wh, wl = high_ref[which], low_ref[which]
    total = mm(xh, wh)
    total = total + mm(xl, wh)
    return total + mm(xh, wl)


def left(x, high_ref, low_ref, which):
    xh, xl = parts(x)
    wh, wl = high_ref[which], low_ref[which]
    total = mm(wh, xh)
    total = total + mm(wl, xh)
    return total + mm(wh, xl)


def cols(re, im):
    return (
        jnp.concatenate([re[:, :HALF] + re[:, HALF:], im[:, :HALF] + im[:, HALF:]], axis=1),
        jnp.concatenate([re[:, :HALF] - re[:, HALF:], im[:, :HALF] - im[:, HALF:]], axis=1),
    )


def rows(re, im):
    return (
        jnp.concatenate([re[:HALF] + re[HALF:], im[:HALF] + im[HALF:]], axis=0),
        jnp.concatenate([re[:HALF] - re[HALF:], im[:HALF] - im[HALF:]], axis=0),
    )


def split_cols(p, q):
    return (
        jnp.concatenate([p[:, :HALF], q[:, :HALF]], axis=1),
        jnp.concatenate([p[:, HALF:], q[:, HALF:]], axis=1),
    )


def split_rows(p, q):
    return (
        jnp.concatenate([p[:HALF], q[:HALF]], axis=0),
        jnp.concatenate([p[HALF:], q[HALF:]], axis=0),
    )


def travel(re, im, hi, lo, conj):
    flip = 1 if conj else 0
    s, d = cols(re, im)
    p, q = right(s, hi, lo, A_PLUS + flip), right(d, hi, lo, A_MINUS + flip)
    re, im = split_cols(p + q, p - q)
    s, d = rows(re, im)
    p, q = left(s, hi, lo, A_PLUS + 1 - flip), left(d, hi, lo, A_MINUS + 1 - flip)
    return split_rows(p + q, p - q)


def to_far(re, im, hi, lo):
    s, d = cols(re, im)
    re, im = split_cols(right(s, hi, lo, F_EVEN), right(d, hi, lo, F_ODD))
    s, d = rows(re, im)
    return split_rows(left(s, hi, lo, F_EVEN + 1), left(d, hi, lo, F_ODD + 1))


def from_far(re, im, hi, lo):
    even, odd = (
        jnp.concatenate([re[:, :HALF], im[:, :HALF]], axis=1),
        jnp.concatenate([re[:, HALF:], im[:, HALF:]], axis=1),
    )
    p, q = right(even, hi, lo, F_EVEN + 1), right(odd, hi, lo, F_ODD + 1)
    re, im = split_cols(p + q, p - q)
    even, odd = (
        jnp.concatenate([re[:HALF], im[:HALF]], axis=0),
        jnp.concatenate([re[HALF:], im[HALF:]], axis=0),
    )
    p, q = left(even, hi, lo, F_EVEN), left(odd, hi, lo, F_ODD)
    return split_rows(p + q, p - q)


def lane_mask(shift):
    return lax.broadcasted_iota(jnp.int32, (SIDE, HALF), 1) < shift


def spots(a, b):
    base = b // HALF
    return [pl.ds(4 * a + jnp.minimum(base + k, 3), SIDE, stride=4) for k in range(3)]


def patch(plane, a, b):
    shift = b % HALF
    back = lax.rem(HALF - shift, HALF)
    tiles = [pltpu.roll(plane[spot, :], back, 1) for spot in spots(a, b)]
    mask = lane_mask(HALF - shift)
    return jnp.concatenate(
        [jnp.where(mask, tiles[0], tiles[1]), jnp.where(mask, tiles[1], tiles[2])], axis=1
    )


def add_patch(plane, a, b, value):
    shift = b % HALF
    first, second = pltpu.roll(value[:, :HALF], shift, 1), pltpu.roll(value[:, HALF:], shift, 1)
    mask = lane_mask(shift)
    zero = jnp.zeros_like(first)
    terms = [jnp.where(mask, zero, first), jnp.where(mask, first, second), jnp.where(mask, second, zero)]
    for spot, term in zip(spots(a, b), terms):
        plane[spot, :] = plane[spot, :] + term


def open_tile(tile, held):
    for plane in range(4):
        for k in range(4):
            held[plane, pl.ds(k, 2 * SIDE, stride=4), :] = tile[
                plane // 2, plane % 2, :, k * HALF : (k + 1) * HALF
            ]


def forward_one(a, b, held, probe, hi, lo):
    ore, oim = patch(held.at[0], a, b), patch(held.at[1], a, b)
    pre, pim = probe[0], probe[1]
    back = travel(pre * ore - pim * oim, pre * oim + pim * ore, hi, lo, False)
    ore, oim = patch(held.at[2], a, b), patch(held.at[3], a, b)
    re, im = back
    return back, to_far(re * ore - im * oim, re * oim + im * ore, hi, lo)


MESH = pl.DeviceIdType.MESH
CORES = 2


def remote(src, dst, send, recv, device):
    return pltpu.make_async_remote_copy(
        src_ref=src, dst_ref=dst, send_sem=send, recv_sem=recv, device_id=device, device_id_type=MESH
    )


def plane_steps(xs, ys):
    tile = lax.axis_index("tile")
    x, y = tile // ys, tile % ys

    def at_xy(j):
        return {"tile": lax.rem(x + j // ys, xs) * ys + lax.rem(y + j % ys, ys)}

    return tile, at_xy, range(1, xs * ys)


def read_lists(notes, tables_ref):
    count = notes.shape[0]
    note = notes[:, 0, :]
    owner = lax.broadcasted_iota(jnp.int32, note.shape, 1)
    source = lax.broadcasted_iota(jnp.int32, note.shape, 0)
    here = jnp.zeros(note.shape, jnp.int32)
    values = [jnp.zeros(note.shape, jnp.int32) for _ in range(3)]
    for i in range(4):
        hit = jnp.where(jnp.broadcast_to(note[:, i : i + 1], note.shape) == owner, 1, 0)
        here = here + hit
        fields = [4 * source + i] + [
            jnp.broadcast_to(note[:, 4 * f + i : 4 * f + i + 1], note.shape) for f in (1, 2)
        ]
        values = [v + hit * f for v, f in zip(values, fields)]
    lower = (
        lax.broadcasted_iota(jnp.int32, (count, count), 0) > lax.broadcasted_iota(jnp.int32, (count, count), 1)
    ).astype(F32)
    rank = mm(lower.astype(BF16), here.astype(F32).astype(BF16)).astype(jnp.int32)
    for k in range(MAX_READS):
        chosen = here * jnp.where(rank == k, 1, 0)
        for f in range(3):
            row = MAX_READS * f + k
            tables_ref[row : row + 1, :] = jnp.sum(chosen * values[f], axis=0, keepdims=True)
    tables_ref[24:25, :] = jnp.sum(here, axis=0, keepdims=True)


def exchange_kernel(
    xs, ys, tile_hbm, offset_hbm, owner_hbm, patterns, tile, probe_hbm, hi_hbm, lo_hbm,
    held, arrived, back, far, info,
    tile_of, offsets, owner_map, opened, probe, hi, lo, notes, lists, lists_smem, mid, stage,
    small_sem, load_sem, own_sem, list_sem, note_send, note_recv, first_send, first_recv, second_send, second_recv,
):
    me, at_xy, shifts = plane_steps(xs, ys)
    piece = mid.shape[1]
    reads = patterns.shape[0]

    def piece_rows(index):
        return pl.ds(pl.multiple_of(index * piece, piece), piece)

    barrier = pltpu.get_barrier_semaphore()
    for j in shifts:
        pl.semaphore_signal(barrier, inc=1, device_id=at_xy(j), device_id_type=MESH)
    smalls = [
        pltpu.make_async_copy(src, dst, small_sem.at[k])
        for k, (src, dst) in enumerate([(tile_hbm, tile_of), (offset_hbm, offsets), (owner_hbm, owner_map)])
    ]
    for load in smalls:
        load.start()
    loads = [
        pltpu.make_async_copy(src, dst, load_sem.at[k])
        for k, (src, dst) in enumerate(
            [(tile, opened), (probe_hbm, probe), (hi_hbm, hi), (lo_hbm, lo)]
        )
    ]
    for load in loads:
        load.start()
    own = pltpu.make_async_copy(
        patterns.at[:, piece_rows(me), :], mid.at[pl.ds(reads * me, reads)], own_sem
    )
    own.start()
    for load in smalls:
        load.wait()
    lane = lax.broadcasted_iota(jnp.int32, (1, HALF), 1)
    note = jnp.zeros((1, HALF), jnp.int32)
    for i in range(reads):
        for f, value in enumerate((owner_map[tile_of[i]], offsets[0, i], offsets[1, i])):
            note = jnp.where(lane == 4 * f + i, value, note)
    notes[me] = note
    pl.semaphore_wait(barrier, len(shifts))

    tells = [
        remote(notes.at[me], notes.at[me], note_send.at[j], note_recv.at[j], at_xy(j)) for j in shifts
    ]
    firsts = [
        remote(
            patterns.at[:, piece_rows(at_xy(j)["tile"]), :], mid.at[pl.ds(reads * me, reads)],
            first_send.at[j], first_recv.at[j], at_xy(j),
        )
        for j in shifts
    ]
    for copy in tells + firsts:
        copy.start()
    loads[0].wait()
    open_tile(opened.at[0], held)
    for copy in tells:
        copy.wait_recv()
    lists[...] = jnp.zeros_like(lists)
    read_lists(notes, lists)
    listed = pltpu.make_async_copy(lists, lists_smem, list_sem)
    listed.start()
    listed.wait()
    for row in range(3):
        for k in range(MAX_READS):
            info[row, k] = lists_smem[MAX_READS * row + k, me]
    for k in range(MAX_READS):
        info[3, k] = lists_smem[24, me]
    own.wait()
    for copy in firsts:
        copy.wait_recv()
    seconds = []
    for j in shifts:
        to = at_xy(j)["tile"]
        for k in range(MAX_READS):
            stage[j, k] = mid[lists_smem[k, to]]
        copy = remote(
            stage.at[j], arrived.at[:, piece_rows(me), :], second_send.at[j], second_recv.at[j], at_xy(j)
        )
        copy.start()
        seconds.append(copy)
    for k in range(MAX_READS):
        arrived[k, piece_rows(me), :] = mid[lists_smem[k, me]]
    for load in loads[1:]:
        load.wait()

    def one(k, carry):
        a, b = lists_smem[MAX_READS + k, me], lists_smem[2 * MAX_READS + k, me]
        (bre, bim), (fre, fim) = forward_one(a, b, held, probe, hi, lo)
        back[k, 0], back[k, 1], far[k, 0], far[k, 1] = bre, bim, fre, fim
        return carry

    lax.fori_loop(0, MAX_READS, one, 0)
    for copy in seconds:
        copy.wait_recv()
    for copy in tells + firsts + seconds:
        copy.wait_send()


def exchange(xs, ys, tile_of, offsets, owner_map, patterns, tile, probe, hi, lo):
    tiles = xs * ys
    piece = SIDE // tiles
    reads = patterns.shape[0]
    dma = pltpu.SemaphoreType.DMA
    vmem, smem, hbm = (
        pl.BlockSpec(memory_space=space) for space in (pltpu.VMEM, pltpu.SMEM, pltpu.HBM)
    )
    field = jax.ShapeDtypeStruct((MAX_READS, 2, SIDE, SIDE), F32)
    return pl.pallas_call(
        functools.partial(exchange_kernel, xs, ys),
        out_shape=(
            jax.ShapeDtypeStruct((4, 2 * SIDE * 4, HALF), F32),
            jax.ShapeDtypeStruct((MAX_READS, SIDE, SIDE), F32),
            field,
            field,
            jax.ShapeDtypeStruct((4, MAX_READS), jnp.int32),
        ),
        in_specs=[hbm] * 8,
        out_specs=(vmem, vmem, vmem, vmem, smem),
        scratch_shapes=[
            pltpu.SMEM(tile_of.shape, jnp.int32),
            pltpu.SMEM(offsets.shape, jnp.int32),
            pltpu.SMEM(owner_map.shape, jnp.int32),
            pltpu.VMEM(tile.shape, F32),
            pltpu.VMEM(probe.shape, F32),
            pltpu.VMEM(hi.shape, BF16),
            pltpu.VMEM(lo.shape, BF16),
            pltpu.VMEM((tiles, 1, HALF), jnp.int32),
            pltpu.VMEM((32, HALF), jnp.int32),
            pltpu.SMEM((32, HALF), jnp.int32),
            pltpu.VMEM((tiles * reads, piece, SIDE), F32),
            pltpu.VMEM((tiles, MAX_READS, piece, SIDE), F32),
            dma((3,)), dma((4,)), dma, dma, dma((tiles,)), dma((tiles,)), dma((tiles,)), dma((tiles,)),
            dma((tiles,)), dma((tiles,)),
        ],
        cost_estimate=pl.CostEstimate(flops=MAX_READS * 24 * 2 * SIDE**3, bytes_accessed=14 << 20, transcendentals=0),
        compiler_params=pltpu.CompilerParams(
            collective_id=0, has_side_effects=True, vmem_limit_bytes=16 << 20
        ),
    )(*(pltpu.with_memory_space_constraint(x, pltpu.HBM) for x in (tile_of, offsets, owner_map, patterns, tile, probe, hi, lo)))


def backward_kernel(
    info, held, probe, hi, lo, shuffle, back, far, arrived, total, probe_grad, mixed
):
    total[...] = jnp.zeros_like(total)
    probe_grad[...] = jnp.zeros_like(probe_grad)

    def one(k, carry):
        a, b = info[1, k], info[2, k]
        for c in range(2):
            mixed[c] = arrived[k, :, c * HALF : (c + 1) * HALF]
        measured = jnp.concatenate(
            [
                jnp.concatenate([mixed[c, pl.ds(odd, HALF, stride=2), :] for c in range(2)], axis=1)
                for odd in range(2)
            ],
            axis=0,
        )
        mh, ml = parts(measured)
        measured = mm(mh, shuffle[...]) + mm(ml, shuffle[...])
        fre, fim = far[k, 0], far[k, 1]
        scale = 2.0 * (fre * fre + fim * fim - measured)
        gre, gim = from_far(scale * fre, scale * fim, hi, lo)
        bre, bim = back[k, 0], back[k, 1]
        add_patch(total.at[2], a, b, bre * gre + bim * gim)
        add_patch(total.at[3], a, b, bre * gim - bim * gre)
        ore, oim = patch(held.at[2], a, b), patch(held.at[3], a, b)
        gre, gim = travel(ore * gre + oim * gim, ore * gim - oim * gre, hi, lo, True)
        pre, pim = probe[0], probe[1]
        add_patch(total.at[0], a, b, pre * gre + pim * gim)
        add_patch(total.at[1], a, b, pre * gim - pim * gre)
        ore, oim = patch(held.at[0], a, b), patch(held.at[1], a, b)
        probe_grad[0] += ore * gre + oim * gim
        probe_grad[1] += ore * gim - oim * gre
        return carry

    lax.fori_loop(0, info[3, 0], one, 0)


def backward(info, held, probe, hi, lo, shuffle, back, far, arrived):
    vmem, smem = pl.BlockSpec(memory_space=pltpu.VMEM), pl.BlockSpec(memory_space=pltpu.SMEM)
    return pl.pallas_call(
        backward_kernel,
        out_shape=(jax.ShapeDtypeStruct(held.shape, F32), jax.ShapeDtypeStruct(probe.shape, F32)),
        in_specs=[smem] + [vmem] * 8,
        out_specs=(vmem, vmem),
        scratch_shapes=[pltpu.VMEM((2, SIDE, HALF), F32)],
        cost_estimate=pl.CostEstimate(flops=MAX_READS * 26 * 2 * SIDE**3, bytes_accessed=20 << 20, transcendentals=0),
        compiler_params=pltpu.CompilerParams(vmem_limit_bytes=8 << 20),
    )(info, held, probe, hi, lo, shuffle, back, far, arrived)


def reduce_kernel(
    zs, xs, ys, grad, probe, out, probe_out,
    own, core_in, half_in, direct_in, plane_in, piece_in, piece_z,
    load_sem, core_send, core_recv, ring_send, ring_recv, part_send, part_recv, probe_send, probe_recv, z_send, z_recv,
    all_send, all_recv, pair_send, pair_recv,
):
    scan = lax.axis_index("scan")
    z, c = scan // CORES, scan % CORES
    tile, at_xy, shifts = plane_steps(xs, ys)
    height = own.shape[3]
    piece = piece_z.shape[1]

    def at_z(step):
        return {"scan": lax.rem(z + step + zs, zs) * CORES + c}

    pair = {"scan": z * CORES + 1 - c}
    steps = [2, 1, -1, 0]

    def rows_of(step, core):
        return pl.ds(pl.multiple_of((lax.rem(z + step + zs, zs) * CORES + core) * height, height), height)

    barrier = pltpu.get_barrier_semaphore()
    partners = [pair] + [at_z(step) for step in (1, 2, 3)] + [at_xy(j) for j in shifts]
    for partner in partners:
        pl.semaphore_signal(barrier, inc=1, device_id=partner, device_id_type=MESH)
    loads = [
        pltpu.make_async_copy(grad.at[:, :, rows_of(step, c), :], own.at[k], load_sem.at[k])
        for k, step in enumerate(steps)
    ]
    for load in loads:
        load.start()
    pl.semaphore_wait(barrier, len(partners))

    started = []

    def go(copy):
        copy.start()
        started.append(copy)
        return copy

    def core_copy(k):
        rows = rows_of(steps[k], 1 - c)
        return go(remote(grad.at[:, :, rows, :], core_in.at[k], core_send.at[k], core_recv.at[k], pair))

    def piece_rows(device):
        return pl.ds(pl.multiple_of(device["tile"] * piece, piece), piece)

    cores = [core_copy(0)]
    probe_pair = go(remote(probe.at[1 - c], plane_in, core_send.at[4], core_recv.at[4], pair))
    cores += [core_copy(k) for k in (1, 2, 3)]

    def merge(k):
        loads[k].wait()
        cores[k].wait_recv()
        own[k] = own[k] + core_in[k]

    def direct(part):
        half = pl.ds(part * (height // 2), height // 2)
        return [
            go(remote(own.at[1, 1, :, half], direct_in.at[0, :, half], part_send.at[0, part], part_recv.at[0, part], at_z(1))),
            go(remote(own.at[2, 0, :, half], direct_in.at[1, :, half], part_send.at[1, part], part_recv.at[1, part], at_z(-1))),
        ]

    merge(0)
    halves = [
        go(remote(own.at[0, 0], half_in.at[0], ring_send.at[0], ring_recv.at[0], at_z(1))),
        go(remote(own.at[0, 1], half_in.at[1], ring_send.at[1], ring_recv.at[1], at_z(-1))),
    ]
    probe_pair.wait_recv()
    plane_in[...] = plane_in[...] + probe[c]
    gathers = [
        go(remote(plane_in.at[piece_rows(at_xy(j))], piece_in.at[j], probe_send.at[j], probe_recv.at[j], at_xy(j)))
        for j in shifts
    ]
    merge(1)
    merge(2)
    straight = direct(0)
    merge(3)
    total = plane_in[piece_rows({"tile": tile}), :]
    for copy, j in zip(gathers, shifts):
        copy.wait_recv()
        total = total + piece_in[j]
    piece_z[0] = total
    across = [go(remote(piece_z.at[0], piece_z.at[k], z_send.at[k], z_recv.at[k], at_z(k))) for k in (1, 2, 3)]
    straight += direct(1)
    halves[0].wait_recv()
    own[1, 0] = own[1, 0] + half_in[0]
    up_sum = go(remote(own.at[1, 0], direct_in.at[2], ring_send.at[4], ring_recv.at[4], at_z(1)))
    halves[1].wait_recv()
    own[2, 1] = own[2, 1] + half_in[1]
    down_sum = go(remote(own.at[2, 1], direct_in.at[3], ring_send.at[5], ring_recv.at[5], at_z(-1)))
    for copy in across:
        copy.wait_recv()
    mine = piece_rows({"tile": tile})
    probe_out[c, mine, :] = (piece_z[0] + piece_z[1]) + (piece_z[2] + piece_z[3])
    spreads = [
        go(remote(probe_out.at[c, mine], probe_out.at[c, mine], all_send.at[j], all_recv.at[j], at_xy(j)))
        for j in shifts
    ]
    for copy in spreads:
        copy.wait_recv()
    last = go(remote(probe_out.at[c], probe_out.at[c], pair_send, pair_recv, pair))
    for copy in straight:
        copy.wait_recv()
    up_sum.wait_recv()
    down_sum.wait_recv()
    own[3, 0] = own[3, 0] + (direct_in[2] + direct_in[1])
    own[3, 1] = own[3, 1] + (direct_in[0] + direct_in[3])
    lines = out.shape[3]
    for plane in range(4):
        for k in range(4):
            out[0, plane // 2, plane % 2, :, k * HALF : (k + 1) * HALF] = own[
                3, plane // 2, plane % 2, pl.ds(k, lines, stride=4), :
            ]
    last.wait_recv()
    for copy in started:
        copy.wait_send()


def reduce_all(sizes, grad, probe):
    zs, xs, ys = sizes
    tiles = xs * ys
    slices, comps, side, width = grad.shape
    height = side // (zs * CORES)
    piece = SIDE // tiles
    dma = pltpu.SemaphoreType.DMA
    return pl.pallas_call(
        functools.partial(reduce_kernel, zs, xs, ys),
        out_shape=(
            jax.ShapeDtypeStruct((1, slices, comps, height // 4, 4 * width), F32),
            jax.ShapeDtypeStruct(probe.shape, F32),
        ),
        in_specs=[pl.BlockSpec(memory_space=pl.ANY), pl.BlockSpec(memory_space=pltpu.VMEM)],
        out_specs=(pl.BlockSpec(memory_space=pltpu.VMEM),) * 2,
        scratch_shapes=[
            pltpu.VMEM((4, slices, comps, height, width), F32),
            pltpu.VMEM((4, slices, comps, height, width), F32),
            pltpu.VMEM((2, comps, height, width), F32),
            pltpu.VMEM((4, comps, height, width), F32),
            pltpu.VMEM((SIDE, SIDE), F32),
            pltpu.VMEM((tiles, piece, SIDE), F32),
            pltpu.VMEM((4, piece, SIDE), F32),
            dma((4,)), dma((5,)), dma((5,)), dma((6,)), dma((6,)), dma((2, 2)), dma((2, 2)), dma((tiles,)), dma((tiles,)),
            dma((4,)), dma((4,)), dma((tiles,)), dma((tiles,)), dma, dma,
        ],
        compiler_params=pltpu.CompilerParams(
            collective_id=1, has_side_effects=True, vmem_limit_bytes=12 << 20
        ),
    )(grad, probe)


def per_device(object_tiles, probe_wave, patterns, tile_of, offsets, owner_map):
    tile_count = lax.axis_size("tile")
    high, low, shuffle = (jnp.asarray(table) for table in tables())
    zs, xs = lax.axis_size("scan") // CORES, math.isqrt(tile_count)
    ys = tile_count // xs
    held, arrived, back, far, info = exchange(
        xs, ys, tile_of, offsets.T, owner_map, patterns, object_tiles, probe_wave, high, low
    )
    tile_grad, probe_part = backward(info, held, probe_wave, high, low, shuffle, back, far, arrived)
    tile_grad = tile_grad.reshape((2, 2) + tile_grad.shape[1:])
    object_part, probe_total = reduce_all((zs, xs, ys), tile_grad, probe_part)
    count = tile_count * lax.axis_size("scan") * patterns.shape[0]
    return object_part, probe_total / jnp.sqrt(jnp.ones((), F32) * count)


def solution(mesh):
    return jax.shard_map(
        per_device,
        mesh=mesh,
        in_specs=(
            P("tile", None, None, None, None),
            P(),
            P(("scan", "tile"), None, None),
            P(("scan", "tile")),
            P(("scan", "tile"), None),
            P(),
        ),
        out_specs=(P("tile", None, None, "scan", None), P()),
        check_vma=False,
    )
```

```python
import functools
import math

import jax
import jax.numpy as jnp
import ml_dtypes
import numpy as np
from jax import lax
from jax.experimental import pallas as pl
from jax.experimental.pallas import tpu as pltpu
from jax.sharding import PartitionSpec as P

PROP_PHASE = 0.75
SIDE = 256
HALF = 128
MAX_READS = 8
F32 = jnp.float32
BF16 = jnp.bfloat16


def embed(block):
    return np.block([[block.real, block.imag], [-block.imag, block.real]])


@functools.cache
def tables():
    index = np.arange(SIDE)
    freq = np.where(index < HALF, index, index - SIDE).astype(np.float64)
    wave = np.exp(-2j * math.pi * (index[:, None] * index[None, :] % SIDE) / SIDE) / math.sqrt(SIDE)
    step = np.exp(-1j * PROP_PHASE * freq**2 / SIDE)
    travel = wave.conj() @ (step[:, None] * wave)
    plus = (travel[:HALF, :HALF] + travel[:HALF, HALF:]) / 2
    minus = (travel[:HALF, :HALF] - travel[:HALF, HALF:]) / 2
    forms = []
    for block in (plus, minus, wave[:HALF, 0::2], wave[:HALF, 1::2]):
        form = embed(block)
        forms += [form, form.T]
    forms = np.stack(forms)
    high = forms.astype(ml_dtypes.bfloat16)
    low = (forms - high.astype(np.float64)).astype(ml_dtypes.bfloat16)
    shuffle = np.zeros((SIDE, SIDE), ml_dtypes.bfloat16)
    shuffle[2 * np.arange(HALF), np.arange(HALF)] = 1
    shuffle[2 * np.arange(HALF) + 1, HALF + np.arange(HALF)] = 1
    return high, low, shuffle


A_PLUS, A_MINUS, F_EVEN, F_ODD = 0, 2, 4, 6


def parts(x):
    high = x.astype(BF16)
    return high, (x - high.astype(F32)).astype(BF16)


def mm(x, y):
    return jnp.dot(x, y, preferred_element_type=F32)


def right(x, high_ref, low_ref, which):
    xh, xl = parts(x)
    wh, wl = high_ref[which], low_ref[which]
    total = mm(xh, wh)
    total = total + mm(xl, wh)
    return total + mm(xh, wl)


def left(x, high_ref, low_ref, which):
    xh, xl = parts(x)
    wh, wl = high_ref[which], low_ref[which]
    total = mm(wh, xh)
    total = total + mm(wl, xh)
    return total + mm(wh, xl)


def cols(re, im):
    return (
        jnp.concatenate([re[:, :HALF] + re[:, HALF:], im[:, :HALF] + im[:, HALF:]], axis=1),
        jnp.concatenate([re[:, :HALF] - re[:, HALF:], im[:, :HALF] - im[:, HALF:]], axis=1),
    )


def rows(re, im):
    return (
        jnp.concatenate([re[:HALF] + re[HALF:], im[:HALF] + im[HALF:]], axis=0),
        jnp.concatenate([re[:HALF] - re[HALF:], im[:HALF] - im[HALF:]], axis=0),
    )


def split_cols(p, q):
    return (
        jnp.concatenate([p[:, :HALF], q[:, :HALF]], axis=1),
        jnp.concatenate([p[:, HALF:], q[:, HALF:]], axis=1),
    )


def split_rows(p, q):
    return (
        jnp.concatenate([p[:HALF], q[:HALF]], axis=0),
        jnp.concatenate([p[HALF:], q[HALF:]], axis=0),
    )


def travel(re, im, hi, lo, conj):
    flip = 1 if conj else 0
    s, d = cols(re, im)
    p, q = right(s, hi, lo, A_PLUS + flip), right(d, hi, lo, A_MINUS + flip)
    re, im = split_cols(p + q, p - q)
    s, d = rows(re, im)
    p, q = left(s, hi, lo, A_PLUS + 1 - flip), left(d, hi, lo, A_MINUS + 1 - flip)
    return split_rows(p + q, p - q)


def to_far(re, im, hi, lo):
    s, d = cols(re, im)
    re, im = split_cols(right(s, hi, lo, F_EVEN), right(d, hi, lo, F_ODD))
    s, d = rows(re, im)
    return split_rows(left(s, hi, lo, F_EVEN + 1), left(d, hi, lo, F_ODD + 1))


def from_far(re, im, hi, lo):
    even, odd = (
        jnp.concatenate([re[:, :HALF], im[:, :HALF]], axis=1),
        jnp.concatenate([re[:, HALF:], im[:, HALF:]], axis=1),
    )
    p, q = right(even, hi, lo, F_EVEN + 1), right(odd, hi, lo, F_ODD + 1)
    re, im = split_cols(p + q, p - q)
    even, odd = (
        jnp.concatenate([re[:HALF], im[:HALF]], axis=0),
        jnp.concatenate([re[HALF:], im[HALF:]], axis=0),
    )
    p, q = left(even, hi, lo, F_EVEN), left(odd, hi, lo, F_ODD)
    return split_rows(p + q, p - q)


def lane_mask(shift):
    return lax.broadcasted_iota(jnp.int32, (SIDE, HALF), 1) < shift


def spots(a, b):
    base = b // HALF
    return [pl.ds(4 * a + jnp.minimum(base + k, 3), SIDE, stride=4) for k in range(3)]


def patch(plane, a, b):
    shift = b % HALF
    back = lax.rem(HALF - shift, HALF)
    tiles = [pltpu.roll(plane[spot, :], back, 1) for spot in spots(a, b)]
    mask = lane_mask(HALF - shift)
    return jnp.concatenate(
        [jnp.where(mask, tiles[0], tiles[1]), jnp.where(mask, tiles[1], tiles[2])], axis=1
    )


def add_patch(plane, a, b, value):
    shift = b % HALF
    first, second = pltpu.roll(value[:, :HALF], shift, 1), pltpu.roll(value[:, HALF:], shift, 1)
    mask = lane_mask(shift)
    zero = jnp.zeros_like(first)
    terms = [jnp.where(mask, zero, first), jnp.where(mask, first, second), jnp.where(mask, second, zero)]
    for spot, term in zip(spots(a, b), terms):
        plane[spot, :] = plane[spot, :] + term


def open_tile(tile, held):
    for plane in range(4):
        for k in range(4):
            held[plane, pl.ds(k, 2 * SIDE, stride=4), :] = tile[
                plane // 2, plane % 2, :, k * HALF : (k + 1) * HALF
            ]


def forward_one(a, b, held, probe, hi, lo):
    ore, oim = patch(held.at[0], a, b), patch(held.at[1], a, b)
    pre, pim = probe[0], probe[1]
    back = travel(pre * ore - pim * oim, pre * oim + pim * ore, hi, lo, False)
    ore, oim = patch(held.at[2], a, b), patch(held.at[3], a, b)
    re, im = back
    return back, to_far(re * ore - im * oim, re * oim + im * ore, hi, lo)


def backward_one(k, a, b, valid, held, probe, hi, lo, shuffle, back, far, arrived, mixed):
    for c in range(2):
        mixed[c] = arrived[k, :, c * HALF : (c + 1) * HALF]
    measured = jnp.concatenate(
        [
            jnp.concatenate([mixed[c, pl.ds(odd, HALF, stride=2), :] for c in range(2)], axis=1)
            for odd in range(2)
        ],
        axis=0,
    )
    mh, ml = parts(measured)
    measured = mm(mh, shuffle[...]) + mm(ml, shuffle[...])
    fre, fim = far[k, 0], far[k, 1]
    scale = valid * (fre * fre + fim * fim - measured)
    gre, gim = from_far(scale * fre, scale * fim, hi, lo)
    bre, bim = back[k, 0], back[k, 1]
    second = (bre * gre + bim * gim, bre * gim - bim * gre)
    ore, oim = patch(held.at[2], a, b), patch(held.at[3], a, b)
    gre, gim = travel(ore * gre + oim * gim, ore * gim - oim * gre, hi, lo, True)
    pre, pim = probe[0], probe[1]
    first = (pre * gre + pim * gim, pre * gim - pim * gre)
    ore, oim = patch(held.at[0], a, b), patch(held.at[1], a, b)
    return second, first, (ore * gre + oim * gim, ore * gim - oim * gre)


MESH = pl.DeviceIdType.MESH
CORES = 2
EARLY = 6
PAIR = 2


def remote(src, dst, send, recv, device):
    return pltpu.make_async_remote_copy(
        src_ref=src, dst_ref=dst, send_sem=send, recv_sem=recv, device_id=device, device_id_type=MESH
    )


def plane_steps(xs, ys):
    tile = lax.axis_index("tile")
    x, y = tile // ys, tile % ys

    def at_xy(j):
        return {"tile": lax.rem(x + j // ys, xs) * ys + lax.rem(y + j % ys, ys)}

    return tile, at_xy, range(1, xs * ys)


def read_lists(notes, tables_ref):
    count = notes.shape[0]
    note = notes[:, 0, :]
    owner = lax.broadcasted_iota(jnp.int32, note.shape, 1)
    source = lax.broadcasted_iota(jnp.int32, note.shape, 0)
    here = jnp.zeros(note.shape, jnp.int32)
    values = [jnp.zeros(note.shape, jnp.int32) for _ in range(3)]
    for i in range(4):
        hit = jnp.where(jnp.broadcast_to(note[:, i : i + 1], note.shape) == owner, 1, 0)
        here = here + hit
        fields = [4 * source + i] + [
            jnp.broadcast_to(note[:, 4 * f + i : 4 * f + i + 1], note.shape) for f in (1, 2)
        ]
        values = [v + hit * f for v, f in zip(values, fields)]
    lower = (
        lax.broadcasted_iota(jnp.int32, (count, count), 0) > lax.broadcasted_iota(jnp.int32, (count, count), 1)
    ).astype(F32)
    rank = mm(lower.astype(BF16), here.astype(F32).astype(BF16)).astype(jnp.int32)
    for k in range(MAX_READS):
        chosen = here * jnp.where(rank == k, 1, 0)
        for f in range(3):
            row = MAX_READS * f + k
            tables_ref[row : row + 1, :] = jnp.sum(chosen * values[f], axis=0, keepdims=True)
    tables_ref[24:25, :] = jnp.sum(here, axis=0, keepdims=True)


def exchange_kernel(
    xs, ys, tile_hbm, offset_hbm, owner_hbm, patterns, tile, probe_hbm, hi_hbm, lo_hbm, shuffle_hbm,
    held, arrived, back, far, grads, probe_grad, info,
    tile_of, offsets, owner_map, opened, probe, hi, lo, shuffle, notes, lists, lists_smem, mid, stage, mixed,
    small_sem, load_sem, own_sem, list_sem, note_send, note_recv, first_send, first_recv, second_send, second_recv,
):
    me, at_xy, shifts = plane_steps(xs, ys)
    piece = mid.shape[1]
    reads = patterns.shape[0]

    def piece_rows(index):
        return pl.ds(pl.multiple_of(index * piece, piece), piece)

    barrier = pltpu.get_barrier_semaphore()
    for j in shifts:
        pl.semaphore_signal(barrier, inc=1, device_id=at_xy(j), device_id_type=MESH)
    smalls = [
        pltpu.make_async_copy(src, dst, small_sem.at[k])
        for k, (src, dst) in enumerate([(tile_hbm, tile_of), (offset_hbm, offsets), (owner_hbm, owner_map)])
    ]
    for load in smalls:
        load.start()
    loads = [
        pltpu.make_async_copy(src, dst, load_sem.at[k])
        for k, (src, dst) in enumerate(
            [(tile, opened), (probe_hbm, probe), (hi_hbm, hi), (lo_hbm, lo), (shuffle_hbm, shuffle)]
        )
    ]
    for load in loads:
        load.start()
    own = pltpu.make_async_copy(
        patterns.at[:, piece_rows(me), :], mid.at[pl.ds(reads * me, reads)], own_sem
    )
    own.start()
    for load in smalls:
        load.wait()
    lane = lax.broadcasted_iota(jnp.int32, (1, HALF), 1)
    note = jnp.zeros((1, HALF), jnp.int32)
    for i in range(reads):
        for f, value in enumerate((owner_map[tile_of[i]], offsets[0, i], offsets[1, i])):
            note = jnp.where(lane == 4 * f + i, value, note)
    notes[me] = note
    pl.semaphore_wait(barrier, len(shifts))

    tells = [
        remote(notes.at[me], notes.at[me], note_send.at[j], note_recv.at[j], at_xy(j)) for j in shifts
    ]
    firsts = [
        remote(
            patterns.at[:, piece_rows(at_xy(j)["tile"]), :], mid.at[pl.ds(reads * me, reads)],
            first_send.at[j], first_recv.at[j], at_xy(j),
        )
        for j in shifts
    ]
    for copy in tells + firsts:
        copy.start()
    loads[0].wait()
    open_tile(opened.at[0], held)
    for copy in tells:
        copy.wait_recv()
    lists[...] = jnp.zeros_like(lists)
    read_lists(notes, lists)
    listed = pltpu.make_async_copy(lists, lists_smem, list_sem)
    listed.start()
    listed.wait()
    for row in range(3):
        for k in range(MAX_READS):
            info[row, k] = lists_smem[MAX_READS * row + k, me]
    for k in range(MAX_READS):
        info[3, k] = lists_smem[24, me]
    for load in loads[1:]:
        load.wait()

    def run_forward(k, carry):
        a, b = lists_smem[MAX_READS + k, me], lists_smem[2 * MAX_READS + k, me]
        (bre, bim), (fre, fim) = forward_one(a, b, held, probe, hi, lo)
        back[k, 0], back[k, 1], far[k, 0], far[k, 1] = bre, bim, fre, fim
        return carry

    lax.fori_loop(0, MAX_READS // 2, run_forward, 0)
    own.wait()
    for copy in firsts:
        copy.wait_recv()

    def second(pair, j):
        ranks = pl.ds(PAIR * pair, PAIR)
        return remote(
            stage.at[j, ranks], arrived.at[ranks, piece_rows(me), :],
            second_send.at[pair, j], second_recv.at[pair, j], at_xy(j),
        )

    for pair in range(MAX_READS // PAIR):
        for j in shifts:
            to = at_xy(j)["tile"]
            for k in range(PAIR * pair, PAIR * pair + PAIR):
                stage[j, k] = mid[lists_smem[k, to]]
            second(pair, j).start()
    for k in range(MAX_READS):
        arrived[k, piece_rows(me), :] = mid[lists_smem[k, me]]
    lax.fori_loop(MAX_READS // 2, MAX_READS, run_forward, 0)
    probe_grad[...] = jnp.zeros_like(probe_grad)

    def run_backward(k, carry):
        a, b = lists_smem[MAX_READS + k, me], lists_smem[2 * MAX_READS + k, me]
        valid = jnp.where(k < lists_smem[24, me], 2.0, 0.0)
        slice1, slice0, probe_term = backward_one(
            k, a, b, valid, held, probe, hi, lo, shuffle, back, far, arrived, mixed
        )
        grads[k, 0], grads[k, 1] = slice0
        grads[k, 2], grads[k, 3] = slice1
        probe_grad[0] += probe_term[0]
        probe_grad[1] += probe_term[1]
        return carry

    def run_pair(pair, carry):
        for j in shifts:
            second(pair, j).wait_recv()
        return lax.fori_loop(PAIR * pair, PAIR * pair + PAIR, run_backward, carry)

    lax.fori_loop(0, EARLY // PAIR, run_pair, 0)
    for pair in range(EARLY // PAIR, MAX_READS // PAIR):
        for j in shifts:
            second(pair, j).wait_recv()
    for copy in tells + firsts:
        copy.wait_send()
    for pair in range(MAX_READS // PAIR):
        for j in shifts:
            second(pair, j).wait_send()


def exchange(xs, ys, *operands):
    tile_of, offsets, owner_map, patterns, tile, probe, hi, lo, shuffle = operands
    tiles = xs * ys
    piece = SIDE // tiles
    reads = patterns.shape[0]
    dma = pltpu.SemaphoreType.DMA
    vmem, smem, hbm = (
        pl.BlockSpec(memory_space=space) for space in (pltpu.VMEM, pltpu.SMEM, pltpu.HBM)
    )
    field = jax.ShapeDtypeStruct((MAX_READS, 2, SIDE, SIDE), F32)
    return pl.pallas_call(
        functools.partial(exchange_kernel, xs, ys),
        out_shape=(
            jax.ShapeDtypeStruct((4, 2 * SIDE * 4, HALF), F32),
            jax.ShapeDtypeStruct((MAX_READS, SIDE, SIDE), F32),
            field,
            field,
            jax.ShapeDtypeStruct((EARLY, 4, SIDE, SIDE), F32),
            jax.ShapeDtypeStruct(probe.shape, F32),
            jax.ShapeDtypeStruct((4, MAX_READS), jnp.int32),
        ),
        in_specs=[hbm] * 9,
        out_specs=(vmem,) * 6 + (smem,),
        scratch_shapes=[
            pltpu.SMEM(tile_of.shape, jnp.int32),
            pltpu.SMEM(offsets.shape, jnp.int32),
            pltpu.SMEM(owner_map.shape, jnp.int32),
            pltpu.VMEM(tile.shape, F32),
            pltpu.VMEM(probe.shape, F32),
            pltpu.VMEM(hi.shape, BF16),
            pltpu.VMEM(lo.shape, BF16),
            pltpu.VMEM(shuffle.shape, BF16),
            pltpu.VMEM((tiles, 1, HALF), jnp.int32),
            pltpu.VMEM((32, HALF), jnp.int32),
            pltpu.SMEM((32, HALF), jnp.int32),
            pltpu.VMEM((tiles * reads, piece, SIDE), F32),
            pltpu.VMEM((tiles, MAX_READS, piece, SIDE), F32),
            pltpu.VMEM((2, SIDE, HALF), F32),
            dma((3,)), dma((5,)), dma, dma, dma((tiles,)), dma((tiles,)), dma((tiles,)), dma((tiles,)),
            dma((MAX_READS // PAIR, tiles)), dma((MAX_READS // PAIR, tiles)),
        ],
        cost_estimate=pl.CostEstimate(flops=MAX_READS * 24 * 2 * SIDE**3, bytes_accessed=14 << 20, transcendentals=0),
        compiler_params=pltpu.CompilerParams(
            collective_id=0, has_side_effects=True, vmem_limit_bytes=16 << 20
        ),
    )(*(pltpu.with_memory_space_constraint(x, pltpu.HBM) for x in operands))


def backward_kernel(
    info, held, probe, hi, lo, shuffle, back, far, arrived, grads, probe_early,
    total, probe_grad, mixed,
):
    total[...] = jnp.zeros_like(total)
    probe_grad[...] = probe_early[...]
    reads = info[3, 0]

    def add(k, carry):
        a, b = info[1, k], info[2, k]
        for plane in range(4):
            add_patch(total.at[plane], a, b, grads[k, plane])
        return carry

    def one(k, carry):
        a, b = info[1, k], info[2, k]
        slice1, slice0, probe_term = backward_one(
            k, a, b, 2.0, held, probe, hi, lo, shuffle, back, far, arrived, mixed
        )
        for plane, value in enumerate(slice0 + slice1):
            add_patch(total.at[plane], a, b, value)
        probe_grad[0] += probe_term[0]
        probe_grad[1] += probe_term[1]
        return carry

    lax.fori_loop(0, jnp.minimum(reads, EARLY), add, 0)
    lax.fori_loop(EARLY, reads, one, 0)


def backward(info, held, probe, *operands):
    vmem, smem = pl.BlockSpec(memory_space=pltpu.VMEM), pl.BlockSpec(memory_space=pltpu.SMEM)
    return pl.pallas_call(
        backward_kernel,
        out_shape=(jax.ShapeDtypeStruct(held.shape, F32), jax.ShapeDtypeStruct(probe.shape, F32)),
        in_specs=[smem] + [vmem] * (2 + len(operands)),
        out_specs=(vmem, vmem),
        scratch_shapes=[pltpu.VMEM((2, SIDE, HALF), F32)],
        cost_estimate=pl.CostEstimate(flops=MAX_READS * 26 * 2 * SIDE**3, bytes_accessed=20 << 20, transcendentals=0),
        compiler_params=pltpu.CompilerParams(vmem_limit_bytes=8 << 20),
    )(info, held, probe, *operands)


def reduce_kernel(
    zs, xs, ys, grad, probe, out, probe_out,
    own, core_in, half_in, direct_in, plane_in, piece_in, piece_z,
    load_sem, core_send, core_recv, ring_send, ring_recv, part_send, part_recv, probe_send, probe_recv, z_send, z_recv,
    all_send, all_recv, pair_send, pair_recv,
):
    scan = lax.axis_index("scan")
    z, c = scan // CORES, scan % CORES
    tile, at_xy, shifts = plane_steps(xs, ys)
    height = own.shape[3]
    piece = piece_z.shape[1]

    def at_z(step):
        return {"scan": lax.rem(z + step + zs, zs) * CORES + c}

    pair = {"scan": z * CORES + 1 - c}
    steps = [2, 1, -1, 0]

    def rows_of(step, core):
        return pl.ds(pl.multiple_of((lax.rem(z + step + zs, zs) * CORES + core) * height, height), height)

    barrier = pltpu.get_barrier_semaphore()
    partners = [pair] + [at_z(step) for step in (1, 2, 3)] + [at_xy(j) for j in shifts]
    for partner in partners:
        pl.semaphore_signal(barrier, inc=1, device_id=partner, device_id_type=MESH)
    loads = [
        pltpu.make_async_copy(grad.at[:, :, rows_of(step, c), :], own.at[k], load_sem.at[k])
        for k, step in enumerate(steps)
    ]
    for load in loads:
        load.start()
    pl.semaphore_wait(barrier, len(partners))

    started = []

    def go(copy):
        copy.start()
        started.append(copy)
        return copy

    def core_copy(k):
        rows = rows_of(steps[k], 1 - c)
        return go(remote(grad.at[:, :, rows, :], core_in.at[k], core_send.at[k], core_recv.at[k], pair))

    def piece_rows(device):
        return pl.ds(pl.multiple_of(device["tile"] * piece, piece), piece)

    cores = [core_copy(0)]
    probe_pair = go(remote(probe.at[1 - c], plane_in, core_send.at[4], core_recv.at[4], pair))
    cores += [core_copy(k) for k in (1, 2, 3)]

    def merge(k):
        loads[k].wait()
        cores[k].wait_recv()
        own[k] = own[k] + core_in[k]

    def direct(part):
        half = pl.ds(part * (height // 2), height // 2)
        return [
            go(remote(own.at[1, 1, :, half], direct_in.at[0, :, half], part_send.at[0, part], part_recv.at[0, part], at_z(1))),
            go(remote(own.at[2, 0, :, half], direct_in.at[1, :, half], part_send.at[1, part], part_recv.at[1, part], at_z(-1))),
        ]

    merge(0)
    halves = [
        go(remote(own.at[0, 0], half_in.at[0], ring_send.at[0], ring_recv.at[0], at_z(1))),
        go(remote(own.at[0, 1], half_in.at[1], ring_send.at[1], ring_recv.at[1], at_z(-1))),
    ]
    probe_pair.wait_recv()
    plane_in[...] = plane_in[...] + probe[c]
    gathers = [
        go(remote(plane_in.at[piece_rows(at_xy(j))], piece_in.at[j], probe_send.at[j], probe_recv.at[j], at_xy(j)))
        for j in shifts
    ]
    merge(1)
    merge(2)
    straight = direct(0)
    merge(3)
    total = plane_in[piece_rows({"tile": tile}), :]
    for copy, j in zip(gathers, shifts):
        copy.wait_recv()
        total = total + piece_in[j]
    piece_z[0] = total
    across = [go(remote(piece_z.at[0], piece_z.at[k], z_send.at[k], z_recv.at[k], at_z(k))) for k in (1, 2, 3)]
    straight += direct(1)
    halves[0].wait_recv()
    own[1, 0] = own[1, 0] + half_in[0]
    up_sum = go(remote(own.at[1, 0], direct_in.at[2], ring_send.at[4], ring_recv.at[4], at_z(1)))
    halves[1].wait_recv()
    own[2, 1] = own[2, 1] + half_in[1]
    down_sum = go(remote(own.at[2, 1], direct_in.at[3], ring_send.at[5], ring_recv.at[5], at_z(-1)))
    for copy in across:
        copy.wait_recv()
    mine = piece_rows({"tile": tile})
    probe_out[c, mine, :] = (piece_z[0] + piece_z[1]) + (piece_z[2] + piece_z[3])
    spreads = [
        go(remote(probe_out.at[c, mine], probe_out.at[c, mine], all_send.at[j], all_recv.at[j], at_xy(j)))
        for j in shifts
    ]
    for copy in spreads:
        copy.wait_recv()
    last = go(remote(probe_out.at[c], probe_out.at[c], pair_send, pair_recv, pair))
    for copy in straight:
        copy.wait_recv()
    up_sum.wait_recv()
    down_sum.wait_recv()
    own[3, 0] = own[3, 0] + (direct_in[2] + direct_in[1])
    own[3, 1] = own[3, 1] + (direct_in[0] + direct_in[3])
    lines = out.shape[3]
    for plane in range(4):
        for k in range(4):
            out[0, plane // 2, plane % 2, :, k * HALF : (k + 1) * HALF] = own[
                3, plane // 2, plane % 2, pl.ds(k, lines, stride=4), :
            ]
    last.wait_recv()
    for copy in started:
        copy.wait_send()


def reduce_all(sizes, grad, probe):
    zs, xs, ys = sizes
    tiles = xs * ys
    slices, comps, side, width = grad.shape
    height = side // (zs * CORES)
    piece = SIDE // tiles
    dma = pltpu.SemaphoreType.DMA
    return pl.pallas_call(
        functools.partial(reduce_kernel, zs, xs, ys),
        out_shape=(
            jax.ShapeDtypeStruct((1, slices, comps, height // 4, 4 * width), F32),
            jax.ShapeDtypeStruct(probe.shape, F32),
        ),
        in_specs=[pl.BlockSpec(memory_space=pl.ANY), pl.BlockSpec(memory_space=pltpu.VMEM)],
        out_specs=(pl.BlockSpec(memory_space=pltpu.VMEM),) * 2,
        scratch_shapes=[
            pltpu.VMEM((4, slices, comps, height, width), F32),
            pltpu.VMEM((4, slices, comps, height, width), F32),
            pltpu.VMEM((2, comps, height, width), F32),
            pltpu.VMEM((4, comps, height, width), F32),
            pltpu.VMEM((SIDE, SIDE), F32),
            pltpu.VMEM((tiles, piece, SIDE), F32),
            pltpu.VMEM((4, piece, SIDE), F32),
            dma((4,)), dma((5,)), dma((5,)), dma((6,)), dma((6,)), dma((2, 2)), dma((2, 2)), dma((tiles,)), dma((tiles,)),
            dma((4,)), dma((4,)), dma((tiles,)), dma((tiles,)), dma, dma,
        ],
        compiler_params=pltpu.CompilerParams(
            collective_id=1, has_side_effects=True, vmem_limit_bytes=12 << 20
        ),
    )(grad, probe)


def per_device(object_tiles, probe_wave, patterns, tile_of, offsets, owner_map):
    tile_count = lax.axis_size("tile")
    high, low, shuffle = (jnp.asarray(table) for table in tables())
    zs, xs = lax.axis_size("scan") // CORES, math.isqrt(tile_count)
    ys = tile_count // xs
    held, arrived, back, far, grads, probe_early, info = exchange(
        xs, ys, tile_of, offsets.T, owner_map, patterns, object_tiles, probe_wave, high, low, shuffle
    )
    tile_grad, probe_part = backward(
        info, held, probe_wave, high, low, shuffle, back, far, arrived, grads, probe_early
    )
    tile_grad = tile_grad.reshape((2, 2) + tile_grad.shape[1:])
    object_part, probe_total = reduce_all((zs, xs, ys), tile_grad, probe_part)
    count = tile_count * lax.axis_size("scan") * patterns.shape[0]
    return object_part, probe_total / jnp.sqrt(jnp.ones((), F32) * count)


def solution(mesh):
    return jax.shard_map(
        per_device,
        mesh=mesh,
        in_specs=(
            P("tile", None, None, None, None),
            P(),
            P(("scan", "tile"), None, None),
            P(("scan", "tile")),
            P(("scan", "tile"), None),
            P(),
        ),
        out_specs=(P("tile", None, None, "scan", None), P()),
        check_vma=False,
    )
```

```python
import functools
import math

import jax
import jax.numpy as jnp
import ml_dtypes
import numpy as np
from jax import lax
from jax.experimental import pallas as pl
from jax.experimental.pallas import tpu as pltpu
from jax.sharding import PartitionSpec as P

PROP_PHASE = 0.75
SIDE = 256
HALF = 128
MAX_READS = 8
F32 = jnp.float32
BF16 = jnp.bfloat16


def embed(block):
    return np.block([[block.real, block.imag], [-block.imag, block.real]])


@functools.cache
def tables():
    index = np.arange(SIDE)
    freq = np.where(index < HALF, index, index - SIDE).astype(np.float64)
    wave = np.exp(-2j * math.pi * (index[:, None] * index[None, :] % SIDE) / SIDE) / math.sqrt(SIDE)
    step = np.exp(-1j * PROP_PHASE * freq**2 / SIDE)
    travel = wave.conj() @ (step[:, None] * wave)
    plus = (travel[:HALF, :HALF] + travel[:HALF, HALF:]) / 2
    minus = (travel[:HALF, :HALF] - travel[:HALF, HALF:]) / 2
    forms = []
    for block in (plus, minus, wave[:HALF, 0::2], wave[:HALF, 1::2]):
        form = embed(block)
        forms += [form, form.T]
    forms = np.stack(forms)
    high = forms.astype(ml_dtypes.bfloat16)
    low = (forms - high.astype(np.float64)).astype(ml_dtypes.bfloat16)
    shuffle = np.zeros((SIDE, SIDE), ml_dtypes.bfloat16)
    shuffle[2 * np.arange(HALF), np.arange(HALF)] = 1
    shuffle[2 * np.arange(HALF) + 1, HALF + np.arange(HALF)] = 1
    return high, low, shuffle


A_PLUS, A_MINUS, F_EVEN, F_ODD = 0, 2, 4, 6


def parts(x):
    high = x.astype(BF16)
    return high, (x - high.astype(F32)).astype(BF16)


def mm(x, y):
    return jnp.dot(x, y, preferred_element_type=F32)


def right(x, high_ref, low_ref, which):
    xh, xl = parts(x)
    wh, wl = high_ref[which], low_ref[which]
    total = mm(xh, wh)
    total = total + mm(xl, wh)
    return total + mm(xh, wl)


def left(x, high_ref, low_ref, which):
    xh, xl = parts(x)
    wh, wl = high_ref[which], low_ref[which]
    total = mm(wh, xh)
    total = total + mm(wl, xh)
    return total + mm(wh, xl)


def cols(re, im):
    return (
        jnp.concatenate([re[:, :HALF] + re[:, HALF:], im[:, :HALF] + im[:, HALF:]], axis=1),
        jnp.concatenate([re[:, :HALF] - re[:, HALF:], im[:, :HALF] - im[:, HALF:]], axis=1),
    )


def rows(re, im):
    return (
        jnp.concatenate([re[:HALF] + re[HALF:], im[:HALF] + im[HALF:]], axis=0),
        jnp.concatenate([re[:HALF] - re[HALF:], im[:HALF] - im[HALF:]], axis=0),
    )


def split_cols(p, q):
    return (
        jnp.concatenate([p[:, :HALF], q[:, :HALF]], axis=1),
        jnp.concatenate([p[:, HALF:], q[:, HALF:]], axis=1),
    )


def split_rows(p, q):
    return (
        jnp.concatenate([p[:HALF], q[:HALF]], axis=0),
        jnp.concatenate([p[HALF:], q[HALF:]], axis=0),
    )


def travel(re, im, hi, lo, conj):
    flip = 1 if conj else 0
    s, d = cols(re, im)
    p, q = right(s, hi, lo, A_PLUS + flip), right(d, hi, lo, A_MINUS + flip)
    re, im = split_cols(p + q, p - q)
    s, d = rows(re, im)
    p, q = left(s, hi, lo, A_PLUS + 1 - flip), left(d, hi, lo, A_MINUS + 1 - flip)
    return split_rows(p + q, p - q)


def to_far(re, im, hi, lo):
    s, d = cols(re, im)
    re, im = split_cols(right(s, hi, lo, F_EVEN), right(d, hi, lo, F_ODD))
    s, d = rows(re, im)
    return split_rows(left(s, hi, lo, F_EVEN + 1), left(d, hi, lo, F_ODD + 1))


def from_far(re, im, hi, lo):
    even, odd = (
        jnp.concatenate([re[:, :HALF], im[:, :HALF]], axis=1),
        jnp.concatenate([re[:, HALF:], im[:, HALF:]], axis=1),
    )
    p, q = right(even, hi, lo, F_EVEN + 1), right(odd, hi, lo, F_ODD + 1)
    re, im = split_cols(p + q, p - q)
    even, odd = (
        jnp.concatenate([re[:HALF], im[:HALF]], axis=0),
        jnp.concatenate([re[HALF:], im[HALF:]], axis=0),
    )
    p, q = left(even, hi, lo, F_EVEN), left(odd, hi, lo, F_ODD)
    return split_rows(p + q, p - q)


def lane_mask(shift):
    return lax.broadcasted_iota(jnp.int32, (SIDE, HALF), 1) < shift


def patch(rows_ref, comp, a, b):
    base, shift = b // HALF, b % HALF
    back = lax.rem(HALF - shift, HALF)
    tiles = [
        pltpu.roll(
            rows_ref[pl.ds(8 * a + 4 * comp + jnp.minimum(base + k, 3), SIDE, stride=8), :], back, 1
        )
        for k in range(3)
    ]
    mask = lane_mask(HALF - shift)
    return jnp.concatenate(
        [jnp.where(mask, tiles[0], tiles[1]), jnp.where(mask, tiles[1], tiles[2])], axis=1
    )


def place(padded, comp, b, value):
    base, shift = b // HALF, b % HALF
    first, second = pltpu.roll(value[:, :HALF], shift, 1), pltpu.roll(value[:, HALF:], shift, 1)
    mask = lane_mask(shift)
    zero = jnp.zeros_like(first)
    u0, u1, u2 = (
        jnp.where(mask, zero, first), jnp.where(mask, first, second), jnp.where(mask, second, zero)
    )
    at0, below2 = lane_mask(HALF * (1 - base)), lane_mask(HALF * (2 - base))
    placed = (
        jnp.where(at0, u0, zero),
        jnp.where(at0, u1, jnp.where(below2, u0, zero)),
        jnp.where(at0, u2, jnp.where(below2, u1, u0)),
        jnp.where(at0, zero, jnp.where(below2, u2, u1)),
    )
    for c in range(4):
        padded[pl.ds(8 * SIDE + 4 * comp + c, SIDE, stride=8), :] = placed[c]


def open_tile(tile, held):
    for part in range(2):
        for comp in range(2):
            for c in range(4):
                held[part, pl.ds(4 * comp + c, 2 * SIDE, stride=8), :] = tile[
                    part, comp, :, c * HALF : (c + 1) * HALF
                ]


def forward_one(a, b, held, probe, hi, lo):
    ore, oim = patch(held.at[0], 0, a, b), patch(held.at[0], 1, a, b)
    pre, pim = probe[0], probe[1]
    back = travel(pre * ore - pim * oim, pre * oim + pim * ore, hi, lo, False)
    ore, oim = patch(held.at[1], 0, a, b), patch(held.at[1], 1, a, b)
    re, im = back
    return back, to_far(re * ore - im * oim, re * oim + im * ore, hi, lo)


def backward_one(k, a, b, valid, held, probe, hi, lo, shuffle, back, far, arrived, mixed):
    for c in range(2):
        mixed[c] = arrived[k, :, c * HALF : (c + 1) * HALF]
    measured = jnp.concatenate(
        [
            jnp.concatenate([mixed[c, pl.ds(odd, HALF, stride=2), :] for c in range(2)], axis=1)
            for odd in range(2)
        ],
        axis=0,
    )
    mh, ml = parts(measured)
    measured = mm(mh, shuffle[...]) + mm(ml, shuffle[...])
    fre, fim = far[k, 0], far[k, 1]
    scale = valid * (fre * fre + fim * fim - measured)
    gre, gim = from_far(scale * fre, scale * fim, hi, lo)
    bre, bim = back[k, 0], back[k, 1]
    second = (bre * gre + bim * gim, bre * gim - bim * gre)
    ore, oim = patch(held.at[1], 0, a, b), patch(held.at[1], 1, a, b)
    gre, gim = travel(ore * gre + oim * gim, ore * gim - oim * gre, hi, lo, True)
    pre, pim = probe[0], probe[1]
    first = (pre * gre + pim * gim, pre * gim - pim * gre)
    ore, oim = patch(held.at[0], 0, a, b), patch(held.at[0], 1, a, b)
    return second, first, (ore * gre + oim * gim, ore * gim - oim * gre)


MESH = pl.DeviceIdType.MESH
CORES = 2
AHEAD = 4


def remote(src, dst, send, recv, device):
    return pltpu.make_async_remote_copy(
        src_ref=src, dst_ref=dst, send_sem=send, recv_sem=recv, device_id=device, device_id_type=MESH
    )


def plane_steps(xs, ys):
    tile = lax.axis_index("tile")
    x, y = tile // ys, tile % ys

    def at_xy(j):
        return {"tile": lax.rem(x + j // ys, xs) * ys + lax.rem(y + j % ys, ys)}

    return tile, at_xy, range(1, xs * ys)


def read_lists(notes, tables_ref):
    count = notes.shape[0]
    note = notes[:, 0, :]
    owner = lax.broadcasted_iota(jnp.int32, note.shape, 1)
    source = lax.broadcasted_iota(jnp.int32, note.shape, 0)
    here = jnp.zeros(note.shape, jnp.int32)
    values = [jnp.zeros(note.shape, jnp.int32) for _ in range(3)]
    for i in range(4):
        hit = jnp.where(jnp.broadcast_to(note[:, i : i + 1], note.shape) == owner, 1, 0)
        here = here + hit
        fields = [4 * source + i] + [
            jnp.broadcast_to(note[:, 4 * f + i : 4 * f + i + 1], note.shape) for f in (1, 2)
        ]
        values = [v + hit * f for v, f in zip(values, fields)]
    lower = (
        lax.broadcasted_iota(jnp.int32, (count, count), 0) > lax.broadcasted_iota(jnp.int32, (count, count), 1)
    ).astype(F32)
    rank = mm(lower.astype(BF16), here.astype(F32).astype(BF16)).astype(jnp.int32)
    for k in range(MAX_READS):
        chosen = here * jnp.where(rank == k, 1, 0)
        for f in range(3):
            row = MAX_READS * f + k
            tables_ref[row : row + 1, :] = jnp.sum(chosen * values[f], axis=0, keepdims=True)
    tables_ref[24:25, :] = jnp.sum(here, axis=0, keepdims=True)


def whole_kernel(
    zs, xs, ys,
    tile_hbm, offset_hbm, owner_hbm, patterns, tile, probe_hbm, hi_hbm, lo_hbm, shuffle_hbm,
    out, probe_out,
    tile_of, offsets, owner_map, opened, probe, hi, lo, shuffle, notes, lists, lists_smem, mid, stage,
    held, arrived, back, far, mixed, padded, grad, probe_grad,
    own, core_in, half_in, direct_in, plane_in, piece_in, piece_z,
    small_sem, load_sem, own_sem, list_sem, note_send, note_recv, first_send, first_recv,
    second_send, second_recv, core_send, core_recv, ring_send, ring_recv, part_send, part_recv,
    probe_send, probe_recv, z_send, z_recv, all_send, all_recv, pair_send, pair_recv,
):
    scan = lax.axis_index("scan")
    z, c = scan // CORES, scan % CORES
    me, at_xy, shifts = plane_steps(xs, ys)
    piece = mid.shape[1]
    reads = patterns.shape[0]
    height = own.shape[2]

    def at_z(step):
        return {"scan": lax.rem(z + step + zs, zs) * CORES + c}

    pair = {"scan": z * CORES + 1 - c}

    def piece_rows(index):
        return pl.ds(pl.multiple_of(index * piece, piece), piece)

    barrier = pltpu.get_barrier_semaphore()
    partners = [pair] + [at_z(step) for step in (1, 2, 3)] + [at_xy(j) for j in shifts]
    for partner in partners:
        pl.semaphore_signal(barrier, inc=1, device_id=partner, device_id_type=MESH)
    smalls = [
        pltpu.make_async_copy(src, dst, small_sem.at[k])
        for k, (src, dst) in enumerate([(tile_hbm, tile_of), (offset_hbm, offsets), (owner_hbm, owner_map)])
    ]
    loads = [
        pltpu.make_async_copy(src, dst, load_sem.at[k])
        for k, (src, dst) in enumerate(
            [(tile, opened), (probe_hbm, probe), (hi_hbm, hi), (lo_hbm, lo), (shuffle_hbm, shuffle)]
        )
    ]
    mine = pltpu.make_async_copy(
        patterns.at[:, piece_rows(me), :], mid.at[pl.ds(reads * me, reads)], own_sem
    )
    for load in smalls + loads + [mine]:
        load.start()
    for load in smalls:
        load.wait()
    lane = lax.broadcasted_iota(jnp.int32, (1, HALF), 1)
    note = jnp.zeros((1, HALF), jnp.int32)
    for i in range(reads):
        for f, value in enumerate((owner_map[tile_of[i]], offsets[0, i], offsets[1, i])):
            note = jnp.where(lane == 4 * f + i, value, note)
    notes[me] = note
    pl.semaphore_wait(barrier, len(partners))

    tells = [
        remote(notes.at[me], notes.at[me], note_send.at[j], note_recv.at[j], at_xy(j)) for j in shifts
    ]
    firsts = [
        remote(
            patterns.at[:, piece_rows(at_xy(j)["tile"]), :], mid.at[pl.ds(reads * me, reads)],
            first_send.at[j], first_recv.at[j], at_xy(j),
        )
        for j in shifts
    ]
    for copy in tells + firsts:
        copy.start()
    loads[0].wait()
    open_tile(opened.at[0], held)
    for copy in tells:
        copy.wait_recv()
    lists[...] = jnp.zeros_like(lists)
    read_lists(notes, lists)
    listed = pltpu.make_async_copy(lists, lists_smem, list_sem)
    listed.start()
    listed.wait()
    for load in loads[1:]:
        load.wait()

    def where(k):
        return lists_smem[MAX_READS + k, me], lists_smem[2 * MAX_READS + k, me]

    def run_forward(k, carry):
        a, b = where(k)
        (bre, bim), (fre, fim) = forward_one(a, b, held, probe, hi, lo)
        back[k, 0], back[k, 1], far[k, 0], far[k, 1] = bre, bim, fre, fim
        return carry

    lax.fori_loop(0, AHEAD, run_forward, 0)
    mine.wait()
    for copy in firsts:
        copy.wait_recv()

    def second(k, j):
        return remote(
            stage.at[j, k], arrived.at[k, piece_rows(me), :],
            second_send.at[k, j], second_recv.at[k, j], at_xy(j),
        )

    def send_rank(k, carry):
        for j in shifts:
            stage[j, k] = mid[lists_smem[k, at_xy(j)["tile"]]]
            second(k, j).start()
        arrived[k, piece_rows(me), :] = mid[lists_smem[k, me]]
        return carry

    lax.fori_loop(0, MAX_READS, send_rank, 0)
    lax.fori_loop(AHEAD, MAX_READS, run_forward, 0)
    probe_grad[...] = jnp.zeros_like(probe_grad)
    grad[...] = jnp.zeros_like(grad)
    padded[...] = jnp.zeros_like(padded)

    def run_backward(k, carry):
        a, b = where(k)
        valid = jnp.where(k < lists_smem[24, me], 2.0, 0.0)
        for j in shifts:
            second(k, j).wait_recv()
        slice1, slice0, probe_term = backward_one(
            k, a, b, valid, held, probe, hi, lo, shuffle, back, far, arrived, mixed
        )
        for part, values in enumerate((slice0, slice1)):
            for comp in range(2):
                place(padded.at[part], comp, b, values[comp])
        probe_grad[0] += probe_term[0]
        probe_grad[1] += probe_term[1]
        lines = 256

        def add(i, inner):
            for part in range(2):
                to = pl.ds(pl.multiple_of(i * lines, 8), lines)
                source = pl.ds((SIDE - a + i * (lines // 8)) * 8, lines)
                grad[part, to, :] = grad[part, to, :] + padded[part, source, :]
            return inner

        lax.fori_loop(0, 8 * 2 * SIDE // lines, add, 0)
        return carry

    lax.fori_loop(0, MAX_READS, run_backward, 0)

    steps = [2, 1, -1, 0]

    def rows_of(step, core):
        return pl.ds(pl.multiple_of((lax.rem(z + step + zs, zs) * CORES + core) * height, height), height)

    started = []

    def go(copy):
        copy.start()
        started.append(copy)
        return copy

    def core_copy(k):
        return go(remote(grad.at[:, rows_of(steps[k], 1 - c), :], core_in.at[k], core_send.at[k], core_recv.at[k], pair))

    cores = [core_copy(0)]
    probe_pair = go(remote(probe_grad.at[1 - c], plane_in, core_send.at[4], core_recv.at[4], pair))
    cores += [core_copy(k) for k in (1, 2, 3)]

    def merge(k):
        cores[k].wait_recv()
        own[k] = grad[:, rows_of(steps[k], c), :] + core_in[k]

    def direct(part):
        half = pl.ds(part * (height // 2), height // 2)
        return [
            go(remote(own.at[1, 1, half], direct_in.at[0, half], part_send.at[0, part], part_recv.at[0, part], at_z(1))),
            go(remote(own.at[2, 0, half], direct_in.at[1, half], part_send.at[1, part], part_recv.at[1, part], at_z(-1))),
        ]

    merge(0)
    halves = [
        go(remote(own.at[0, 0], half_in.at[0], ring_send.at[0], ring_recv.at[0], at_z(1))),
        go(remote(own.at[0, 1], half_in.at[1], ring_send.at[1], ring_recv.at[1], at_z(-1))),
    ]
    probe_pair.wait_recv()
    plane_in[...] = plane_in[...] + probe_grad[c]
    gathers = [
        go(remote(plane_in.at[piece_rows(at_xy(j)["tile"])], piece_in.at[j], probe_send.at[j], probe_recv.at[j], at_xy(j)))
        for j in shifts
    ]
    merge(1)
    merge(2)
    straight = direct(0)
    merge(3)
    total = plane_in[piece_rows(me), :]
    for copy, j in zip(gathers, shifts):
        copy.wait_recv()
        total = total + piece_in[j]
    piece_z[0] = total
    across = [go(remote(piece_z.at[0], piece_z.at[k], z_send.at[k], z_recv.at[k], at_z(k))) for k in (1, 2, 3)]
    straight += direct(1)
    halves[0].wait_recv()
    own[1, 0] = own[1, 0] + half_in[0]
    up_sum = go(remote(own.at[1, 0], direct_in.at[2], ring_send.at[2], ring_recv.at[2], at_z(1)))
    halves[1].wait_recv()
    own[2, 1] = own[2, 1] + half_in[1]
    down_sum = go(remote(own.at[2, 1], direct_in.at[3], ring_send.at[3], ring_recv.at[3], at_z(-1)))
    for copy in across:
        copy.wait_recv()
    probe_out[c, piece_rows(me), :] = (piece_z[0] + piece_z[1]) + (piece_z[2] + piece_z[3])
    spreads = [
        go(remote(probe_out.at[c, piece_rows(me)], probe_out.at[c, piece_rows(me)], all_send.at[j], all_recv.at[j], at_xy(j)))
        for j in shifts
    ]
    for copy in spreads:
        copy.wait_recv()
    last = go(remote(probe_out.at[c], probe_out.at[c], pair_send, pair_recv, pair))
    for copy in straight:
        copy.wait_recv()
    up_sum.wait_recv()
    down_sum.wait_recv()
    own[3, 0] = own[3, 0] + (direct_in[2] + direct_in[1])
    own[3, 1] = own[3, 1] + (direct_in[0] + direct_in[3])
    lines = out.shape[3]
    for plane in range(4):
        for k in range(4):
            out[0, plane // 2, plane % 2, :, k * HALF : (k + 1) * HALF] = own[
                3, plane // 2, pl.ds(4 * (plane % 2) + k, lines, stride=8), :
            ]
    last.wait_recv()
    for copy in tells + firsts + started:
        copy.wait_send()

    def sent(k, carry):
        for j in shifts:
            second(k, j).wait_send()
        return carry

    lax.fori_loop(0, MAX_READS, sent, 0)


def whole(zs, xs, ys, *operands):
    tile_of, offsets, owner_map, patterns, tile, probe, hi, lo, shuffle = operands
    tiles = xs * ys
    piece = SIDE // tiles
    reads = patterns.shape[0]
    lines = 2 * SIDE // (zs * CORES)
    height = 8 * lines
    dma = pltpu.SemaphoreType.DMA

    def vmem(*shape):
        return pltpu.VMEM(shape, F32)

    return pl.pallas_call(
        functools.partial(whole_kernel, zs, xs, ys),
        out_shape=(
            jax.ShapeDtypeStruct((1, 2, 2, lines, 2 * SIDE), F32),
            jax.ShapeDtypeStruct(probe.shape, F32),
        ),
        in_specs=[pl.BlockSpec(memory_space=pltpu.HBM)] * len(operands),
        out_specs=(pl.BlockSpec(memory_space=pltpu.VMEM),) * 2,
        scratch_shapes=[
            pltpu.SMEM(tile_of.shape, jnp.int32),
            pltpu.SMEM(offsets.shape, jnp.int32),
            pltpu.SMEM(owner_map.shape, jnp.int32),
            vmem(*tile.shape),
            vmem(*probe.shape),
            pltpu.VMEM(hi.shape, BF16),
            pltpu.VMEM(lo.shape, BF16),
            pltpu.VMEM(shuffle.shape, BF16),
            pltpu.VMEM((tiles, 1, HALF), jnp.int32),
            pltpu.VMEM((32, HALF), jnp.int32),
            pltpu.SMEM((32, HALF), jnp.int32),
            vmem(tiles * reads, piece, SIDE),
            vmem(tiles, MAX_READS, piece, SIDE),
            vmem(2, 8 * 2 * SIDE, HALF),
            vmem(MAX_READS, SIDE, SIDE),
            vmem(MAX_READS, 2, SIDE, SIDE),
            vmem(MAX_READS, 2, SIDE, SIDE),
            vmem(2, SIDE, HALF),
            vmem(2, 8 * 3 * SIDE, HALF),
            vmem(2, 8 * 2 * SIDE, HALF),
            vmem(2, SIDE, SIDE),
            vmem(4, 2, height, HALF),
            vmem(4, 2, height, HALF),
            vmem(2, height, HALF),
            vmem(4, height, HALF),
            vmem(SIDE, SIDE),
            vmem(tiles, piece, SIDE),
            vmem(4, piece, SIDE),
            dma((3,)), dma((5,)), dma, dma, dma((tiles,)), dma((tiles,)), dma((tiles,)), dma((tiles,)),
            dma((MAX_READS, tiles)), dma((MAX_READS, tiles)), dma((5,)), dma((5,)), dma((4,)), dma((4,)),
            dma((2, 2)), dma((2, 2)), dma((tiles,)), dma((tiles,)), dma((4,)), dma((4,)),
            dma((tiles,)), dma((tiles,)), dma, dma,
        ],
        cost_estimate=pl.CostEstimate(
            flops=MAX_READS * 50 * 2 * SIDE**3, bytes_accessed=10 << 20, transcendentals=0
        ),
        compiler_params=pltpu.CompilerParams(
            collective_id=0, has_side_effects=True, vmem_limit_bytes=56 << 20
        ),
    )(*(pltpu.with_memory_space_constraint(x, pltpu.HBM) for x in operands))


def per_device(object_tiles, probe_wave, patterns, tile_of, offsets, owner_map):
    tile_count = lax.axis_size("tile")
    high, low, shuffle = (jnp.asarray(table) for table in tables())
    zs, xs = lax.axis_size("scan") // CORES, math.isqrt(tile_count)
    ys = tile_count // xs
    object_part, probe_total = whole(
        zs, xs, ys,
        tile_of, offsets.T, owner_map, patterns, object_tiles, probe_wave, high, low, shuffle,
    )
    count = tile_count * lax.axis_size("scan") * patterns.shape[0]
    return object_part, probe_total / jnp.sqrt(jnp.ones((), F32) * count)


def solution(mesh):
    return jax.shard_map(
        per_device,
        mesh=mesh,
        in_specs=(
            P("tile", None, None, None, None),
            P(),
            P(("scan", "tile"), None, None),
            P(("scan", "tile")),
            P(("scan", "tile"), None),
            P(),
        ),
        out_specs=(P("tile", None, None, "scan", None), P()),
        check_vma=False,
    )
```

```python
import functools
import math

import jax
import jax.numpy as jnp
import ml_dtypes
import numpy as np
from jax import lax
from jax.experimental import pallas as pl
from jax.experimental.pallas import tpu as pltpu
from jax.sharding import PartitionSpec as P

PROP_PHASE = 0.75
SIDE = 256
HALF = 128
MAX_READS = 8
F32 = jnp.float32
BF16 = jnp.bfloat16


def embed(block):
    return np.block([[block.real, block.imag], [-block.imag, block.real]])


@functools.cache
def tables():
    index = np.arange(SIDE)
    freq = np.where(index < HALF, index, index - SIDE).astype(np.float64)
    wave = np.exp(-2j * math.pi * (index[:, None] * index[None, :] % SIDE) / SIDE) / math.sqrt(SIDE)
    step = np.exp(-1j * PROP_PHASE * freq**2 / SIDE)
    travel = wave.conj() @ (step[:, None] * wave)
    plus = (travel[:HALF, :HALF] + travel[:HALF, HALF:]) / 2
    minus = (travel[:HALF, :HALF] - travel[:HALF, HALF:]) / 2
    forms = []
    for block in (plus, minus, wave[:HALF, 0::2], wave[:HALF, 1::2]):
        form = embed(block)
        forms += [form, form.T]
    forms = np.stack(forms)
    high = forms.astype(ml_dtypes.bfloat16)
    low = (forms - high.astype(np.float64)).astype(ml_dtypes.bfloat16)
    shuffle = np.zeros((SIDE, SIDE), ml_dtypes.bfloat16)
    shuffle[2 * np.arange(HALF), np.arange(HALF)] = 1
    shuffle[2 * np.arange(HALF) + 1, HALF + np.arange(HALF)] = 1
    return high, low, shuffle


A_PLUS, A_MINUS, F_EVEN, F_ODD = 0, 2, 4, 6


def parts(x):
    high = x.astype(BF16)
    return high, (x - high.astype(F32)).astype(BF16)


def mm(x, y):
    return jnp.dot(x, y, preferred_element_type=F32)


def right(x, high_ref, low_ref, which):
    xh, xl = parts(x)
    wh, wl = high_ref[which], low_ref[which]
    total = mm(xh, wh)
    total = total + mm(xl, wh)
    return total + mm(xh, wl)


def left(x, high_ref, low_ref, which):
    xh, xl = parts(x)
    wh, wl = high_ref[which], low_ref[which]
    total = mm(wh, xh)
    total = total + mm(wl, xh)
    return total + mm(wh, xl)


def cols(re, im):
    return (
        jnp.concatenate([re[:, :HALF] + re[:, HALF:], im[:, :HALF] + im[:, HALF:]], axis=1),
        jnp.concatenate([re[:, :HALF] - re[:, HALF:], im[:, :HALF] - im[:, HALF:]], axis=1),
    )


def rows(re, im):
    return (
        jnp.concatenate([re[:HALF] + re[HALF:], im[:HALF] + im[HALF:]], axis=0),
        jnp.concatenate([re[:HALF] - re[HALF:], im[:HALF] - im[HALF:]], axis=0),
    )


def split_cols(p, q):
    return (
        jnp.concatenate([p[:, :HALF], q[:, :HALF]], axis=1),
        jnp.concatenate([p[:, HALF:], q[:, HALF:]], axis=1),
    )


def split_rows(p, q):
    return (
        jnp.concatenate([p[:HALF], q[:HALF]], axis=0),
        jnp.concatenate([p[HALF:], q[HALF:]], axis=0),
    )


def travel(re, im, hi, lo, conj):
    flip = 1 if conj else 0
    s, d = cols(re, im)
    p, q = right(s, hi, lo, A_PLUS + flip), right(d, hi, lo, A_MINUS + flip)
    re, im = split_cols(p + q, p - q)
    s, d = rows(re, im)
    p, q = left(s, hi, lo, A_PLUS + 1 - flip), left(d, hi, lo, A_MINUS + 1 - flip)
    return split_rows(p + q, p - q)


def to_far(re, im, hi, lo):
    s, d = cols(re, im)
    re, im = split_cols(right(s, hi, lo, F_EVEN), right(d, hi, lo, F_ODD))
    s, d = rows(re, im)
    return split_rows(left(s, hi, lo, F_EVEN + 1), left(d, hi, lo, F_ODD + 1))


def from_far(re, im, hi, lo):
    even, odd = (
        jnp.concatenate([re[:, :HALF], im[:, :HALF]], axis=1),
        jnp.concatenate([re[:, HALF:], im[:, HALF:]], axis=1),
    )
    p, q = right(even, hi, lo, F_EVEN + 1), right(odd, hi, lo, F_ODD + 1)
    re, im = split_cols(p + q, p - q)
    even, odd = (
        jnp.concatenate([re[:HALF], im[:HALF]], axis=0),
        jnp.concatenate([re[HALF:], im[HALF:]], axis=0),
    )
    p, q = left(even, hi, lo, F_EVEN), left(odd, hi, lo, F_ODD)
    return split_rows(p + q, p - q)


def lane_mask(shift):
    return lax.broadcasted_iota(jnp.int32, (SIDE, HALF), 1) < shift


def patch(rows_ref, comp, a, b):
    base, shift = b // HALF, b % HALF
    back = lax.rem(HALF - shift, HALF)
    tiles = [
        pltpu.roll(
            rows_ref[pl.ds(8 * a + 4 * comp + jnp.minimum(base + k, 3), SIDE, stride=8), :], back, 1
        )
        for k in range(3)
    ]
    mask = lane_mask(HALF - shift)
    return jnp.concatenate(
        [jnp.where(mask, tiles[0], tiles[1]), jnp.where(mask, tiles[1], tiles[2])], axis=1
    )


def place(padded, comp, b, value):
    base, shift = b // HALF, b % HALF
    first, second = pltpu.roll(value[:, :HALF], shift, 1), pltpu.roll(value[:, HALF:], shift, 1)
    mask = lane_mask(shift)
    zero = jnp.zeros_like(first)
    u0, u1, u2 = (
        jnp.where(mask, zero, first), jnp.where(mask, first, second), jnp.where(mask, second, zero)
    )
    at0, below2 = lane_mask(HALF * (1 - base)), lane_mask(HALF * (2 - base))
    placed = (
        jnp.where(at0, u0, zero),
        jnp.where(at0, u1, jnp.where(below2, u0, zero)),
        jnp.where(at0, u2, jnp.where(below2, u1, u0)),
        jnp.where(at0, zero, jnp.where(below2, u2, u1)),
    )
    for c in range(4):
        padded[pl.ds(8 * SIDE + 4 * comp + c, SIDE, stride=8), :] = placed[c]


def open_tile(tile, held):
    for part in range(2):
        for comp in range(2):
            for c in range(4):
                held[part, pl.ds(4 * comp + c, 2 * SIDE, stride=8), :] = tile[
                    part, comp, :, c * HALF : (c + 1) * HALF
                ]


def forward_one(a, b, held, probe, hi, lo):
    ore, oim = patch(held.at[0], 0, a, b), patch(held.at[0], 1, a, b)
    pre, pim = probe[0], probe[1]
    back = travel(pre * ore - pim * oim, pre * oim + pim * ore, hi, lo, False)
    ore, oim = patch(held.at[1], 0, a, b), patch(held.at[1], 1, a, b)
    re, im = back
    return back, to_far(re * ore - im * oim, re * oim + im * ore, hi, lo)


def backward_one(k, a, b, valid, held, probe, hi, lo, shuffle, back, far, arrived, mixed):
    for c in range(2):
        mixed[c] = arrived[k, :, c * HALF : (c + 1) * HALF]
    measured = jnp.concatenate(
        [
            jnp.concatenate([mixed[c, pl.ds(odd, HALF, stride=2), :] for c in range(2)], axis=1)
            for odd in range(2)
        ],
        axis=0,
    )
    mh, ml = parts(measured)
    measured = mm(mh, shuffle[...]) + mm(ml, shuffle[...])
    fre, fim = far[k, 0], far[k, 1]
    scale = valid * (fre * fre + fim * fim - measured)
    gre, gim = from_far(scale * fre, scale * fim, hi, lo)
    bre, bim = back[k, 0], back[k, 1]
    second = (bre * gre + bim * gim, bre * gim - bim * gre)
    ore, oim = patch(held.at[1], 0, a, b), patch(held.at[1], 1, a, b)
    gre, gim = travel(ore * gre + oim * gim, ore * gim - oim * gre, hi, lo, True)
    pre, pim = probe[0], probe[1]
    first = (pre * gre + pim * gim, pre * gim - pim * gre)
    ore, oim = patch(held.at[0], 0, a, b), patch(held.at[0], 1, a, b)
    return second, first, (ore * gre + oim * gim, ore * gim - oim * gre)


MESH = pl.DeviceIdType.MESH
CORES = 2
AHEAD = 4


def remote(src, dst, send, recv, device):
    return pltpu.make_async_remote_copy(
        src_ref=src, dst_ref=dst, send_sem=send, recv_sem=recv, device_id=device, device_id_type=MESH
    )


def plane_steps(xs, ys):
    tile = lax.axis_index("tile")
    x, y = tile // ys, tile % ys

    def at_xy(j):
        return {"tile": lax.rem(x + j // ys, xs) * ys + lax.rem(y + j % ys, ys)}

    return tile, at_xy, range(1, xs * ys)


def read_lists(notes, tables_ref):
    count = notes.shape[0]
    note = notes[:, 0, :]
    owner = lax.broadcasted_iota(jnp.int32, note.shape, 1)
    source = lax.broadcasted_iota(jnp.int32, note.shape, 0)
    here = jnp.zeros(note.shape, jnp.int32)
    values = [jnp.zeros(note.shape, jnp.int32) for _ in range(3)]
    for i in range(4):
        hit = jnp.where(jnp.broadcast_to(note[:, i : i + 1], note.shape) == owner, 1, 0)
        here = here + hit
        fields = [4 * source + i] + [
            jnp.broadcast_to(note[:, 4 * f + i : 4 * f + i + 1], note.shape) for f in (1, 2)
        ]
        values = [v + hit * f for v, f in zip(values, fields)]
    lower = (
        lax.broadcasted_iota(jnp.int32, (count, count), 0) > lax.broadcasted_iota(jnp.int32, (count, count), 1)
    ).astype(F32)
    rank = mm(lower.astype(BF16), here.astype(F32).astype(BF16)).astype(jnp.int32)
    for k in range(MAX_READS):
        chosen = here * jnp.where(rank == k, 1, 0)
        for f in range(3):
            row = MAX_READS * f + k
            tables_ref[row : row + 1, :] = jnp.sum(chosen * values[f], axis=0, keepdims=True)
    tables_ref[24:25, :] = jnp.sum(here, axis=0, keepdims=True)


def whole_kernel(
    zs, xs, ys,
    tile_hbm, offset_hbm, owner_hbm, patterns, tile, probe_hbm, hi_hbm, lo_hbm, shuffle_hbm,
    out, probe_out,
    tile_of, offsets, owner_map, opened, probe, hi, lo, shuffle, notes, lists, lists_smem, mid, stage,
    held, arrived, back, far, mixed, padded, grad, probe_grad,
    own, core_in, half_in, direct_in, plane_in, piece_in, piece_z,
    small_sem, load_sem, own_sem, list_sem, note_send, note_recv, first_send, first_recv,
    second_send, second_recv, core_send, core_recv, ring_send, ring_recv, part_send, part_recv,
    probe_send, probe_recv, z_send, z_recv, all_send, all_recv, pair_send, pair_recv,
):
    scan = lax.axis_index("scan")
    z, c = scan // CORES, scan % CORES
    me, at_xy, shifts = plane_steps(xs, ys)
    piece = mid.shape[1]
    reads = patterns.shape[0]
    height = own.shape[2]

    def at_z(step):
        return {"scan": lax.rem(z + step + zs, zs) * CORES + c}

    pair = {"scan": z * CORES + 1 - c}

    def piece_rows(index):
        return pl.ds(pl.multiple_of(index * piece, piece), piece)

    barrier = pltpu.get_barrier_semaphore()
    partners = [pair] + [at_z(step) for step in (1, 2, 3)] + [at_xy(j) for j in shifts]
    for partner in partners:
        pl.semaphore_signal(barrier, inc=1, device_id=partner, device_id_type=MESH)
    smalls = [
        pltpu.make_async_copy(src, dst, small_sem.at[k])
        for k, (src, dst) in enumerate([(tile_hbm, tile_of), (offset_hbm, offsets), (owner_hbm, owner_map)])
    ]
    loads = [
        pltpu.make_async_copy(src, dst, load_sem.at[k])
        for k, (src, dst) in enumerate(
            [(tile, opened), (probe_hbm, probe), (hi_hbm, hi), (lo_hbm, lo), (shuffle_hbm, shuffle)]
        )
    ]
    mine = pltpu.make_async_copy(
        patterns.at[:, piece_rows(me), :], mid.at[pl.ds(reads * me, reads)], own_sem
    )
    for load in smalls + loads + [mine]:
        load.start()
    for load in smalls:
        load.wait()
    lane = lax.broadcasted_iota(jnp.int32, (1, HALF), 1)
    note = jnp.zeros((1, HALF), jnp.int32)
    for i in range(reads):
        for f, value in enumerate((owner_map[tile_of[i]], offsets[0, i], offsets[1, i])):
            note = jnp.where(lane == 4 * f + i, value, note)
    notes[me] = note
    pl.semaphore_wait(barrier, len(partners))

    tells = [
        remote(notes.at[me], notes.at[me], note_send.at[j], note_recv.at[j], at_xy(j)) for j in shifts
    ]
    firsts = [
        remote(
            patterns.at[:, piece_rows(at_xy(j)["tile"]), :], mid.at[pl.ds(reads * me, reads)],
            first_send.at[j], first_recv.at[j], at_xy(j),
        )
        for j in shifts
    ]
    for copy in tells + firsts:
        copy.start()
    probe_grad[...] = jnp.zeros_like(probe_grad)
    grad[...] = jnp.zeros_like(grad)
    border = jnp.zeros((2, 8 * SIDE, HALF), F32)
    padded[:, : 8 * SIDE, :] = border
    padded[:, 16 * SIDE :, :] = border
    loads[0].wait()
    open_tile(opened.at[0], held)
    for copy in tells:
        copy.wait_recv()
    lists[...] = jnp.zeros_like(lists)
    read_lists(notes, lists)
    listed = pltpu.make_async_copy(lists, lists_smem, list_sem)
    listed.start()
    listed.wait()
    for load in loads[1:]:
        load.wait()

    def where(k):
        return lists_smem[MAX_READS + k, me], lists_smem[2 * MAX_READS + k, me]

    def run_forward(k, carry):
        a, b = where(k)
        (bre, bim), (fre, fim) = forward_one(a, b, held, probe, hi, lo)
        back[k, 0], back[k, 1], far[k, 0], far[k, 1] = bre, bim, fre, fim
        return carry

    lax.fori_loop(0, AHEAD, run_forward, 0)
    mine.wait()
    for copy in firsts:
        copy.wait_recv()

    def second(k, j):
        return remote(
            stage.at[j, k], arrived.at[k, piece_rows(me), :],
            second_send.at[k, j], second_recv.at[k, j], at_xy(j),
        )

    def send_rank(k, carry):
        for j in shifts:
            stage[j, k] = mid[lists_smem[k, at_xy(j)["tile"]]]
            second(k, j).start()
        arrived[k, piece_rows(me), :] = mid[lists_smem[k, me]]
        return carry

    lax.fori_loop(0, MAX_READS, send_rank, 0)
    lax.fori_loop(AHEAD, MAX_READS, run_forward, 0)

    def run_backward(k, carry):
        a, b = where(k)
        valid = jnp.where(k < lists_smem[24, me], 2.0, 0.0)
        for j in shifts:
            second(k, j).wait_recv()
        slice1, slice0, probe_term = backward_one(
            k, a, b, valid, held, probe, hi, lo, shuffle, back, far, arrived, mixed
        )
        for part, values in enumerate((slice0, slice1)):
            for comp in range(2):
                place(padded.at[part], comp, b, values[comp])
        probe_grad[0] += probe_term[0]
        probe_grad[1] += probe_term[1]
        lines = 512

        def add(i, inner):
            for part in range(2):
                to = pl.ds(pl.multiple_of(i * lines, 8), lines)
                source = pl.ds((SIDE - a + i * (lines // 8)) * 8, lines)
                grad[part, to, :] = grad[part, to, :] + padded[part, source, :]
            return inner

        lax.fori_loop(0, 8 * 2 * SIDE // lines, add, 0)
        return carry

    lax.fori_loop(0, MAX_READS, run_backward, 0)

    steps = [2, 1, -1, 0]

    def rows_of(step, core):
        return pl.ds(pl.multiple_of((lax.rem(z + step + zs, zs) * CORES + core) * height, height), height)

    started = []

    def go(copy):
        copy.start()
        started.append(copy)
        return copy

    def core_copy(k):
        return go(remote(grad.at[:, rows_of(steps[k], 1 - c), :], core_in.at[k], core_send.at[k], core_recv.at[k], pair))

    cores = [core_copy(0)]
    probe_pair = go(remote(probe_grad.at[1 - c], plane_in, core_send.at[4], core_recv.at[4], pair))
    cores += [core_copy(k) for k in (1, 2, 3)]

    def merge(k):
        cores[k].wait_recv()
        own[k] = grad[:, rows_of(steps[k], c), :] + core_in[k]

    def direct(part):
        half = pl.ds(part * (height // 2), height // 2)
        return [
            go(remote(own.at[1, 1, half], direct_in.at[0, half], part_send.at[0, part], part_recv.at[0, part], at_z(1))),
            go(remote(own.at[2, 0, half], direct_in.at[1, half], part_send.at[1, part], part_recv.at[1, part], at_z(-1))),
        ]

    merge(0)
    halves = [
        go(remote(own.at[0, 0], half_in.at[0], ring_send.at[0], ring_recv.at[0], at_z(1))),
        go(remote(own.at[0, 1], half_in.at[1], ring_send.at[1], ring_recv.at[1], at_z(-1))),
    ]
    probe_pair.wait_recv()
    plane_in[...] = plane_in[...] + probe_grad[c]
    gathers = [
        go(remote(plane_in.at[piece_rows(at_xy(j)["tile"])], piece_in.at[j], probe_send.at[j], probe_recv.at[j], at_xy(j)))
        for j in shifts
    ]
    merge(1)
    merge(2)
    straight = direct(0)
    merge(3)
    total = plane_in[piece_rows(me), :]
    for copy, j in zip(gathers, shifts):
        copy.wait_recv()
        total = total + piece_in[j]
    piece_z[0] = total
    across = [go(remote(piece_z.at[0], piece_z.at[k], z_send.at[k], z_recv.at[k], at_z(k))) for k in (1, 2, 3)]
    straight += direct(1)
    halves[0].wait_recv()
    own[1, 0] = own[1, 0] + half_in[0]
    up_sum = go(remote(own.at[1, 0], direct_in.at[2], ring_send.at[2], ring_recv.at[2], at_z(1)))
    halves[1].wait_recv()
    own[2, 1] = own[2, 1] + half_in[1]
    down_sum = go(remote(own.at[2, 1], direct_in.at[3], ring_send.at[3], ring_recv.at[3], at_z(-1)))
    for copy in across:
        copy.wait_recv()
    probe_out[c, piece_rows(me), :] = (piece_z[0] + piece_z[1]) + (piece_z[2] + piece_z[3])
    spreads = [
        go(remote(probe_out.at[c, piece_rows(me)], probe_out.at[c, piece_rows(me)], all_send.at[j], all_recv.at[j], at_xy(j)))
        for j in shifts
    ]
    for copy in spreads:
        copy.wait_recv()
    last = go(remote(probe_out.at[c], probe_out.at[c], pair_send, pair_recv, pair))
    for copy in straight:
        copy.wait_recv()
    up_sum.wait_recv()
    down_sum.wait_recv()
    own[3, 0] = own[3, 0] + (direct_in[2] + direct_in[1])
    own[3, 1] = own[3, 1] + (direct_in[0] + direct_in[3])
    lines = out.shape[3]
    for plane in range(4):
        for k in range(4):
            out[0, plane // 2, plane % 2, :, k * HALF : (k + 1) * HALF] = own[
                3, plane // 2, pl.ds(4 * (plane % 2) + k, lines, stride=8), :
            ]
    last.wait_recv()
    for copy in tells + firsts + started:
        copy.wait_send()

    def sent(k, carry):
        for j in shifts:
            second(k, j).wait_send()
        return carry

    lax.fori_loop(0, MAX_READS, sent, 0)


def whole(zs, xs, ys, *operands):
    tile_of, offsets, owner_map, patterns, tile, probe, hi, lo, shuffle = operands
    tiles = xs * ys
    piece = SIDE // tiles
    reads = patterns.shape[0]
    lines = 2 * SIDE // (zs * CORES)
    height = 8 * lines
    dma = pltpu.SemaphoreType.DMA

    def vmem(*shape):
        return pltpu.VMEM(shape, F32)

    return pl.pallas_call(
        functools.partial(whole_kernel, zs, xs, ys),
        out_shape=(
            jax.ShapeDtypeStruct((1, 2, 2, lines, 2 * SIDE), F32),
            jax.ShapeDtypeStruct(probe.shape, F32),
        ),
        in_specs=[pl.BlockSpec(memory_space=pltpu.HBM)] * len(operands),
        out_specs=(pl.BlockSpec(memory_space=pltpu.VMEM),) * 2,
        scratch_shapes=[
            pltpu.SMEM(tile_of.shape, jnp.int32),
            pltpu.SMEM(offsets.shape, jnp.int32),
            pltpu.SMEM(owner_map.shape, jnp.int32),
            vmem(*tile.shape),
            vmem(*probe.shape),
            pltpu.VMEM(hi.shape, BF16),
            pltpu.VMEM(lo.shape, BF16),
            pltpu.VMEM(shuffle.shape, BF16),
            pltpu.VMEM((tiles, 1, HALF), jnp.int32),
            pltpu.VMEM((32, HALF), jnp.int32),
            pltpu.SMEM((32, HALF), jnp.int32),
            vmem(tiles * reads, piece, SIDE),
            vmem(tiles, MAX_READS, piece, SIDE),
            vmem(2, 8 * 2 * SIDE, HALF),
            vmem(MAX_READS, SIDE, SIDE),
            vmem(MAX_READS, 2, SIDE, SIDE),
            vmem(MAX_READS, 2, SIDE, SIDE),
            vmem(2, SIDE, HALF),
            vmem(2, 8 * 3 * SIDE, HALF),
            vmem(2, 8 * 2 * SIDE, HALF),
            vmem(2, SIDE, SIDE),
            vmem(4, 2, height, HALF),
            vmem(4, 2, height, HALF),
            vmem(2, height, HALF),
            vmem(4, height, HALF),
            vmem(SIDE, SIDE),
            vmem(tiles, piece, SIDE),
            vmem(4, piece, SIDE),
            dma((3,)), dma((5,)), dma, dma, dma((tiles,)), dma((tiles,)), dma((tiles,)), dma((tiles,)),
            dma((MAX_READS, tiles)), dma((MAX_READS, tiles)), dma((5,)), dma((5,)), dma((4,)), dma((4,)),
            dma((2, 2)), dma((2, 2)), dma((tiles,)), dma((tiles,)), dma((4,)), dma((4,)),
            dma((tiles,)), dma((tiles,)), dma, dma,
        ],
        cost_estimate=pl.CostEstimate(
            flops=MAX_READS * 50 * 2 * SIDE**3, bytes_accessed=10 << 20, transcendentals=0
        ),
        compiler_params=pltpu.CompilerParams(
            collective_id=0, has_side_effects=True, vmem_limit_bytes=46 << 20
        ),
    )(*(pltpu.with_memory_space_constraint(x, pltpu.HBM) for x in operands))


def per_device(object_tiles, probe_wave, patterns, tile_of, offsets, owner_map):
    tile_count = lax.axis_size("tile")
    high, low, shuffle = (jnp.asarray(table) for table in tables())
    zs, xs = lax.axis_size("scan") // CORES, math.isqrt(tile_count)
    ys = tile_count // xs
    object_part, probe_total = whole(
        zs, xs, ys,
        tile_of, offsets.T, owner_map, patterns, object_tiles, probe_wave, high, low, shuffle,
    )
    count = tile_count * lax.axis_size("scan") * patterns.shape[0]
    return object_part, probe_total / jnp.sqrt(jnp.ones((), F32) * count)


def solution(mesh):
    return jax.shard_map(
        per_device,
        mesh=mesh,
        in_specs=(
            P("tile", None, None, None, None),
            P(),
            P(("scan", "tile"), None, None),
            P(("scan", "tile")),
            P(("scan", "tile"), None),
            P(),
        ),
        out_specs=(P("tile", None, None, "scan", None), P()),
        check_vma=False,
    )
```

```python
import functools
import math

import jax
import jax.numpy as jnp
import ml_dtypes
import numpy as np
from jax import lax
from jax.experimental import pallas as pl
from jax.experimental.pallas import tpu as pltpu
from jax.sharding import PartitionSpec as P

PROP_PHASE = 0.75
SIDE = 256
HALF = 128
MAX_READS = 8
F32 = jnp.float32
BF16 = jnp.bfloat16


def embed(block):
    return np.block([[block.real, block.imag], [-block.imag, block.real]])


@functools.cache
def tables():
    index = np.arange(SIDE)
    freq = np.where(index < HALF, index, index - SIDE).astype(np.float64)
    wave = np.exp(-2j * math.pi * (index[:, None] * index[None, :] % SIDE) / SIDE) / math.sqrt(SIDE)
    step = np.exp(-1j * PROP_PHASE * freq**2 / SIDE)
    travel = wave.conj() @ (step[:, None] * wave)
    plus = (travel[:HALF, :HALF] + travel[:HALF, HALF:]) / 2
    minus = (travel[:HALF, :HALF] - travel[:HALF, HALF:]) / 2
    forms = []
    for block in (plus, minus, wave[:HALF, 0::2], wave[:HALF, 1::2]):
        form = embed(block)
        forms += [form, form.T]
    forms = np.stack(forms)
    high = forms.astype(ml_dtypes.bfloat16)
    low = (forms - high.astype(np.float64)).astype(ml_dtypes.bfloat16)
    shuffle = np.zeros((SIDE, SIDE), ml_dtypes.bfloat16)
    shuffle[2 * np.arange(HALF), np.arange(HALF)] = 1
    shuffle[2 * np.arange(HALF) + 1, HALF + np.arange(HALF)] = 1
    return high, low, shuffle


A_PLUS, A_MINUS, F_EVEN, F_ODD = 0, 2, 4, 6


def parts(x):
    high = x.astype(BF16)
    return high, (x - high.astype(F32)).astype(BF16)


def mm(x, y):
    return jnp.dot(x, y, preferred_element_type=F32)


def right(x, high_ref, low_ref, which):
    xh, xl = parts(x)
    wh, wl = high_ref[which], low_ref[which]
    total = mm(xh, wh)
    total = total + mm(xl, wh)
    return total + mm(xh, wl)


def left(x, high_ref, low_ref, which):
    xh, xl = parts(x)
    wh, wl = high_ref[which], low_ref[which]
    total = mm(wh, xh)
    total = total + mm(wl, xh)
    return total + mm(wh, xl)


def cols(re, im):
    return (
        jnp.concatenate([re[:, :HALF] + re[:, HALF:], im[:, :HALF] + im[:, HALF:]], axis=1),
        jnp.concatenate([re[:, :HALF] - re[:, HALF:], im[:, :HALF] - im[:, HALF:]], axis=1),
    )


def rows(re, im):
    return (
        jnp.concatenate([re[:HALF] + re[HALF:], im[:HALF] + im[HALF:]], axis=0),
        jnp.concatenate([re[:HALF] - re[HALF:], im[:HALF] - im[HALF:]], axis=0),
    )


def split_cols(p, q):
    return (
        jnp.concatenate([p[:, :HALF], q[:, :HALF]], axis=1),
        jnp.concatenate([p[:, HALF:], q[:, HALF:]], axis=1),
    )


def split_rows(p, q):
    return (
        jnp.concatenate([p[:HALF], q[:HALF]], axis=0),
        jnp.concatenate([p[HALF:], q[HALF:]], axis=0),
    )


def travel(re, im, hi, lo, conj):
    flip = 1 if conj else 0
    s, d = cols(re, im)
    p, q = right(s, hi, lo, A_PLUS + flip), right(d, hi, lo, A_MINUS + flip)
    re, im = split_cols(p + q, p - q)
    s, d = rows(re, im)
    p, q = left(s, hi, lo, A_PLUS + 1 - flip), left(d, hi, lo, A_MINUS + 1 - flip)
    return split_rows(p + q, p - q)


def to_far(re, im, hi, lo):
    s, d = cols(re, im)
    re, im = split_cols(right(s, hi, lo, F_EVEN), right(d, hi, lo, F_ODD))
    s, d = rows(re, im)
    return split_rows(left(s, hi, lo, F_EVEN + 1), left(d, hi, lo, F_ODD + 1))


def from_far(re, im, hi, lo):
    even, odd = (
        jnp.concatenate([re[:, :HALF], im[:, :HALF]], axis=1),
        jnp.concatenate([re[:, HALF:], im[:, HALF:]], axis=1),
    )
    p, q = right(even, hi, lo, F_EVEN + 1), right(odd, hi, lo, F_ODD + 1)
    re, im = split_cols(p + q, p - q)
    even, odd = (
        jnp.concatenate([re[:HALF], im[:HALF]], axis=0),
        jnp.concatenate([re[HALF:], im[HALF:]], axis=0),
    )
    p, q = left(even, hi, lo, F_EVEN), left(odd, hi, lo, F_ODD)
    return split_rows(p + q, p - q)


def lane_mask(shift):
    return lax.broadcasted_iota(jnp.int32, (SIDE, HALF), 1) < shift


def patch(rows_ref, comp, a, b):
    base, shift = b // HALF, b % HALF
    back = lax.rem(HALF - shift, HALF)
    tiles = [
        pltpu.roll(
            rows_ref[pl.ds(8 * a + 4 * comp + jnp.minimum(base + k, 3), SIDE, stride=8), :], back, 1
        )
        for k in range(3)
    ]
    mask = lane_mask(HALF - shift)
    return jnp.concatenate(
        [jnp.where(mask, tiles[0], tiles[1]), jnp.where(mask, tiles[1], tiles[2])], axis=1
    )


def place(padded, comp, b, value):
    base, shift = b // HALF, b % HALF
    first, second = pltpu.roll(value[:, :HALF], shift, 1), pltpu.roll(value[:, HALF:], shift, 1)
    mask = lane_mask(shift)
    zero = jnp.zeros_like(first)
    u0, u1, u2 = (
        jnp.where(mask, zero, first), jnp.where(mask, first, second), jnp.where(mask, second, zero)
    )
    at0, below2 = lane_mask(HALF * (1 - base)), lane_mask(HALF * (2 - base))
    placed = (
        jnp.where(at0, u0, zero),
        jnp.where(at0, u1, jnp.where(below2, u0, zero)),
        jnp.where(at0, u2, jnp.where(below2, u1, u0)),
        jnp.where(at0, zero, jnp.where(below2, u2, u1)),
    )
    for c in range(4):
        padded[pl.ds(8 * SIDE + 4 * comp + c, SIDE, stride=8), :] = placed[c]


def open_tile(tile, held):
    for part in range(2):
        for comp in range(2):
            for c in range(4):
                held[part, pl.ds(4 * comp + c, 2 * SIDE, stride=8), :] = tile[
                    part, comp, :, c * HALF : (c + 1) * HALF
                ]


def forward_one(a, b, held, probe, hi, lo):
    ore, oim = patch(held.at[0], 0, a, b), patch(held.at[0], 1, a, b)
    pre, pim = probe[0], probe[1]
    back = travel(pre * ore - pim * oim, pre * oim + pim * ore, hi, lo, False)
    ore, oim = patch(held.at[1], 0, a, b), patch(held.at[1], 1, a, b)
    re, im = back
    return back, to_far(re * ore - im * oim, re * oim + im * ore, hi, lo)


def backward_far(k, valid, hi, lo, shuffle, back, far, arrived, mixed):
    for c in range(2):
        mixed[c] = arrived[k, :, c * HALF : (c + 1) * HALF]
    measured = jnp.concatenate(
        [
            jnp.concatenate([mixed[c, pl.ds(odd, HALF, stride=2), :] for c in range(2)], axis=1)
            for odd in range(2)
        ],
        axis=0,
    )
    mh, ml = parts(measured)
    measured = mm(mh, shuffle[...]) + mm(ml, shuffle[...])
    fre, fim = far[k, 0], far[k, 1]
    scale = valid * (fre * fre + fim * fim - measured)
    gre, gim = from_far(scale * fre, scale * fim, hi, lo)
    bre, bim = back[k, 0], back[k, 1]
    return (gre, gim), (bre * gre + bim * gim, bre * gim - bim * gre)


def backward_near(a, b, gre, gim, held, probe, hi, lo):
    ore, oim = patch(held.at[1], 0, a, b), patch(held.at[1], 1, a, b)
    gre, gim = travel(ore * gre + oim * gim, ore * gim - oim * gre, hi, lo, True)
    pre, pim = probe[0], probe[1]
    first = (pre * gre + pim * gim, pre * gim - pim * gre)
    ore, oim = patch(held.at[0], 0, a, b), patch(held.at[0], 1, a, b)
    return first, (ore * gre + oim * gim, ore * gim - oim * gre)


MESH = pl.DeviceIdType.MESH
CORES = 2
AHEAD = 4


def remote(src, dst, send, recv, device):
    return pltpu.make_async_remote_copy(
        src_ref=src, dst_ref=dst, send_sem=send, recv_sem=recv, device_id=device, device_id_type=MESH
    )


def plane_steps(xs, ys):
    tile = lax.axis_index("tile")
    x, y = tile // ys, tile % ys

    def at_xy(j):
        return {"tile": lax.rem(x + j // ys, xs) * ys + lax.rem(y + j % ys, ys)}

    return tile, at_xy, range(1, xs * ys)


def read_lists(notes, tables_ref):
    count = notes.shape[0]
    note = notes[:, 0, :]
    owner = lax.broadcasted_iota(jnp.int32, note.shape, 1)
    source = lax.broadcasted_iota(jnp.int32, note.shape, 0)
    here = jnp.zeros(note.shape, jnp.int32)
    values = [jnp.zeros(note.shape, jnp.int32) for _ in range(3)]
    for i in range(4):
        hit = jnp.where(jnp.broadcast_to(note[:, i : i + 1], note.shape) == owner, 1, 0)
        here = here + hit
        fields = [4 * source + i] + [
            jnp.broadcast_to(note[:, 4 * f + i : 4 * f + i + 1], note.shape) for f in (1, 2)
        ]
        values = [v + hit * f for v, f in zip(values, fields)]
    lower = (
        lax.broadcasted_iota(jnp.int32, (count, count), 0) > lax.broadcasted_iota(jnp.int32, (count, count), 1)
    ).astype(F32)
    rank = mm(lower.astype(BF16), here.astype(F32).astype(BF16)).astype(jnp.int32)
    for k in range(MAX_READS):
        chosen = here * jnp.where(rank == k, 1, 0)
        for f in range(3):
            row = MAX_READS * f + k
            tables_ref[row : row + 1, :] = jnp.sum(chosen * values[f], axis=0, keepdims=True)
    tables_ref[24:25, :] = jnp.sum(here, axis=0, keepdims=True)


def whole_kernel(
    zs, xs, ys,
    tile_hbm, offset_hbm, owner_hbm, patterns, tile, probe_hbm, hi_hbm, lo_hbm, shuffle_hbm,
    out, probe_out,
    tile_of, offsets, owner_map, opened, probe, hi, lo, shuffle, notes, lists, lists_smem, mid, stage,
    held, arrived, back, far, mixed, padded, grad, probe_grad,
    own, core_in, half_in, direct_in, plane_in, piece_in, piece_z,
    small_sem, load_sem, own_sem, list_sem, note_send, note_recv, first_send, first_recv,
    second_send, second_recv, core_send, core_recv, ring_send, ring_recv,
    probe_send, probe_recv, z_send, z_recv, all_send, all_recv, pair_send, pair_recv,
):
    scan = lax.axis_index("scan")
    z, c = scan // CORES, scan % CORES
    me, at_xy, shifts = plane_steps(xs, ys)
    piece = mid.shape[1]
    reads = patterns.shape[0]
    height = own.shape[2]

    def at_z(step):
        return {"scan": lax.rem(z + step + zs, zs) * CORES + c}

    pair = {"scan": z * CORES + 1 - c}

    def piece_rows(index):
        return pl.ds(pl.multiple_of(index * piece, piece), piece)

    barrier = pltpu.get_barrier_semaphore()
    partners = [pair] + [at_z(step) for step in (1, 2, 3)] + [at_xy(j) for j in shifts]
    for partner in partners:
        pl.semaphore_signal(barrier, inc=1, device_id=partner, device_id_type=MESH)
    smalls = [
        pltpu.make_async_copy(src, dst, small_sem.at[k])
        for k, (src, dst) in enumerate([(tile_hbm, tile_of), (offset_hbm, offsets), (owner_hbm, owner_map)])
    ]
    loads = [
        pltpu.make_async_copy(src, dst, load_sem.at[k])
        for k, (src, dst) in enumerate(
            [(tile, opened), (probe_hbm, probe), (hi_hbm, hi), (lo_hbm, lo), (shuffle_hbm, shuffle)]
        )
    ]
    mine = pltpu.make_async_copy(
        patterns.at[:, piece_rows(me), :], mid.at[pl.ds(reads * me, reads)], own_sem
    )
    for load in smalls + loads + [mine]:
        load.start()
    for load in smalls:
        load.wait()
    lane = lax.broadcasted_iota(jnp.int32, (1, HALF), 1)
    note = jnp.zeros((1, HALF), jnp.int32)
    for i in range(reads):
        for f, value in enumerate((owner_map[tile_of[i]], offsets[0, i], offsets[1, i])):
            note = jnp.where(lane == 4 * f + i, value, note)
    notes[me] = note
    pl.semaphore_wait(barrier, len(partners))

    tells = [
        remote(notes.at[me], notes.at[me], note_send.at[j], note_recv.at[j], at_xy(j)) for j in shifts
    ]
    firsts = [
        remote(
            patterns.at[:, piece_rows(at_xy(j)["tile"]), :], mid.at[pl.ds(reads * me, reads)],
            first_send.at[j], first_recv.at[j], at_xy(j),
        )
        for j in shifts
    ]
    for copy in tells + firsts:
        copy.start()
    probe_grad[...] = jnp.zeros_like(probe_grad)
    grad[...] = jnp.zeros_like(grad)
    border = jnp.zeros((2, 8 * SIDE, HALF), F32)
    padded[:, : 8 * SIDE, :] = border
    padded[:, 16 * SIDE :, :] = border
    loads[0].wait()
    open_tile(opened.at[0], held)
    for copy in tells:
        copy.wait_recv()
    lists[...] = jnp.zeros_like(lists)
    read_lists(notes, lists)
    listed = pltpu.make_async_copy(lists, lists_smem, list_sem)
    listed.start()
    listed.wait()
    for load in loads[1:]:
        load.wait()

    def where(k):
        return lists_smem[MAX_READS + k, me], lists_smem[2 * MAX_READS + k, me]

    def run_forward(k, carry):
        a, b = where(k)
        (bre, bim), (fre, fim) = forward_one(a, b, held, probe, hi, lo)
        back[k, 0], back[k, 1], far[k, 0], far[k, 1] = bre, bim, fre, fim
        return carry

    lax.fori_loop(0, AHEAD, run_forward, 0)
    mine.wait()
    for copy in firsts:
        copy.wait_recv()

    def second(k, j):
        return remote(
            stage.at[j, k], arrived.at[k, piece_rows(me), :],
            second_send.at[k, j], second_recv.at[k, j], at_xy(j),
        )

    def send_rank(k, carry):
        for j in shifts:
            stage[j, k] = mid[lists_smem[k, at_xy(j)["tile"]]]
            second(k, j).start()
        arrived[k, piece_rows(me), :] = mid[lists_smem[k, me]]
        return carry

    lax.fori_loop(0, MAX_READS, send_rank, 0)
    lax.fori_loop(AHEAD, MAX_READS, run_forward, 0)

    def add_parts(a, b, values):
        for part, pair_of in values.items():
            for comp in range(2):
                place(padded.at[part], comp, b, pair_of[comp])
        lines = 512

        def add(i, inner):
            to = pl.ds(pl.multiple_of(i * lines, 8), lines)
            source = pl.ds((SIDE - a + i * (lines // 8)) * 8, lines)
            for part in values:
                grad[part, to, :] = grad[part, to, :] + padded[part, source, :]
            return inner

        lax.fori_loop(0, 8 * 2 * SIDE // lines, add, 0)

    def far_side(k):
        valid = jnp.where(k < lists_smem[24, me], 2.0, 0.0)
        for j in shifts:
            second(k, j).wait_recv()
        return backward_far(k, valid, hi, lo, shuffle, back, far, arrived, mixed)

    def near_side(k, wave):
        a, b = where(k)
        slice0, probe_term = backward_near(a, b, *wave, held, probe, hi, lo)
        probe_grad[0] += probe_term[0]
        probe_grad[1] += probe_term[1]
        return slice0

    def run_backward(k, carry):
        wave, slice1 = far_side(k)
        slice0 = near_side(k, wave)
        add_parts(*where(k), {0: slice0, 1: slice1})
        return carry

    lax.fori_loop(0, MAX_READS - 1, run_backward, 0)

    steps = [2, 1, -1, 0]

    def rows_of(step, core):
        return pl.ds(pl.multiple_of((lax.rem(z + step + zs, zs) * CORES + core) * height, height), height)

    started = []

    def go(copy):
        copy.start()
        started.append(copy)
        return copy

    up_rows, down_rows = pl.ds(0, height // 2), pl.ds(height // 2, height // 2)

    def core_copy(k, p):
        return go(remote(grad.at[p, rows_of(steps[k], 1 - c), :], core_in.at[k, p], core_send.at[k, p], core_recv.at[k, p], pair))

    def merge(copy, k, p):
        copy.wait_recv()
        own[k, p] = grad[p, rows_of(steps[k], c), :] + core_in[k, p]

    def hop(src, dst, kind, p, way):
        return go(remote(src, dst, ring_send.at[kind, p, way], ring_recv.at[kind, p, way], at_z(1 - 2 * way)))

    def farthest(p):
        return [
            hop(own.at[0, p, up_rows], half_in.at[p, 0], 0, p, 0),
            hop(own.at[0, p, down_rows], half_in.at[p, 1], 0, p, 1),
        ]

    def straight(p):
        return [
            hop(own.at[1, p, down_rows], direct_in.at[p, 0], 1, p, 0),
            hop(own.at[2, p, up_rows], direct_in.at[p, 1], 1, p, 1),
        ]

    def summed(p, halves):
        halves[0].wait_recv()
        own[1, p, up_rows] = own[1, p, up_rows] + half_in[p, 0]
        first = hop(own.at[1, p, up_rows], direct_in.at[p, 2], 2, p, 0)
        halves[1].wait_recv()
        own[2, p, down_rows] = own[2, p, down_rows] + half_in[p, 1]
        return [first, hop(own.at[2, p, down_rows], direct_in.at[p, 3], 2, p, 1)]

    final = MAX_READS - 1
    wave, slice1 = far_side(final)
    add_parts(*where(final), {1: slice1})
    cores1 = [core_copy(k, 1) for k in range(4)]
    slice0 = near_side(final, wave)
    probe_pair = go(remote(probe_grad.at[1 - c], plane_in, pair_send.at[0], pair_recv.at[0], pair))
    for k in range(3):
        merge(cores1[k], k, 1)
        if k == 0:
            halves1 = farthest(1)
    waits = straight(1)
    probe_pair.wait_recv()
    plane_in[...] = plane_in[...] + probe_grad[c]
    gathers = [
        go(remote(plane_in.at[piece_rows(at_xy(j)["tile"])], piece_in.at[j], probe_send.at[j], probe_recv.at[j], at_xy(j)))
        for j in shifts
    ]
    add_parts(*where(final), {0: slice0})
    cores0 = [core_copy(k, 0) for k in range(4)]
    merge(cores0[0], 0, 0)
    halves0 = farthest(0)
    for k in range(1, 4):
        merge(cores0[k], k, 0)
    merge(cores1[3], 3, 1)
    total = plane_in[piece_rows(me), :]
    for copy, j in zip(gathers, shifts):
        copy.wait_recv()
        total = total + piece_in[j]
    piece_z[0] = total
    across = [go(remote(piece_z.at[0], piece_z.at[k], z_send.at[k], z_recv.at[k], at_z(k))) for k in (1, 2, 3)]
    waits += summed(1, halves1)
    waits += straight(0)
    waits += summed(0, halves0)
    for copy in across:
        copy.wait_recv()
    probe_out[c, piece_rows(me), :] = (piece_z[0] + piece_z[1]) + (piece_z[2] + piece_z[3])
    spreads = [
        go(remote(probe_out.at[c, piece_rows(me)], probe_out.at[c, piece_rows(me)], all_send.at[j], all_recv.at[j], at_xy(j)))
        for j in shifts
    ]
    for copy in spreads:
        copy.wait_recv()
    last = go(remote(probe_out.at[c], probe_out.at[c], pair_send.at[1], pair_recv.at[1], pair))
    for copy in waits:
        copy.wait_recv()
    for p in range(2):
        own[3, p, up_rows] = own[3, p, up_rows] + (direct_in[p, 2] + direct_in[p, 1])
        own[3, p, down_rows] = own[3, p, down_rows] + (direct_in[p, 0] + direct_in[p, 3])
    lines = out.shape[3]
    for plane in range(4):
        for k in range(4):
            out[0, plane // 2, plane % 2, :, k * HALF : (k + 1) * HALF] = own[
                3, plane // 2, pl.ds(4 * (plane % 2) + k, lines, stride=8), :
            ]
    last.wait_recv()
    for copy in tells + firsts + started:
        copy.wait_send()

    def sent(k, carry):
        for j in shifts:
            second(k, j).wait_send()
        return carry

    lax.fori_loop(0, MAX_READS, sent, 0)


def whole(zs, xs, ys, *operands):
    tile_of, offsets, owner_map, patterns, tile, probe, hi, lo, shuffle = operands
    tiles = xs * ys
    piece = SIDE // tiles
    reads = patterns.shape[0]
    lines = 2 * SIDE // (zs * CORES)
    height = 8 * lines
    dma = pltpu.SemaphoreType.DMA

    def vmem(*shape):
        return pltpu.VMEM(shape, F32)

    return pl.pallas_call(
        functools.partial(whole_kernel, zs, xs, ys),
        out_shape=(
            jax.ShapeDtypeStruct((1, 2, 2, lines, 2 * SIDE), F32),
            jax.ShapeDtypeStruct(probe.shape, F32),
        ),
        in_specs=[pl.BlockSpec(memory_space=pltpu.HBM)] * len(operands),
        out_specs=(pl.BlockSpec(memory_space=pltpu.VMEM),) * 2,
        scratch_shapes=[
            pltpu.SMEM(tile_of.shape, jnp.int32),
            pltpu.SMEM(offsets.shape, jnp.int32),
            pltpu.SMEM(owner_map.shape, jnp.int32),
            vmem(*tile.shape),
            vmem(*probe.shape),
            pltpu.VMEM(hi.shape, BF16),
            pltpu.VMEM(lo.shape, BF16),
            pltpu.VMEM(shuffle.shape, BF16),
            pltpu.VMEM((tiles, 1, HALF), jnp.int32),
            pltpu.VMEM((32, HALF), jnp.int32),
            pltpu.SMEM((32, HALF), jnp.int32),
            vmem(tiles * reads, piece, SIDE),
            vmem(tiles, MAX_READS, piece, SIDE),
            vmem(2, 8 * 2 * SIDE, HALF),
            vmem(MAX_READS, SIDE, SIDE),
            vmem(MAX_READS, 2, SIDE, SIDE),
            vmem(MAX_READS, 2, SIDE, SIDE),
            vmem(2, SIDE, HALF),
            vmem(2, 8 * 3 * SIDE, HALF),
            vmem(2, 8 * 2 * SIDE, HALF),
            vmem(2, SIDE, SIDE),
            vmem(4, 2, height, HALF),
            vmem(4, 2, height, HALF),
            vmem(2, 2, height // 2, HALF),
            vmem(2, 4, height // 2, HALF),
            vmem(SIDE, SIDE),
            vmem(tiles, piece, SIDE),
            vmem(4, piece, SIDE),
            dma((3,)), dma((5,)), dma, dma, dma((tiles,)), dma((tiles,)), dma((tiles,)), dma((tiles,)),
            dma((MAX_READS, tiles)), dma((MAX_READS, tiles)), dma((4, 2)), dma((4, 2)),
            dma((3, 2, 2)), dma((3, 2, 2)), dma((tiles,)), dma((tiles,)), dma((4,)), dma((4,)),
            dma((tiles,)), dma((tiles,)), dma((2,)), dma((2,)),
        ],
        cost_estimate=pl.CostEstimate(
            flops=MAX_READS * 50 * 2 * SIDE**3, bytes_accessed=10 << 20, transcendentals=0
        ),
        compiler_params=pltpu.CompilerParams(
            collective_id=0, has_side_effects=True, vmem_limit_bytes=46 << 20
        ),
    )(*(pltpu.with_memory_space_constraint(x, pltpu.HBM) for x in operands))


def close_kernel(scale, object_in, probe_in, object_out, probe_out):
    object_out[...] = object_in[...]
    probe_out[...] = probe_in[...] * scale


def close(scale, object_part, probe_total):
    vmem = pl.BlockSpec(memory_space=pltpu.VMEM)
    return pl.pallas_call(
        functools.partial(close_kernel, scale),
        out_shape=tuple(jax.ShapeDtypeStruct(x.shape, F32) for x in (object_part, probe_total)),
        in_specs=[vmem, vmem],
        out_specs=(vmem, vmem),
        compiler_params=pltpu.CompilerParams(vmem_limit_bytes=4 << 20),
    )(object_part, probe_total)


def per_device(object_tiles, probe_wave, patterns, tile_of, offsets, owner_map):
    tile_count = lax.axis_size("tile")
    high, low, shuffle = (jnp.asarray(table) for table in tables())
    zs, xs = lax.axis_size("scan") // CORES, math.isqrt(tile_count)
    ys = tile_count // xs
    object_part, probe_total = whole(
        zs, xs, ys,
        tile_of, offsets.T, owner_map, patterns, object_tiles, probe_wave, high, low, shuffle,
    )
    count = tile_count * lax.axis_size("scan") * patterns.shape[0]
    return close(1.0 / math.sqrt(count), object_part, probe_total)


def solution(mesh):
    return jax.shard_map(
        per_device,
        mesh=mesh,
        in_specs=(
            P("tile", None, None, None, None),
            P(),
            P(("scan", "tile"), None, None),
            P(("scan", "tile")),
            P(("scan", "tile"), None),
            P(),
        ),
        out_specs=(P("tile", None, None, "scan", None), P()),
        check_vma=False,
    )
```

```python
import functools
import math

import jax
import jax.numpy as jnp
import ml_dtypes
import numpy as np
from jax import lax
from jax.experimental import pallas as pl
from jax.experimental.pallas import tpu as pltpu
from jax.sharding import PartitionSpec as P

PROP_PHASE = 0.75
SIDE = 256
HALF = 128
MAX_READS = 8
F32 = jnp.float32
BF16 = jnp.bfloat16


def embed(block):
    return np.block([[block.real, block.imag], [-block.imag, block.real]])


@functools.cache
def tables():
    index = np.arange(SIDE)
    freq = np.where(index < HALF, index, index - SIDE).astype(np.float64)
    wave = np.exp(-2j * math.pi * (index[:, None] * index[None, :] % SIDE) / SIDE) / math.sqrt(SIDE)
    step = np.exp(-1j * PROP_PHASE * freq**2 / SIDE)
    travel = wave.conj() @ (step[:, None] * wave)
    plus = (travel[:HALF, :HALF] + travel[:HALF, HALF:]) / 2
    minus = (travel[:HALF, :HALF] - travel[:HALF, HALF:]) / 2
    forms = []
    for block in (plus, minus, wave[:HALF, 0::2], wave[:HALF, 1::2]):
        form = embed(block)
        forms += [form, form.T]
    forms = np.stack(forms)
    high = forms.astype(ml_dtypes.bfloat16)
    low = (forms - high.astype(np.float64)).astype(ml_dtypes.bfloat16)
    shuffle = np.zeros((SIDE, SIDE), ml_dtypes.bfloat16)
    shuffle[2 * np.arange(HALF), np.arange(HALF)] = 1
    shuffle[2 * np.arange(HALF) + 1, HALF + np.arange(HALF)] = 1
    return high, low, shuffle


A_PLUS, A_MINUS, F_EVEN, F_ODD = 0, 2, 4, 6


def parts(x):
    high = x.astype(BF16)
    return high, (x - high.astype(F32)).astype(BF16)


def mm(x, y):
    return jnp.dot(x, y, preferred_element_type=F32)


def right(x, high_ref, low_ref, which):
    xh, xl = parts(x)
    wh, wl = high_ref[which], low_ref[which]
    total = mm(xh, wh)
    total = total + mm(xl, wh)
    return total + mm(xh, wl)


def left(x, high_ref, low_ref, which):
    xh, xl = parts(x)
    wh, wl = high_ref[which], low_ref[which]
    total = mm(wh, xh)
    total = total + mm(wl, xh)
    return total + mm(wh, xl)


def cols(re, im):
    return (
        jnp.concatenate([re[:, :HALF] + re[:, HALF:], im[:, :HALF] + im[:, HALF:]], axis=1),
        jnp.concatenate([re[:, :HALF] - re[:, HALF:], im[:, :HALF] - im[:, HALF:]], axis=1),
    )


def rows(re, im):
    return (
        jnp.concatenate([re[:HALF] + re[HALF:], im[:HALF] + im[HALF:]], axis=0),
        jnp.concatenate([re[:HALF] - re[HALF:], im[:HALF] - im[HALF:]], axis=0),
    )


def split_cols(p, q):
    return (
        jnp.concatenate([p[:, :HALF], q[:, :HALF]], axis=1),
        jnp.concatenate([p[:, HALF:], q[:, HALF:]], axis=1),
    )


def split_rows(p, q):
    return (
        jnp.concatenate([p[:HALF], q[:HALF]], axis=0),
        jnp.concatenate([p[HALF:], q[HALF:]], axis=0),
    )


def travel(re, im, hi, lo, conj):
    flip = 1 if conj else 0
    s, d = cols(re, im)
    p, q = right(s, hi, lo, A_PLUS + flip), right(d, hi, lo, A_MINUS + flip)
    re, im = split_cols(p + q, p - q)
    s, d = rows(re, im)
    p, q = left(s, hi, lo, A_PLUS + 1 - flip), left(d, hi, lo, A_MINUS + 1 - flip)
    return split_rows(p + q, p - q)


def to_far(re, im, hi, lo):
    s, d = cols(re, im)
    re, im = split_cols(right(s, hi, lo, F_EVEN), right(d, hi, lo, F_ODD))
    s, d = rows(re, im)
    return split_rows(left(s, hi, lo, F_EVEN + 1), left(d, hi, lo, F_ODD + 1))


def from_far(re, im, hi, lo):
    even, odd = (
        jnp.concatenate([re[:, :HALF], im[:, :HALF]], axis=1),
        jnp.concatenate([re[:, HALF:], im[:, HALF:]], axis=1),
    )
    p, q = right(even, hi, lo, F_EVEN + 1), right(odd, hi, lo, F_ODD + 1)
    re, im = split_cols(p + q, p - q)
    even, odd = (
        jnp.concatenate([re[:HALF], im[:HALF]], axis=0),
        jnp.concatenate([re[HALF:], im[HALF:]], axis=0),
    )
    p, q = left(even, hi, lo, F_EVEN), left(odd, hi, lo, F_ODD)
    return split_rows(p + q, p - q)


def lane_mask(shift):
    return lax.broadcasted_iota(jnp.int32, (SIDE, HALF), 1) < shift


def patch(rows_ref, comp, a, b):
    base, shift = b // HALF, b % HALF
    back = lax.rem(HALF - shift, HALF)
    tiles = [
        pltpu.roll(
            rows_ref[pl.ds(8 * a + 4 * comp + jnp.minimum(base + k, 3), SIDE, stride=8), :], back, 1
        )
        for k in range(3)
    ]
    mask = lane_mask(HALF - shift)
    return jnp.concatenate(
        [jnp.where(mask, tiles[0], tiles[1]), jnp.where(mask, tiles[1], tiles[2])], axis=1
    )


def place(padded, comp, b, value):
    base, shift = b // HALF, b % HALF
    first, second = pltpu.roll(value[:, :HALF], shift, 1), pltpu.roll(value[:, HALF:], shift, 1)
    mask = lane_mask(shift)
    zero = jnp.zeros_like(first)
    u0, u1, u2 = (
        jnp.where(mask, zero, first), jnp.where(mask, first, second), jnp.where(mask, second, zero)
    )
    at0, below2 = lane_mask(HALF * (1 - base)), lane_mask(HALF * (2 - base))
    placed = (
        jnp.where(at0, u0, zero),
        jnp.where(at0, u1, jnp.where(below2, u0, zero)),
        jnp.where(at0, u2, jnp.where(below2, u1, u0)),
        jnp.where(at0, zero, jnp.where(below2, u2, u1)),
    )
    for c in range(4):
        padded[pl.ds(8 * SIDE + 4 * comp + c, SIDE, stride=8), :] = placed[c]


def open_tile(tile, held):
    for part in range(2):
        for comp in range(2):
            for c in range(4):
                held[part, pl.ds(4 * comp + c, 2 * SIDE, stride=8), :] = tile[
                    part, comp, :, c * HALF : (c + 1) * HALF
                ]


def forward_one(a, b, held, probe, hi, lo):
    ore, oim = patch(held.at[0], 0, a, b), patch(held.at[0], 1, a, b)
    pre, pim = probe[0], probe[1]
    back = travel(pre * ore - pim * oim, pre * oim + pim * ore, hi, lo, False)
    ore, oim = patch(held.at[1], 0, a, b), patch(held.at[1], 1, a, b)
    re, im = back
    return back, to_far(re * ore - im * oim, re * oim + im * ore, hi, lo)


def backward_far(k, valid, hi, lo, shuffle, back, far, arrived, mixed):
    for c in range(2):
        mixed[c] = arrived[k, :, c * HALF : (c + 1) * HALF]
    measured = jnp.concatenate(
        [
            jnp.concatenate([mixed[c, pl.ds(odd, HALF, stride=2), :] for c in range(2)], axis=1)
            for odd in range(2)
        ],
        axis=0,
    )
    mh, ml = parts(measured)
    measured = mm(mh, shuffle[...]) + mm(ml, shuffle[...])
    fre, fim = far[k, 0], far[k, 1]
    scale = valid * (fre * fre + fim * fim - measured)
    gre, gim = from_far(scale * fre, scale * fim, hi, lo)
    bre, bim = back[k, 0], back[k, 1]
    return (gre, gim), (bre * gre + bim * gim, bre * gim - bim * gre)


def backward_near(a, b, gre, gim, held, probe, hi, lo):
    ore, oim = patch(held.at[1], 0, a, b), patch(held.at[1], 1, a, b)
    gre, gim = travel(ore * gre + oim * gim, ore * gim - oim * gre, hi, lo, True)
    pre, pim = probe[0], probe[1]
    first = (pre * gre + pim * gim, pre * gim - pim * gre)
    ore, oim = patch(held.at[0], 0, a, b), patch(held.at[0], 1, a, b)
    return first, (ore * gre + oim * gim, ore * gim - oim * gre)


MESH = pl.DeviceIdType.MESH
CORES = 2
AHEAD = 4


def remote(src, dst, send, recv, device):
    return pltpu.make_async_remote_copy(
        src_ref=src, dst_ref=dst, send_sem=send, recv_sem=recv, device_id=device, device_id_type=MESH
    )


def plane_steps(xs, ys):
    tile = lax.axis_index("tile")
    x, y = tile // ys, tile % ys

    def at_xy(j):
        return {"tile": lax.rem(x + j // ys, xs) * ys + lax.rem(y + j % ys, ys)}

    def hops(j):
        dx, dy = j // ys, j % ys
        return min(dx, xs - dx) + min(dy, ys - dy)

    return tile, at_xy, sorted(range(1, xs * ys), key=lambda j: -hops(j))


def read_lists(notes, tables_ref):
    count = notes.shape[0]
    note = notes[:, 0, :]
    owner = lax.broadcasted_iota(jnp.int32, note.shape, 1)
    source = lax.broadcasted_iota(jnp.int32, note.shape, 0)
    here = jnp.zeros(note.shape, jnp.int32)
    values = [jnp.zeros(note.shape, jnp.int32) for _ in range(3)]
    for i in range(4):
        hit = jnp.where(jnp.broadcast_to(note[:, i : i + 1], note.shape) == owner, 1, 0)
        here = here + hit
        fields = [4 * source + i] + [
            jnp.broadcast_to(note[:, 4 * f + i : 4 * f + i + 1], note.shape) for f in (1, 2)
        ]
        values = [v + hit * f for v, f in zip(values, fields)]
    lower = (
        lax.broadcasted_iota(jnp.int32, (count, count), 0) > lax.broadcasted_iota(jnp.int32, (count, count), 1)
    ).astype(F32)
    rank = mm(lower.astype(BF16), here.astype(F32).astype(BF16)).astype(jnp.int32)
    for k in range(MAX_READS):
        chosen = here * jnp.where(rank == k, 1, 0)
        for f in range(3):
            row = MAX_READS * f + k
            tables_ref[row : row + 1, :] = jnp.sum(chosen * values[f], axis=0, keepdims=True)
    tables_ref[24:25, :] = jnp.sum(here, axis=0, keepdims=True)


def whole_kernel(
    zs, xs, ys,
    tile_hbm, offset_hbm, owner_hbm, patterns, tile, probe_hbm, hi_hbm, lo_hbm, shuffle_hbm,
    out, probe_out,
    tile_of, offsets, owner_map, opened, probe, hi, lo, shuffle, notes, lists, lists_smem, mid, stage,
    held, arrived, back, far, mixed, padded, grad, probe_grad,
    own, core_in, half_in, direct_in, plane_in, piece_in, piece_z,
    small_sem, load_sem, own_sem, list_sem, note_send, note_recv, first_send, first_recv,
    second_send, second_recv, core_send, core_recv, ring_send, ring_recv,
    probe_send, probe_recv, z_send, z_recv, all_send, all_recv, pair_send, pair_recv,
):
    scan = lax.axis_index("scan")
    z, c = scan // CORES, scan % CORES
    me, at_xy, shifts = plane_steps(xs, ys)
    piece = mid.shape[1]
    reads = patterns.shape[0]
    height = own.shape[2]

    def at_z(step):
        return {"scan": lax.rem(z + step + zs, zs) * CORES + c}

    pair = {"scan": z * CORES + 1 - c}

    def piece_rows(index):
        return pl.ds(pl.multiple_of(index * piece, piece), piece)

    barrier = pltpu.get_barrier_semaphore()
    partners = [pair] + [at_z(step) for step in (1, 2, 3)] + [at_xy(j) for j in shifts]
    for partner in partners:
        pl.semaphore_signal(barrier, inc=1, device_id=partner, device_id_type=MESH)
    smalls = [
        pltpu.make_async_copy(src, dst, small_sem.at[k])
        for k, (src, dst) in enumerate([(tile_hbm, tile_of), (offset_hbm, offsets), (owner_hbm, owner_map)])
    ]
    loads = [
        pltpu.make_async_copy(src, dst, load_sem.at[k])
        for k, (src, dst) in enumerate(
            [(tile, opened), (probe_hbm, probe), (hi_hbm, hi), (lo_hbm, lo), (shuffle_hbm, shuffle)]
        )
    ]
    mine = pltpu.make_async_copy(
        patterns.at[:, piece_rows(me), :], mid.at[pl.ds(reads * me, reads)], own_sem
    )
    for load in smalls + loads + [mine]:
        load.start()
    for load in smalls:
        load.wait()
    lane = lax.broadcasted_iota(jnp.int32, (1, HALF), 1)
    note = jnp.zeros((1, HALF), jnp.int32)
    for i in range(reads):
        for f, value in enumerate((owner_map[tile_of[i]], offsets[0, i], offsets[1, i])):
            note = jnp.where(lane == 4 * f + i, value, note)
    notes[me] = note
    pl.semaphore_wait(barrier, len(partners))

    tells = [
        remote(notes.at[me], notes.at[me], note_send.at[j], note_recv.at[j], at_xy(j)) for j in shifts
    ]
    firsts = [
        remote(
            patterns.at[:, piece_rows(at_xy(j)["tile"]), :], mid.at[pl.ds(reads * me, reads)],
            first_send.at[j], first_recv.at[j], at_xy(j),
        )
        for j in shifts
    ]
    for copy in tells + firsts:
        copy.start()
    probe_grad[...] = jnp.zeros_like(probe_grad)
    grad[...] = jnp.zeros_like(grad)
    border = jnp.zeros((2, 8 * SIDE, HALF), F32)
    padded[:, : 8 * SIDE, :] = border
    padded[:, 16 * SIDE :, :] = border
    loads[0].wait()
    open_tile(opened.at[0], held)
    for copy in tells:
        copy.wait_recv()
    lists[...] = jnp.zeros_like(lists)
    read_lists(notes, lists)
    listed = pltpu.make_async_copy(lists, lists_smem, list_sem)
    listed.start()
    listed.wait()
    for load in loads[1:]:
        load.wait()

    def where(k):
        return lists_smem[MAX_READS + k, me], lists_smem[2 * MAX_READS + k, me]

    def run_forward(k, carry):
        a, b = where(k)
        (bre, bim), (fre, fim) = forward_one(a, b, held, probe, hi, lo)
        back[k, 0], back[k, 1], far[k, 0], far[k, 1] = bre, bim, fre, fim
        return carry

    lax.fori_loop(0, AHEAD, run_forward, 0)
    mine.wait()
    for copy in firsts:
        copy.wait_recv()

    def second(k, j):
        return remote(
            stage.at[j, k], arrived.at[k, piece_rows(me), :],
            second_send.at[k, j], second_recv.at[k, j], at_xy(j),
        )

    def send_rank(k, carry):
        for j in shifts:
            stage[j, k] = mid[lists_smem[k, at_xy(j)["tile"]]]
            second(k, j).start()
        arrived[k, piece_rows(me), :] = mid[lists_smem[k, me]]
        return carry

    lax.fori_loop(0, MAX_READS, send_rank, 0)
    lax.fori_loop(AHEAD, MAX_READS, run_forward, 0)

    def add_parts(a, b, values):
        for part, pair_of in values.items():
            for comp in range(2):
                place(padded.at[part], comp, b, pair_of[comp])
        lines = 512

        def add(i, inner):
            to = pl.ds(pl.multiple_of(i * lines, 8), lines)
            source = pl.ds((SIDE - a + i * (lines // 8)) * 8, lines)
            for part in values:
                grad[part, to, :] = grad[part, to, :] + padded[part, source, :]
            return inner

        lax.fori_loop(0, 8 * 2 * SIDE // lines, add, 0)

    def far_side(k):
        valid = jnp.where(k < lists_smem[24, me], 2.0, 0.0)
        for j in shifts:
            second(k, j).wait_recv()
        return backward_far(k, valid, hi, lo, shuffle, back, far, arrived, mixed)

    def near_side(k, wave):
        a, b = where(k)
        slice0, probe_term = backward_near(a, b, *wave, held, probe, hi, lo)
        probe_grad[0] += probe_term[0]
        probe_grad[1] += probe_term[1]
        return slice0

    def run_backward(k, carry):
        wave, slice1 = far_side(k)
        slice0 = near_side(k, wave)
        add_parts(*where(k), {0: slice0, 1: slice1})
        return carry

    lax.fori_loop(0, MAX_READS - 1, run_backward, 0)

    steps = [2, 1, -1, 0]

    def rows_of(step, core):
        return pl.ds(pl.multiple_of((lax.rem(z + step + zs, zs) * CORES + core) * height, height), height)

    started = []

    def go(copy):
        copy.start()
        started.append(copy)
        return copy

    up_rows, down_rows = pl.ds(0, height // 2), pl.ds(height // 2, height // 2)

    def core_copy(k, p):
        return go(remote(grad.at[p, rows_of(steps[k], 1 - c), :], core_in.at[k, p], core_send.at[k, p], core_recv.at[k, p], pair))

    def merge(copy, k, p):
        copy.wait_recv()
        own[k, p] = grad[p, rows_of(steps[k], c), :] + core_in[k, p]

    def hop(src, dst, kind, p, way):
        return go(remote(src, dst, ring_send.at[kind, p, way], ring_recv.at[kind, p, way], at_z(1 - 2 * way)))

    def farthest(p):
        return [
            hop(own.at[0, p, up_rows], half_in.at[p, 0], 0, p, 0),
            hop(own.at[0, p, down_rows], half_in.at[p, 1], 0, p, 1),
        ]

    def straight(p):
        return [
            hop(own.at[1, p, down_rows], direct_in.at[p, 0], 1, p, 0),
            hop(own.at[2, p, up_rows], direct_in.at[p, 1], 1, p, 1),
        ]

    def summed(p, halves):
        halves[0].wait_recv()
        own[1, p, up_rows] = own[1, p, up_rows] + half_in[p, 0]
        first = hop(own.at[1, p, up_rows], direct_in.at[p, 2], 2, p, 0)
        halves[1].wait_recv()
        own[2, p, down_rows] = own[2, p, down_rows] + half_in[p, 1]
        return [first, hop(own.at[2, p, down_rows], direct_in.at[p, 3], 2, p, 1)]

    final = MAX_READS - 1
    wave, slice1 = far_side(final)
    add_parts(*where(final), {1: slice1})
    cores1 = [core_copy(k, 1) for k in range(4)]
    slice0 = near_side(final, wave)
    probe_pair = go(remote(probe_grad.at[1 - c], plane_in, pair_send.at[0], pair_recv.at[0], pair))
    for k in range(3):
        merge(cores1[k], k, 1)
        if k == 0:
            halves1 = farthest(1)
    waits = straight(1)
    probe_pair.wait_recv()
    plane_in[...] = plane_in[...] + probe_grad[c]
    gathers = [
        go(remote(plane_in.at[piece_rows(at_xy(j)["tile"])], piece_in.at[j], probe_send.at[j], probe_recv.at[j], at_xy(j)))
        for j in shifts
    ]
    add_parts(*where(final), {0: slice0})
    cores0 = [core_copy(k, 0) for k in range(4)]
    merge(cores0[0], 0, 0)
    halves0 = farthest(0)
    for k in range(1, 4):
        merge(cores0[k], k, 0)
    merge(cores1[3], 3, 1)
    total = plane_in[piece_rows(me), :]
    for copy, j in zip(gathers, shifts):
        copy.wait_recv()
        total = total + piece_in[j]
    piece_z[0] = total
    across = [go(remote(piece_z.at[0], piece_z.at[k], z_send.at[k], z_recv.at[k], at_z(k))) for k in (1, 2, 3)]
    waits += summed(1, halves1)
    waits += straight(0)
    waits += summed(0, halves0)
    for copy in across:
        copy.wait_recv()
    probe_out[c, piece_rows(me), :] = (piece_z[0] + piece_z[1]) + (piece_z[2] + piece_z[3])
    spreads = [
        go(remote(probe_out.at[c, piece_rows(me)], probe_out.at[c, piece_rows(me)], all_send.at[j], all_recv.at[j], at_xy(j)))
        for j in shifts
    ]
    for copy in spreads:
        copy.wait_recv()
    last = go(remote(probe_out.at[c], probe_out.at[c], pair_send.at[1], pair_recv.at[1], pair))
    for copy in waits:
        copy.wait_recv()
    for p in range(2):
        own[3, p, up_rows] = own[3, p, up_rows] + (direct_in[p, 2] + direct_in[p, 1])
        own[3, p, down_rows] = own[3, p, down_rows] + (direct_in[p, 0] + direct_in[p, 3])
    lines = out.shape[3]
    for plane in range(4):
        for k in range(4):
            out[0, plane // 2, plane % 2, :, k * HALF : (k + 1) * HALF] = own[
                3, plane // 2, pl.ds(4 * (plane % 2) + k, lines, stride=8), :
            ]
    last.wait_recv()
    for copy in tells + firsts + started:
        copy.wait_send()

    def sent(k, carry):
        for j in shifts:
            second(k, j).wait_send()
        return carry

    lax.fori_loop(0, MAX_READS, sent, 0)


def whole(zs, xs, ys, *operands):
    tile_of, offsets, owner_map, patterns, tile, probe, hi, lo, shuffle = operands
    tiles = xs * ys
    piece = SIDE // tiles
    reads = patterns.shape[0]
    lines = 2 * SIDE // (zs * CORES)
    height = 8 * lines
    dma = pltpu.SemaphoreType.DMA

    def vmem(*shape):
        return pltpu.VMEM(shape, F32)

    return pl.pallas_call(
        functools.partial(whole_kernel, zs, xs, ys),
        out_shape=(
            jax.ShapeDtypeStruct((1, 2, 2, lines, 2 * SIDE), F32),
            jax.ShapeDtypeStruct(probe.shape, F32),
        ),
        in_specs=[pl.BlockSpec(memory_space=pltpu.HBM)] * len(operands),
        out_specs=(pl.BlockSpec(memory_space=pltpu.VMEM),) * 2,
        scratch_shapes=[
            pltpu.SMEM(tile_of.shape, jnp.int32),
            pltpu.SMEM(offsets.shape, jnp.int32),
            pltpu.SMEM(owner_map.shape, jnp.int32),
            vmem(*tile.shape),
            vmem(*probe.shape),
            pltpu.VMEM(hi.shape, BF16),
            pltpu.VMEM(lo.shape, BF16),
            pltpu.VMEM(shuffle.shape, BF16),
            pltpu.VMEM((tiles, 1, HALF), jnp.int32),
            pltpu.VMEM((32, HALF), jnp.int32),
            pltpu.SMEM((32, HALF), jnp.int32),
            vmem(tiles * reads, piece, SIDE),
            vmem(tiles, MAX_READS, piece, SIDE),
            vmem(2, 8 * 2 * SIDE, HALF),
            vmem(MAX_READS, SIDE, SIDE),
            vmem(MAX_READS, 2, SIDE, SIDE),
            vmem(MAX_READS, 2, SIDE, SIDE),
            vmem(2, SIDE, HALF),
            vmem(2, 8 * 3 * SIDE, HALF),
            vmem(2, 8 * 2 * SIDE, HALF),
            vmem(2, SIDE, SIDE),
            vmem(4, 2, height, HALF),
            vmem(4, 2, height, HALF),
            vmem(2, 2, height // 2, HALF),
            vmem(2, 4, height // 2, HALF),
            vmem(SIDE, SIDE),
            vmem(tiles, piece, SIDE),
            vmem(4, piece, SIDE),
            dma((3,)), dma((5,)), dma, dma, dma((tiles,)), dma((tiles,)), dma((tiles,)), dma((tiles,)),
            dma((MAX_READS, tiles)), dma((MAX_READS, tiles)), dma((4, 2)), dma((4, 2)),
            dma((3, 2, 2)), dma((3, 2, 2)), dma((tiles,)), dma((tiles,)), dma((4,)), dma((4,)),
            dma((tiles,)), dma((tiles,)), dma((2,)), dma((2,)),
        ],
        cost_estimate=pl.CostEstimate(
            flops=MAX_READS * 50 * 2 * SIDE**3, bytes_accessed=10 << 20, transcendentals=0
        ),
        compiler_params=pltpu.CompilerParams(
            collective_id=0, has_side_effects=True, vmem_limit_bytes=46 << 20
        ),
    )(*(pltpu.with_memory_space_constraint(x, pltpu.HBM) for x in operands))


def close_kernel(scale, object_in, probe_in, object_out, probe_out):
    object_out[...] = object_in[...]
    probe_out[...] = probe_in[...] * scale


def close(scale, object_part, probe_total):
    vmem = pl.BlockSpec(memory_space=pltpu.VMEM)
    return pl.pallas_call(
        functools.partial(close_kernel, scale),
        out_shape=tuple(jax.ShapeDtypeStruct(x.shape, F32) for x in (object_part, probe_total)),
        in_specs=[vmem, vmem],
        out_specs=(vmem, vmem),
        compiler_params=pltpu.CompilerParams(vmem_limit_bytes=4 << 20),
    )(object_part, probe_total)


def per_device(object_tiles, probe_wave, patterns, tile_of, offsets, owner_map):
    tile_count = lax.axis_size("tile")
    high, low, shuffle = (jnp.asarray(table) for table in tables())
    zs, xs = lax.axis_size("scan") // CORES, math.isqrt(tile_count)
    ys = tile_count // xs
    object_part, probe_total = whole(
        zs, xs, ys,
        tile_of, offsets.T, owner_map, patterns, object_tiles, probe_wave, high, low, shuffle,
    )
    count = tile_count * lax.axis_size("scan") * patterns.shape[0]
    return close(1.0 / math.sqrt(count), object_part, probe_total)


def solution(mesh):
    return jax.shard_map(
        per_device,
        mesh=mesh,
        in_specs=(
            P("tile", None, None, None, None),
            P(),
            P(("scan", "tile"), None, None),
            P(("scan", "tile")),
            P(("scan", "tile"), None),
            P(),
        ),
        out_specs=(P("tile", None, None, "scan", None), P()),
        check_vma=False,
    )
```
